32 devices in a mesh: crop: 2 (over y), dp: 16 (over z, x, core).
Axes of the slice: x: 2, y: 2, z: 4, core: 2. Of those that a mesh axis runs over, the one named last changes fastest.
Arguments:
- patches: bfloat16 [256, 197, 384], P(('crop', 'dp')), may hold values from -6 to 6
- kept_index: int32 [256, 137], P(('crop', 'dp')), may hold values from 0 to 195, as said below
- lengths: int32 [256], P(('crop', 'dp')), may hold values from 11 to 137, as said below
- source_order: int32 [256], P(('crop', 'dp')), may hold values from 0 to 255, each once
- cot_tokens: bfloat16 [256, 144, 384], P(('crop', 'dp')), may hold values from -6 to 6
- cot_cls: bfloat16 [256, 384], P(('crop', 'dp')), may hold values from -6 to 6
- step_count: int32 [1], replicated, may hold values from 1 to 5
- master_qkv: float32 [2, 442368], P(None, ('crop', 'dp')), may hold values from -0.3125 to 0.3125
- master_proj: float32 [2, 147456], P(None, ('crop', 'dp')), may hold values from -0.875 to 0.875
- master_up: float32 [2, 589824], P(None, ('crop', 'dp')), may hold values from -0.3125 to 0.3125
- master_down: float32 [2, 589824], P(None, ('crop', 'dp')), may hold values from -0.15625 to 0.15625
- master_small: float32 [2, 4608], P(None, ('crop', 'dp'))
- first_qkv: float32 [2, 442368], P(None, ('crop', 'dp'))
- first_proj: float32 [2, 147456], P(None, ('crop', 'dp'))
- first_up: float32 [2, 589824], P(None, ('crop', 'dp'))
- first_down: float32 [2, 589824], P(None, ('crop', 'dp'))
- first_small: float32 [2, 4608], P(None, ('crop', 'dp'))
- second_qkv: float32 [2, 442368], P(None, ('crop', 'dp')), may hold values from 3840 to 15360
- second_proj: float32 [2, 147456], P(None, ('crop', 'dp')), may hold values from 3840 to 15360
- second_up: float32 [2, 589824], P(None, ('crop', 'dp')), may hold values from 3840 to 15360
- second_down: float32 [2, 589824], P(None, ('crop', 'dp')), may hold values from 3840 to 15360
- second_small: float32 [2, 4608], P(None, ('crop', 'dp')), may hold values from 15360 to 61440
Outputs:
- block_out: bfloat16 [256, 144, 384], P(('crop', 'dp'))
- cls_grouped: bfloat16 [256, 384], P(('crop', 'dp'))
- patch_grad: float32 [256, 197, 384], P(('crop', 'dp'))
- updated_qkv: float32 [2, 442368], P(None, ('crop', 'dp'))
- updated_proj: float32 [2, 147456], P(None, ('crop', 'dp'))
- updated_up: float32 [2, 589824], P(None, ('crop', 'dp'))
- updated_down: float32 [2, 589824], P(None, ('crop', 'dp'))
- updated_small: float32 [2, 4608], P(None, ('crop', 'dp'))
- moment_qkv: float32 [2, 442368], P(None, ('crop', 'dp'))
- moment_proj: float32 [2, 147456], P(None, ('crop', 'dp'))
- moment_up: float32 [2, 589824], P(None, ('crop', 'dp'))
- moment_down: float32 [2, 589824], P(None, ('crop', 'dp'))
- moment_small: float32 [2, 4608], P(None, ('crop', 'dp'))
- square_qkv: float32 [2, 442368], P(None, ('crop', 'dp'))
- square_proj: float32 [2, 147456], P(None, ('crop', 'dp'))
- square_up: float32 [2, 589824], P(None, ('crop', 'dp'))
- square_down: float32 [2, 589824], P(None, ('crop', 'dp'))
- square_small: float32 [2, 4608], P(None, ('crop', 'dp'))
The draws below stay inside these ranges and needn't reach their ends.
Inputs may be any that keep to these rules, and one draw needn't show every extreme that they name: `kept_index`: the first lengths[c] entries of row c are distinct; for the focal crops (the last half of the 256 crops) they are under 36. `lengths`: the first half of the crops are views with at least 3 * 196 / 10 kept patches (rounded up); the second half are focal crops with at most 25. `source_order`: a permutation of the 256 crops.
All inputs are finite; a program needn't handle non-finite values.
Results may differ from the reference program's by a relative error of at most 0.015.
Values may be sent and summed in bfloat16 or wider, within the bound.
No kernel may reach another device: no remote copies, remote signals or barrier semaphores. Data moves between devices by JAX's collectives and lax.ppermute only.
A program may use at most 192 MiB of HBM per device.

```python
import math
import jax
import jax.numpy as jnp
from jax import lax

D = 384
HEADS = 6
HEAD_DIM = 64
FF = 1536
LAYERS = 2
PATCHES = 196
FOCAL_PATCHES = 36
SLOTS = 144
KEEP = 137
FOCAL_KEEP = 25
CROPS = 256


def focal_flags():
    return jnp.arange(CROPS, dtype=jnp.int32) >= CROPS // 2


def draw_lengths(key, part):
    focal_rows = focal_flags()
    view_least = (3 * PATCHES + 9) // 10
    focal_least = (3 * FOCAL_PATCHES + 9) // 10
    view_count = jax.random.randint(jax.random.fold_in(key, 11), (CROPS,), view_least, KEEP + 1)
    focal_count = jax.random.randint(jax.random.fold_in(key, 12), (CROPS,), focal_least, FOCAL_KEEP + 1)
    counts = jnp.where(focal_rows, focal_count, view_count)
    counts = counts.at[0].set(KEEP)
    counts = counts.at[CROPS - 1].set(focal_least)
    return counts.astype(jnp.int32)


def draw_kept_index(key, part):
    focal_rows = focal_flags()[:, None]
    patch_ids = jnp.arange(PATCHES, dtype=jnp.int32)[None, :]
    noise_bits = jax.random.randint(jax.random.fold_in(key, 13), (CROPS, PATCHES), 0, 1 << 20)
    sort_score = noise_bits * 256 + patch_ids
    sort_score = sort_score + jnp.where(focal_rows & (patch_ids >= FOCAL_PATCHES), 1 << 29, 0)
    patch_order = jnp.argsort(sort_score, axis=1)
    return patch_order[:, :KEEP].astype(jnp.int32)


def first_moment(key, salt, array_shape, square_scale):
    salted = jax.random.fold_in(jax.random.fold_in(key, 31), salt)
    return jax.random.normal(salted, array_shape, jnp.float32) * math.sqrt(square_scale)


def second_moment(key, salt, array_shape, square_scale):
    salted = jax.random.fold_in(jax.random.fold_in(key, 32), salt)
    spread = jax.random.uniform(salted, array_shape, jnp.float32, 0.0, math.log(4.0))
    return square_scale * jnp.exp(spread)


def draw_master_small(key, part):
    column_count = 8 + FF // D
    column_ids = jnp.arange(column_count, dtype=jnp.int32)[None, None, :]
    biases = 0.3 * jax.random.normal(jax.random.fold_in(key, 21), (LAYERS, D, column_count), jnp.float32)
    gains = jax.random.uniform(jax.random.fold_in(key, 22), (LAYERS, D, column_count), jnp.float32, 0.7, 1.3)
    table = jnp.where((column_ids == 0) | (column_ids == 5), gains, biases)
    return table.reshape(LAYERS, D * column_count)


def draw_first_qkv(key, part):
    return first_moment(key, 1, (LAYERS, 3 * D * D), CROPS * 15.0)


def draw_first_proj(key, part):
    return first_moment(key, 2, (LAYERS, D * D), CROPS * 15.0)


def draw_first_up(key, part):
    return first_moment(key, 3, (LAYERS, D * FF), CROPS * 15.0)


def draw_first_down(key, part):
    return first_moment(key, 4, (LAYERS, FF * D), CROPS * 15.0)


def draw_first_small(key, part):
    return first_moment(key, 5, (LAYERS, 8 * D + FF), CROPS * 60.0)


def draw_second_qkv(key, part):
    return second_moment(key, 1, (LAYERS, 3 * D * D), CROPS * 15.0)


def draw_second_proj(key, part):
    return second_moment(key, 2, (LAYERS, D * D), CROPS * 15.0)


def draw_second_up(key, part):
    return second_moment(key, 3, (LAYERS, D * FF), CROPS * 15.0)


def draw_second_down(key, part):
    return second_moment(key, 4, (LAYERS, FF * D), CROPS * 15.0)


def draw_second_small(key, part):
    return second_moment(key, 5, (LAYERS, 8 * D + FF), CROPS * 60.0)


def level_of(rng, extent, cuts, least, largest):
    level, own = 1.0, jax.random.fold_in(rng, 6)
    for dim, blocks in cuts:
        draws = jnp.exp(jax.random.uniform(jax.random.fold_in(own, dim), (blocks,), jnp.float32, least / len(cuts), largest / len(cuts)))
        level = level * jnp.repeat(draws, extent[dim] // blocks).reshape([-1 if axis == dim else 1 for axis in range(len(extent))])
    return level


def noise(own_key, dims, deviation, bound, pieces=(), held_as=jnp.bfloat16):
    entries = deviation * jax.random.normal(own_key, dims, jnp.float32)
    if pieces:
        entries = entries * level_of(own_key, dims, pieces, -0.22, 0.18)
    return jnp.clip(entries, -bound, bound).astype(held_as)


def setup_inputs(seed: int = 0) -> dict:
    seeds = jax.random.split(jax.random.key(seed), 23)
    patches = noise(seeds[0], (CROPS, PATCHES + 1, D), 1.0, 6.0, ((0, 32),))
    kept_index = draw_kept_index(jax.random.fold_in(seeds[22], 71), 0)
    lengths = draw_lengths(jax.random.fold_in(seeds[22], 71), 0)
    source_order = jax.random.permutation(seeds[3], CROPS).astype(jnp.int32)
    cot_tokens = noise(seeds[4], (CROPS, SLOTS, D), 1.0, 6.0, ((0, 32),))
    cot_cls = noise(seeds[5], (CROPS, D), 1.0, 6.0, ((0, 32),))
    step_count = jax.random.randint(seeds[6], (1,), 1, 6).astype(jnp.int32)
    master_qkv = noise(seeds[7], (LAYERS, 3 * D * D), D ** -0.5, 0.3125, ((1, 32),), jnp.float32)
    master_proj = noise(seeds[8], (LAYERS, D * D), (D // 8) ** -0.5, 0.875, ((1, 32),), jnp.float32)
    master_up = noise(seeds[9], (LAYERS, D * FF), D ** -0.5, 0.3125, ((1, 32),), jnp.float32)
    master_down = noise(seeds[10], (LAYERS, FF * D), FF ** -0.5, 0.15625, ((1, 32),), jnp.float32)
    master_small = draw_master_small(jax.random.fold_in(seeds[22], 71), 0)
    first_qkv = draw_first_qkv(jax.random.fold_in(seeds[22], 71), 0)
    first_proj = draw_first_proj(jax.random.fold_in(seeds[22], 71), 0)
    first_up = draw_first_up(jax.random.fold_in(seeds[22], 71), 0)
    first_down = draw_first_down(jax.random.fold_in(seeds[22], 71), 0)
    first_small = draw_first_small(jax.random.fold_in(seeds[22], 71), 0)
    second_qkv = draw_second_qkv(jax.random.fold_in(seeds[22], 71), 0)
    second_proj = draw_second_proj(jax.random.fold_in(seeds[22], 71), 0)
    second_up = draw_second_up(jax.random.fold_in(seeds[22], 71), 0)
    second_down = draw_second_down(jax.random.fold_in(seeds[22], 71), 0)
    second_small = draw_second_small(jax.random.fold_in(seeds[22], 71), 0)
    return dict(patches=patches, kept_index=kept_index, lengths=lengths, source_order=source_order, cot_tokens=cot_tokens, cot_cls=cot_cls, step_count=step_count, master_qkv=master_qkv, master_proj=master_proj, master_up=master_up, master_down=master_down, master_small=master_small, first_qkv=first_qkv, first_proj=first_proj, first_up=first_up, first_down=first_down, first_small=first_small, second_qkv=second_qkv, second_proj=second_proj, second_up=second_up, second_down=second_down, second_small=second_small)


@jax.custom_vjp
def low(v):
    return lax.optimization_barrier(v.astype(jnp.bfloat16)).astype(jnp.float32)

@jax.custom_vjp
def low_back(v):
    return v

def low_keep(v):
    return (low(v), None)

def low_pass(kept, grad):
    return (grad,)

def back_keep(v):
    return (v, None)

def back_low(kept, grad):
    return (low(grad),)
low.defvjp(low_keep, low_pass)
low_back.defvjp(back_keep, back_low)
eps_norm = 1e-06
neg_big = -1e+30
highest = lax.Precision.HIGHEST
beta_one = 0.5
beta_two = 0.5
adam_eps = 1e-08
rate_matrix = 0.04
decay_matrix = 0.05
rate_small = 0.4
group_crops = 16

def layer_norm(values, norm_gain, norm_bias):
    average = lax.optimization_barrier(jnp.mean(values, -1, keepdims=True))
    centered = values - average
    variance = lax.optimization_barrier(jnp.mean(centered * centered, -1, keepdims=True))
    return centered * lax.rsqrt(variance + eps_norm) * norm_gain + norm_bias

def gelu_tanh(values):
    return jax.nn.gelu(values, approximate=True)

def matmul(left_side, right_side):
    return jnp.einsum('...i,ij->...j', left_side, right_side, precision=highest)

def shape_weights(flat_parts):
    small_matrix = flat_parts[4].reshape(D, 8 + FF // D)
    stacked = jnp.transpose(small_matrix[:, :8])
    up_bias = small_matrix[:, 8:].reshape(FF)
    return (flat_parts[0].reshape(D, 3 * D), flat_parts[1].reshape(D, D), flat_parts[2].reshape(D, FF), flat_parts[3].reshape(FF, D), stacked, up_bias)

def assemble(group_patches, group_kept, group_lengths):
    crop_count = group_kept.shape[0]
    slot_index = jnp.concatenate([jnp.zeros((crop_count, 1), jnp.int32), group_kept.astype(jnp.int32) + 1], 1)
    picked = jnp.take_along_axis(group_patches, slot_index[:, :, None], 1)
    positions = jnp.arange(KEEP + 1, dtype=jnp.int32)
    live_kept = positions[None, :] <= group_lengths[:, None]
    picked = jnp.where(live_kept[:, :, None], picked, jnp.zeros_like(picked))
    tokens = jnp.concatenate([picked, jnp.zeros((crop_count, SLOTS - KEEP - 1, D), jnp.float32)], 1)
    live_slots = jnp.arange(SLOTS, dtype=jnp.int32)[None, :] <= group_lengths[:, None]
    return (tokens, live_slots)

def encoder_layer(tokens, live_slots, params):
    qkv_weight, proj_weight, up_weight, down_weight, stacked, up_bias = params
    group_size = tokens.shape[0]
    score_scale = HEAD_DIM ** (-0.5)
    normed_one = low(layer_norm(tokens, stacked[0], stacked[1]))
    qkv_bias = jnp.concatenate([stacked[2], jnp.zeros((D,), jnp.float32), stacked[3]])
    qkv_rows = low(low_back(matmul(normed_one, qkv_weight) + qkv_bias))
    split_rows = qkv_rows.reshape(group_size, SLOTS, 3, HEADS, HEAD_DIM)
    query = split_rows[:, :, 0]
    key_part = split_rows[:, :, 1]
    value_part = split_rows[:, :, 2]
    scores = low_back(jnp.einsum('bqhd,bkhd->bhqk', query, key_part, precision=highest) * score_scale)
    scores = jnp.where(live_slots[:, None, None, :], scores, neg_big)
    row_max = lax.optimization_barrier(jnp.max(scores, -1, keepdims=True))
    exp_scores = jnp.exp(scores - row_max)
    probabilities = low(exp_scores / lax.optimization_barrier(jnp.sum(exp_scores, -1, keepdims=True)))
    attended = jnp.einsum('bhqk,bkhd->bqhd', probabilities, value_part, precision=highest)
    attended = low(low_back(attended.reshape(group_size, SLOTS, D)))
    mid_rows = tokens + low_back(matmul(attended, proj_weight) + stacked[4])
    normed_two = low(layer_norm(mid_rows, stacked[5], stacked[6]))
    hidden = low_back(matmul(normed_two, up_weight) + up_bias)
    active = low(gelu_tanh(hidden))
    return mid_rows + low_back(matmul(active, down_weight) + stacked[7])

def forward_all(masters, patch_values, kept_index, lengths, source_order):
    layer_params = []
    for layer_index in range(LAYERS):
        layer_params.append(shape_weights([low(item[layer_index]) for item in masters]))

    def one_group(inputs):
        group_patches, group_kept, group_lengths = inputs
        tokens, live_slots = assemble(group_patches, group_kept, group_lengths)
        for params in layer_params:
            tokens = encoder_layer(tokens, live_slots, params)
        return tokens * live_slots[:, :, None].astype(jnp.float32)
    batches = CROPS // group_crops
    outputs = lax.map(jax.checkpoint(one_group), (patch_values.reshape(batches, group_crops, PATCHES + 1, D), kept_index.reshape(batches, group_crops, KEEP), lengths.reshape(batches, group_crops)))
    outputs = outputs.reshape(CROPS, SLOTS, D)
    cls_rows = low(outputs[:, 0])
    return (outputs, jnp.take(cls_rows, source_order, axis=0))

def adam_update(master, old_first, old_second, gradient, step_rate, decay_rate, step_value):
    moment = beta_one * old_first + (1.0 - beta_one) * gradient
    square = beta_two * old_second + (1.0 - beta_two) * gradient * gradient
    fix_one = 1.0 - jnp.power(beta_one, step_value)
    fix_two = 1.0 - jnp.power(beta_two, step_value)
    update = moment / fix_one / (jnp.sqrt(square / fix_two) + adam_eps) + decay_rate * master
    return (master - step_rate * update, moment, square)

def reference(patches, kept_index, lengths, source_order, cot_tokens, cot_cls, step_count, master_qkv, master_proj, master_up, master_down, master_small, first_qkv, first_proj, first_up, first_down, first_small, second_qkv, second_proj, second_up, second_down, second_small):
    masters = (master_qkv, master_proj, master_up, master_down, master_small)
    first_list = (first_qkv, first_proj, first_up, first_down, first_small)
    second_list = (second_qkv, second_proj, second_up, second_down, second_small)
    patch_values = patches.astype(jnp.float32)

    def wrapped(masters_in, patch_in):
        return forward_all(masters_in, patch_in, kept_index, lengths, source_order)
    (outputs, grouped), pullback = jax.vjp(wrapped, masters, patch_values)
    grad_masters, grad_patches = pullback((cot_tokens.astype(jnp.float32), cot_cls.astype(jnp.float32)))
    step_value = step_count[0].astype(jnp.float32)
    results = []
    for kind_index in range(5):
        step_rate = rate_small if kind_index == 4 else rate_matrix
        decay_rate = 0.0 if kind_index == 4 else decay_matrix
        results.append(adam_update(masters[kind_index], first_list[kind_index], second_list[kind_index], grad_masters[kind_index], step_rate, decay_rate, step_value))
    return (outputs.astype(jnp.bfloat16), grouped.astype(jnp.bfloat16), grad_patches, results[0][0], results[1][0], results[2][0], results[3][0], results[4][0], results[0][1], results[1][1], results[2][1], results[3][1], results[4][1], results[0][2], results[1][2], results[2][2], results[3][2], results[4][2])
```

```python
import functools

import jax
import jax.numpy as jnp
from jax import lax
from jax.experimental import pallas as pl
from jax.experimental.pallas import tpu as pltpu
from jax.sharding import PartitionSpec as P

D = 384
HEADS = 6
HEAD_DIM = 64
FF = 1536
LAYERS = 2
SLOTS = 144
FOCAL_SLOTS = 32
LEN_ROW = 143

eps_norm = 1e-06
neg_big = -1e30
adam_eps = 1e-08
rate_matrix = 0.04
decay_matrix = 0.05
rate_small = 0.4

F32 = jnp.float32
BF16 = jnp.bfloat16
VM = pl.BlockSpec(memory_space=pltpu.VMEM)
SM = pl.BlockSpec(memory_space=pltpu.SMEM)
AXES = ("crop", "dp")
VMEM_LIMIT = 48 * 1024 * 1024


def sds(shape, dtype):
    return jax.ShapeDtypeStruct(shape, dtype)


def call(body, out_shape, scratch=(), smem=1, cost=None):
    def run(*operands):
        moved = sum(a.size * a.dtype.itemsize for a in operands)
        moved += sum(a.size * a.dtype.itemsize for a in jax.tree.leaves(out_shape))
        return pl.pallas_call(
            body,
            out_shape=out_shape,
            in_specs=[SM] * smem + [VM] * (len(operands) - smem),
            out_specs=jax.tree.map(lambda _: VM, out_shape),
            scratch_shapes=list(scratch),
            compiler_params=pltpu.CompilerParams(vmem_limit_bytes=VMEM_LIMIT),
            cost_estimate=pl.CostEstimate(flops=cost or 0, bytes_accessed=moved, transcendentals=0),
        )(*operands)

    return run


def iota(shape, axis):
    return lax.broadcasted_iota(jnp.int32, shape, axis)


def dot(a, b, ca, cb):
    return lax.dot_general(a, b, (((ca,), (cb,)), ((), ())), preferred_element_type=F32)


def slot_onehot(slots, c, patch_count):
    row = slots[pl.ds(c, 1), :]
    return row, (iota((patch_count, SLOTS), 0) == row).astype(F32).astype(BF16)


def tokens_body(half, patch_count, place, patches, slots, keep, send):
    y = place[0]
    row_index = iota((SLOTS, D), 0)
    for i in range(half):
        for out, c in ((keep, half * y + i), (send, half * (1 - y) + i)):
            row, onehot = slot_onehot(slots, c, patch_count)
            count = jnp.sum((row >= 0).astype(F32), axis=1, keepdims=True) - 1.0
            picked = dot(onehot, patches[c], 0, 0)
            out[i] = jnp.where(row_index == LEN_ROW, count, picked).astype(BF16)


def arrange_body(half, place, keep, recv, x_ref, bias_ref, lens_ref):
    y = place[0]
    base = half * SLOTS
    used = half * FOCAL_SLOTS

    def run(v_src, f_src):
        q = iota((SLOTS, SLOTS), 0)
        k = iota((SLOTS, SLOTS), 1)
        row_index = iota((SLOTS, D), 0)
        for i in range(half):
            t = v_src[i].astype(F32)
            n = t[LEN_ROW : LEN_ROW + 1, 0:1]
            x_ref[SLOTS * i : SLOTS * (i + 1), :] = jnp.where(row_index == LEN_ROW, 0.0, t)
            bias_ref[i] = jnp.where(k.astype(F32) <= n, 0.0, neg_big)
            lens_ref[i : i + 1, :] = jnp.broadcast_to(n, (1, 128))
        limit = jnp.full((SLOTS, SLOTS), 1000.0, F32)
        for i in range(half):
            x_ref[base + FOCAL_SLOTS * i : base + FOCAL_SLOTS * (i + 1), :] = f_src[
                i, 0:FOCAL_SLOTS
            ].astype(F32)
            n = f_src[i, SLOTS - 16 : SLOTS].astype(F32)[15:16, 0:1]
            limit = jnp.where((k // FOCAL_SLOTS) == i, n, limit)
            lens_ref[half + i : half + i + 1, :] = jnp.broadcast_to(n, (1, 128))
        if used < SLOTS:
            x_ref[base + used : base + SLOTS, :] = jnp.zeros((SLOTS - used, D), F32)
        same = (q // FOCAL_SLOTS) == (k // FOCAL_SLOTS)
        inside = (k % FOCAL_SLOTS).astype(F32) <= limit
        bias_ref[half] = jnp.where(same & inside, 0.0, neg_big)

    @pl.when(y == 0)
    def _():
        run(keep, recv)

    @pl.when(y == 1)
    def _():
        run(recv, keep)


def top_body(half, place, cot, recv, lens, gcls, g_ref):
    y = place[0]
    base = half * SLOTS
    used = half * FOCAL_SLOTS

    def piece(values, n, top, rows):
        index = iota((rows, D), 0)
        masked = jnp.where(index.astype(F32) <= n, values, 0.0)
        return masked + jnp.where(index == 0, top, 0.0)

    def run(v_get, f_get):
        for i in range(half):
            g_ref[SLOTS * i : SLOTS * (i + 1), :] = piece(
                v_get(i).astype(F32), lens[i : i + 1, 0:1], gcls[i : i + 1, :], SLOTS
            )
            g_ref[base + FOCAL_SLOTS * i : base + FOCAL_SLOTS * (i + 1), :] = piece(
                f_get(i)[0:FOCAL_SLOTS].astype(F32),
                lens[half + i : half + i + 1, 0:1],
                gcls[half + i : half + i + 1, :],
                FOCAL_SLOTS,
            )
        if used < SLOTS:
            g_ref[base + used : base + SLOTS, :] = jnp.zeros((SLOTS - used, D), F32)

    @pl.when(y == 0)
    def _():
        run(lambda i: cot[i], lambda i: recv[i])

    @pl.when(y == 1)
    def _():
        run(lambda i: recv[i], lambda i: cot[half + i])


def split_body(half, masked, place, x_ref, lens, keep, send, *cls_out):
    y = place[0]
    base = half * SLOTS

    def run(v_out, f_out):
        for i in range(half):
            v = x_ref[SLOTS * i : SLOTS * (i + 1), :]
            f = x_ref[base + FOCAL_SLOTS * i : base + FOCAL_SLOTS * (i + 1), :]
            if cls_out:
                cls_out[0][i : i + 1, :] = v[0:1]
                cls_out[0][half + i : half + i + 1, :] = f[0:1]
            if masked:
                v = jnp.where(iota((SLOTS, D), 0).astype(F32) <= lens[i : i + 1, 0:1], v, 0.0)
                f = jnp.where(
                    iota((FOCAL_SLOTS, D), 0).astype(F32) <= lens[half + i : half + i + 1, 0:1],
                    f,
                    0.0,
                )
            v_out[i] = v.astype(BF16)
            f_out[i, 0:FOCAL_SLOTS] = f.astype(BF16)
            f_out[i, FOCAL_SLOTS:SLOTS] = jnp.zeros((SLOTS - FOCAL_SLOTS, D), BF16)

    @pl.when(y == 0)
    def _():
        run(keep, send)

    @pl.when(y == 1)
    def _():
        run(send, keep)


def join_body(half, place, keep, recv, out):
    y = place[0]
    for i in range(half):
        out[half * y + i] = keep[i]
        out[half * (1 - y) + i] = recv[i]


def scatter_body(half, patch_count, place, keep, recv, slots, out):
    y = place[0]
    for i in range(half):
        for src, c in ((keep, half * y + i), (recv, half * (1 - y) + i)):
            _, onehot = slot_onehot(slots, c, patch_count)
            out[c] = dot(onehot, src[i], 1, 0)


def lane_mask(second, value):
    lane = iota((1, 128), 1)
    chosen = (lane >= HEAD_DIM) if second else (lane < HEAD_DIM)
    return jnp.where(chosen, value, 0.0).astype(BF16)


def attend_forward_body(qkv_ref, bias_ref, att_ref, prob_ref):
    bias = bias_ref[0]
    for pair in range(HEADS // 2):
        at = 128 * pair
        q = qkv_ref[:, at : at + 128]
        k = qkv_ref[:, D + at : D + at + 128]
        v = qkv_ref[:, 2 * D + at : 2 * D + at + 128]
        total = None
        for h in range(2):
            s = dot(q * lane_mask(h, HEAD_DIM**-0.5), k, 1, 1) + bias
            e = jnp.exp(s - jnp.max(s, -1, keepdims=True))
            p = (e / jnp.sum(e, -1, keepdims=True)).astype(BF16)
            prob_ref[0, 2 * pair + h] = p
            o = dot(p, v * lane_mask(h, 1.0), 1, 0)
            total = o if total is None else total + o
        att_ref[:, at : at + 128] = total.astype(BF16)


def attend_backward_body(qkv_ref, prob_ref, grad_ref, out_ref):
    for pair in range(HEADS // 2):
        at = 128 * pair
        q = qkv_ref[:, at : at + 128]
        k = qkv_ref[:, D + at : D + at + 128]
        v = qkv_ref[:, 2 * D + at : 2 * D + at + 128]
        g = grad_ref[:, at : at + 128]
        dq = dk = dv = None
        for h in range(2):
            pb = prob_ref[0, 2 * pair + h]
            p = pb.astype(F32)
            gh = g * lane_mask(h, 1.0)
            scaled = lane_mask(h, HEAD_DIM**-0.5)
            dp = dot(gh, v, 1, 1)
            ds = (p * (dp - jnp.sum(p * dp, -1, keepdims=True))).astype(BF16)
            parts = (dot(ds, k * scaled, 1, 0), dot(ds, q * scaled, 0, 0), dot(pb, gh, 0, 0))
            if dq is None:
                dq, dk, dv = parts
            else:
                dq, dk, dv = dq + parts[0], dk + parts[1], dv + parts[2]
        out_ref[:, at : at + 128] = dq.astype(BF16)
        out_ref[:, D + at : D + at + 128] = dk.astype(BF16)
        out_ref[:, 2 * D + at : 2 * D + at + 128] = dv.astype(BF16)


def row_block(width):
    return pl.BlockSpec((SLOTS, width), lambda b: (b, 0))


def attend_forward(qkv, bias):
    blocks = bias.shape[0]
    return pl.pallas_call(
        attend_forward_body,
        grid=(blocks,),
        in_specs=[row_block(3 * D), pl.BlockSpec((1, SLOTS, SLOTS), lambda b: (b, 0, 0))],
        out_specs=[row_block(D), pl.BlockSpec((1, HEADS, SLOTS, SLOTS), lambda b: (b, 0, 0, 0))],
        out_shape=[
            sds((blocks * SLOTS, D), BF16),
            sds((blocks, HEADS, SLOTS, SLOTS), BF16),
        ],
        compiler_params=pltpu.CompilerParams(vmem_limit_bytes=VMEM_LIMIT),
        cost_estimate=pl.CostEstimate(
            flops=blocks * HEADS * SLOTS * SLOTS * 512,
            bytes_accessed=blocks * SLOTS * D * 16,
            transcendentals=blocks * HEADS * SLOTS * SLOTS,
        ),
    )(qkv, bias)


def attend_backward(qkv, prob, grad):
    blocks = prob.shape[0]
    return pl.pallas_call(
        attend_backward_body,
        grid=(blocks,),
        in_specs=[
            row_block(3 * D),
            pl.BlockSpec((1, HEADS, SLOTS, SLOTS), lambda b: (b, 0, 0, 0)),
            row_block(D),
        ],
        out_specs=row_block(3 * D),
        out_shape=sds((blocks * SLOTS, 3 * D), BF16),
        compiler_params=pltpu.CompilerParams(vmem_limit_bytes=VMEM_LIMIT),
        cost_estimate=pl.CostEstimate(
            flops=blocks * HEADS * SLOTS * SLOTS * 1024,
            bytes_accessed=blocks * SLOTS * D * 24,
            transcendentals=0,
        ),
    )(qkv, prob, grad)


def normalized(values):
    centered = values - jnp.mean(values, -1, keepdims=True)
    scale = lax.rsqrt(jnp.mean(centered * centered, -1, keepdims=True) + eps_norm)
    return centered * scale, scale


def norm_back(grad, values, gain):
    unit, scale = normalized(values)
    inner = grad * gain
    back = scale * (
        inner
        - jnp.mean(inner, -1, keepdims=True)
        - unit * jnp.mean(inner * unit, -1, keepdims=True)
    )
    return back, jnp.sum(grad * unit, 0), jnp.sum(grad, 0)


def gelu_parts(v):
    c = 0.7978845608028654
    a = 0.044715
    square = v * v
    t = jnp.tanh(c * (v + a * v * square))
    value = 0.5 * v * (1.0 + t)
    slope = 0.5 * (1.0 + t) + 0.5 * v * (1.0 - t * t) * c * (1.0 + 3.0 * a * square)
    return value, slope


def layer_forward_one(x, bias, qkv_w, proj_w, small):
    unit, _ = normalized(x)
    normed_one = (unit * small[0] + small[1]).astype(BF16)
    qkv_bias = jnp.concatenate([small[2], jnp.zeros((D,), F32), small[3]])
    qkv = (jnp.dot(normed_one, qkv_w, preferred_element_type=F32) + qkv_bias).astype(BF16)
    attended, prob = attend_forward(qkv, bias)
    mid = x + jnp.dot(attended, proj_w, preferred_element_type=F32) + small[4]
    unit, _ = normalized(mid)
    normed_two = (unit * small[5] + small[6]).astype(BF16)
    return normed_one, qkv, attended, prob, mid, normed_two


def layer_forward_two(mid, normed_two, up_w, down_w, small, up_bias):
    hidden = jnp.dot(normed_two, up_w, preferred_element_type=F32) + up_bias
    value, slope = gelu_parts(hidden)
    active, slope = value.astype(BF16), slope.astype(BF16)
    out = mid + jnp.dot(active, down_w, preferred_element_type=F32) + small[7]
    return out, active, slope


def layer_backward_two(g, mid, normed_two, active, slope, up_w, down_w, small):
    branch = g.astype(BF16)
    g_down = dot(active, branch, 0, 0).astype(BF16)
    bias_down = jnp.sum(branch.astype(F32), 0)
    g_hidden = (dot(branch, down_w, 1, 1) * slope.astype(F32)).astype(BF16)
    g_up = dot(normed_two, g_hidden, 0, 0).astype(BF16)
    bias_up = jnp.sum(g_hidden.astype(F32), 0)
    back, gain, shift = norm_back(dot(g_hidden, up_w, 1, 1), mid, small[5])
    return g + back, g_up, g_down, (gain, shift, bias_down, bias_up)


def layer_backward_one(g_mid, x, normed_one, qkv, attended, prob, qkv_w, proj_w, small):
    proj_out = g_mid.astype(BF16)
    g_proj = dot(attended, proj_out, 0, 0).astype(BF16)
    bias_proj = jnp.sum(proj_out.astype(F32), 0)
    g_attended = dot(proj_out, proj_w, 1, 1).astype(BF16)
    g_qkv = attend_backward(qkv, prob, g_attended)
    g_qkv_w = dot(normed_one, g_qkv, 0, 0).astype(BF16)
    bias_qkv = jnp.sum(g_qkv.astype(F32), 0)
    back, gain, shift = norm_back(dot(g_qkv, qkv_w, 1, 1), x, small[0])
    return g_mid + back, g_qkv_w, g_proj, (gain, shift, bias_qkv, bias_proj)


def small_gradient(two, one):
    gain_two, shift_two, bias_down, bias_up = two
    gain_one, shift_one, bias_qkv, bias_proj = one
    rows = [gain_one, shift_one, bias_qkv[:D], bias_qkv[2 * D :], bias_proj]
    rows += [gain_two, shift_two, bias_down]
    return jnp.concatenate([jnp.stack(rows, 1), bias_up.reshape(D, FF // D)], 1)


ROWS = 12
PAIR = 24
QKV, PROJ, UP, SMALL, CLS, ORDER, PAD = 3 * D, D, FF, 128, D, 128, 128


class Chunk:
    def __init__(self, names, widths, down):
        self.names, self.widths, self.down = names, widths, down
        self.half = sum(widths) // 2
        self.width = self.half + (2 * D if down else 0)

    def pieces(self, which):
        low, high, start, found = which * self.half, (which + 1) * self.half, 0, []
        for name, width in zip(self.names, self.widths):
            a, b = max(start, low), min(start + width, high)
            if a < b:
                found.append((name, a - start, a - low, b - a))
            start += width
        return found


GATHERED = (
    Chunk(("qkv0", "proj0", "small", "pad"), (QKV, PROJ, SMALL, PAD), False),
    Chunk(("up0",), (UP,), True),
    Chunk(("qkv1", "proj1", "up1", "cls", "order"), (QKV, PROJ, UP, CLS, ORDER), True),
)
REDUCED = (
    Chunk(("up1",), (UP,), True),
    Chunk(("qkv1", "proj1", "cls", "pad"), (QKV, PROJ, CLS, PAD), False),
    Chunk(("up0",), (UP,), True),
    Chunk(("qkv0", "proj0", "small", "pad"), (QKV, PROJ, SMALL, PAD), False),
)
FLAT = {"qkv": QKV, "proj": PROJ, "up": UP}
EXTRA = {"cls": (0, CLS), "order": (CLS, ORDER), "small": (CLS + ORDER, SMALL)}


def by_core(place, run):
    for b in range(2):

        @pl.when(place[3] == b)
        def _(b=b):
            run(b)


def pack_body(
    place, own_qkv, own_proj, own_up, own_extra, sib_qkv, sib_proj, sib_up, sib_extra, down, *rest
):
    outs, work = rest[:3], rest[3]
    own = {"qkv": own_qkv, "proj": own_proj, "up": own_up, "extra": own_extra}
    sib = {"qkv": sib_qkv, "proj": sib_proj, "up": sib_up, "extra": sib_extra}

    def run(b):
        for at, (chunk, out) in enumerate(zip(GATHERED, outs)):
            layer = 1 if at == 2 else 0
            for core in range(2):
                source = own if core == b else sib
                to = slice(ROWS * core, ROWS * (core + 1))
                for name, column, place_at, width in chunk.pieces(b):
                    if name == "pad":
                        work[to, place_at : place_at + width] = jnp.zeros((ROWS, width), F32)
                    elif name in EXTRA:
                        first = EXTRA[name][0] + column
                        work[to, place_at : place_at + width] = source["extra"][
                            0:ROWS, first : first + width
                        ]
                    else:
                        flat, full = source[name[:-1]], FLAT[name[:-1]]
                        for r in range(ROWS):
                            first = r * full + column
                            work[ROWS * core + r : ROWS * core + r + 1, place_at : place_at + width] = (
                                flat[layer : layer + 1, first : first + width]
                            )
            if chunk.down:
                for r in range(2 * PAIR):
                    first = chunk.half + (r // PAIR) * D
                    work[r % PAIR : r % PAIR + 1, first : first + D] = down[
                        layer : layer + 1, r * D : (r + 1) * D
                    ]
            out[...] = work[:, : chunk.width].astype(BF16)

    by_core(place, run)


def chip_at(place, j, z):
    x = place[2] ^ (j & 1)
    y = place[0] ^ (j >> 1)
    return 8 * y + 2 * z + x


def unpack_body(chunk, place, *refs):
    own, sib, outs = refs[0:4], refs[4:8], refs[8:]
    names = [n for n in chunk.names if n != "pad"] + (["down"] if chunk.down else [])
    target = dict(zip(names, outs))

    def run(b):
        sides = (own, sib) if b == 0 else (sib, own)
        for j in range(4):
            for jz in range(4):
                chip = chip_at(place, j, place[1] ^ jz)
                for which in range(2):
                    source = sides[which][j]
                    for name, column, at, width in chunk.pieces(which):
                        if name != "pad":
                            target[name][chip, :, column : column + width] = source[
                                jz, :, at : at + width
                            ]
                    if chunk.down:
                        for part in range(2):
                            first = chunk.half + part * D
                            target["down"][chip * 4 + 2 * which + part] = source[
                                jz, :, first : first + D
                            ]

    by_core(place, run)


def permute(x, mask):
    count = 32
    return lax.ppermute(x, AXES, [(i, i ^ mask) for i in range(count)])


def gather_chunk(chunk, packed, place):
    lines = jnp.stack([packed, permute(packed, 4), permute(packed, 8), permute(packed, 12)])
    own = [lines, permute(lines, 2), permute(lines, 16), permute(lines, 18)]
    sib = [permute(item, 1) for item in own]
    shapes = [
        sds((16, PAIR, width), BF16)
        for name, width in zip(chunk.names, chunk.widths)
        if name != "pad"
    ]
    if chunk.down:
        shapes.append(sds((64, PAIR, D), BF16))
    blocks = call(functools.partial(unpack_body, chunk), shapes)(place, *own, *sib)
    return [b.reshape(-1, b.shape[2]) for b in blocks]


def reduce_one_body(chunk, place, *refs):
    names = [n for n in chunk.names if n != "pad"] + (["down"] if chunk.down else [])
    source = dict(zip(names, refs))
    keep, send = refs[len(names) :]

    def run(b):
        def chip_step(chip, _):
            for out, which in ((keep, b), (send, 1 - b)):
                for name, column, at, width in chunk.pieces(which):
                    if name == "pad":
                        out[chip, :, at : at + width] = jnp.zeros((PAIR, width), BF16)
                    else:
                        out[chip, :, at : at + width] = source[name][
                            chip, :, column : column + width
                        ]
                if chunk.down:
                    for part in range(2):
                        at = chunk.half + part * D
                        out[chip, :, at : at + D] = source["down"][chip * 4 + 2 * which + part]
            return 0

        lax.fori_loop(0, 16, chip_step, 0)

    by_core(place, run)


def reduce_two_body(place, keep, recv, *outs):
    for j in range(4):
        for z in range(4):
            chip = chip_at(place, j, z)
            outs[j][z] = (keep[chip].astype(F32) + recv[chip].astype(F32)).astype(BF16)


def reduce_three_body(place, own, rx, ry, rxy, keep, *sends):
    for j in range(4):
        z = place[1] ^ j
        total = (own[z].astype(F32) + rx[z].astype(F32)) + (ry[z].astype(F32) + rxy[z].astype(F32))
        if j == 0:
            keep[...] = total
        else:
            sends[j - 1][...] = total.astype(BF16)


def reduce_four_body(chunk, place, own, r1, r2, r3, keep, send, *down_out):
    def run(b):
        total = (own[...] + r1[...].astype(F32)) + (r2[...].astype(F32) + r3[...].astype(F32))
        for out, core in ((keep, b), (send, 1 - b)):
            out[...] = total[ROWS * core : ROWS * (core + 1), : chunk.half]
        if chunk.down:
            down_out[0][...] = total[:, chunk.half :]

    by_core(place, run)


def reduce_chunk(chunk, matrices, place):
    block = sds((16, PAIR, chunk.width), BF16)
    matrices = [m.reshape(-1, PAIR, m.shape[1]) for m in matrices]
    keep, send = call(functools.partial(reduce_one_body, chunk), [block, block])(place, *matrices)
    recv = permute(send, 1)
    line = sds((4, PAIR, chunk.width), BF16)
    own, sx, sy, sxy = call(reduce_two_body, [line] * 4)(place, keep, recv)
    rx, ry, rxy = permute(sx, 2), permute(sy, 16), permute(sxy, 18)
    last = sds((PAIR, chunk.width), BF16)
    own, s1, s2, s3 = call(reduce_three_body, [sds((PAIR, chunk.width), F32)] + [last] * 3)(
        place, own, rx, ry, rxy
    )
    r1, r2, r3 = permute(s1, 4), permute(s2, 8), permute(s3, 12)
    shapes = [sds((ROWS, chunk.half), F32)] * 2
    if chunk.down:
        shapes.append(sds((PAIR, 2 * D), F32))
    out = call(functools.partial(reduce_four_body, chunk), shapes)(place, own, r1, r2, r3)
    return (out[0], permute(out[1], 1)) + tuple(out[2:])


def adam_math(fix, master, first, second, grad, rate, decay):
    moment = 0.5 * first + 0.5 * grad
    square = 0.5 * second + 0.5 * grad * grad
    update = moment / fix / (jnp.sqrt(square / fix) + adam_eps) + decay * master
    return master - rate * update, moment, square


def halves(b, keep, recv):
    return (keep, recv) if b == 0 else (recv, keep)


def adam_body(plan, place, fix_ref, *refs):
    chunks, names = plan
    grads, at = [], 0
    for chunk, _ in chunks:
        size = 3 if chunk.down else 2
        grads.append(refs[at : at + size])
        at += size
    flats = refs[at : at + 3 * len(names)]
    outs = refs[at + 3 * len(names) : at + 6 * len(names)]
    rest = refs[at + 6 * len(names) :]
    work = dict(zip(names, rest[-len(names) :]))
    extra = dict(zip(("cls", "small"), rest[: -len(names)]))

    def run(b):
        for (chunk, layer), parts in zip(chunks, grads):
            sides = halves(b, parts[0], parts[1])
            for which in range(2):
                for name, column, first, width in chunk.pieces(which):
                    if name == "pad":
                        continue
                    if name in extra:
                        extra[name][:, column : column + width] = sides[which][
                            :, first : first + width
                        ]
                        continue
                    full = FLAT[name[:-1]]
                    for r in range(ROWS):
                        to = r * full + column
                        work[name[:-1]][layer : layer + 1, to : to + width] = sides[which][
                            r : r + 1, first : first + width
                        ]
            if chunk.down:
                for r in range(2 * PAIR):
                    first = (r // PAIR) * D
                    work["down"][layer : layer + 1, r * D : (r + 1) * D] = parts[2][
                        r % PAIR : r % PAIR + 1, first : first + D
                    ]

    by_core(place, run)
    for i, name in enumerate(names):
        new = adam_math(
            fix_ref[0],
            flats[3 * i][...],
            flats[3 * i + 1][...],
            flats[3 * i + 2][...],
            work[name][...],
            rate_matrix,
            decay_matrix,
        )
        for k in range(3):
            outs[3 * i + k][...] = new[k]


def fetch_generic(masters, layer):
    flat = [lax.all_gather(m[layer].astype(BF16), AXES, axis=0, tiled=True) for m in masters]
    small = flat[4].reshape(D, 8 + FF // D)
    return (
        flat[0].reshape(D, 3 * D),
        flat[1].reshape(D, D),
        flat[2].reshape(D, FF),
        flat[3].reshape(FF, D),
        small,
    )


def on_device(crop_devices, dp_devices, *arguments):
    patches, kept_index, lengths, source_order, cot_tokens, cot_cls, step_count = arguments[:7]
    masters, firsts, seconds = arguments[7:12], arguments[12:17], arguments[17:22]
    crop_count, patch_count = patches.shape[0], patches.shape[1]
    keep_count = kept_index.shape[1]
    half = crop_count // 2
    devices = crop_devices * dp_devices
    owned = masters[0].shape[1] // (3 * D)
    staged = devices == 32 and owned == ROWS and crop_count <= ROWS
    y = lax.axis_index("crop")
    dp = lax.axis_index("dp")
    place = jnp.stack([y, (dp >> 2) & 3, (dp >> 1) & 1, dp & 1]).astype(jnp.int32)
    swap = functools.partial(lax.ppermute, axis_name="crop", perm=[(0, 1), (1, 0)])

    positions = jnp.arange(SLOTS, dtype=jnp.int32)[None, :]
    slots = jnp.concatenate([jnp.zeros((crop_count, 1), jnp.int32), kept_index + 1], 1)
    slots = jnp.pad(slots, ((0, 0), (0, SLOTS - keep_count - 1)))
    slots = jnp.where(positions <= lengths[:, None], slots, -1)

    crops_half = sds((half, SLOTS, D), BF16)
    tok_keep, tok_send = call(
        functools.partial(tokens_body, half, patch_count), [crops_half, crops_half]
    )(place, patches, slots)

    if staged:
        order = jnp.stack([source_order // 128, source_order % 128], 1).astype(F32)
        extra = jnp.zeros((16, CLS + ORDER + SMALL), F32)
        extra = extra.at[:, CLS : CLS + ORDER].set(-1.0)
        extra = extra.at[:crop_count, :CLS].set(cot_cls.astype(F32))
        extra = extra.at[:crop_count, CLS : CLS + 2].set(order)
        small_rows = jnp.transpose(masters[4].reshape(LAYERS, ROWS, ROWS), (1, 0, 2))
        extra = extra.at[:ROWS, CLS + ORDER : CLS + ORDER + 24].set(small_rows.reshape(ROWS, 24))
        own = (masters[0], masters[1], masters[2], extra)
        sib = [permute(item, 1) for item in own]
        packed = call(
            pack_body,
            [sds((PAIR, chunk.width), BF16) for chunk in GATHERED],
            scratch=[pltpu.VMEM((PAIR, max(c.width for c in GATHERED)), F32)],
        )(place, *own, *sib, masters[3])

    tok_recv = swap(tok_send)
    rows = (half + 1) * SLOTS
    x, bias, lens = call(
        functools.partial(arrange_body, half),
        [
            sds((rows, D), F32),
            sds((half + 1, SLOTS, SLOTS), F32),
            sds((2 * half, 128), F32),
        ],
    )(place, tok_keep, tok_recv)

    view_ids = crop_count * dp + half * y + jnp.arange(half, dtype=jnp.int32)
    focal_ids = view_ids + crop_count * dp_devices
    ids = jnp.concatenate([view_ids, focal_ids]).astype(F32)

    if staged:
        qkv0, proj0, small_table = gather_chunk(GATHERED[0], packed[0], place)
        up0, down0 = gather_chunk(GATHERED[1], packed[1], place)
        qkv1, proj1, up1, every_cot, every_order, down1 = gather_chunk(
            GATHERED[2], packed[2], place
        )
        matrices = ((qkv0, proj0, up0, down0), (qkv1, proj1, up1, down1))
        smalls = [small_table[:, 12 * layer : 12 * layer + 12] for layer in range(LAYERS)]
        order_column = every_order[:, 0:1].astype(F32) * 128.0 + every_order[:, 1:2].astype(F32)
    else:
        fetched = [fetch_generic(masters, layer) for layer in range(LAYERS)]
        matrices = [item[:4] for item in fetched]
        smalls = [item[4] for item in fetched]
        every_cot = lax.all_gather(cot_cls, AXES, axis=0, tiled=True)
        order_column = lax.all_gather(source_order, AXES, axis=0, tiled=True)
        order_column = order_column.astype(F32)[:, None]
    stacked = [jnp.transpose(item[:, :8]).astype(F32) for item in smalls]
    up_biases = [item[:, 8:].reshape(FF).astype(F32) for item in smalls]

    saved = []
    for layer in range(LAYERS):
        qkv_w, proj_w, up_w, down_w = matrices[layer]
        small = stacked[layer]
        one = layer_forward_one(x, bias, qkv_w, proj_w, small)
        normed_one, qkv, attended, prob, mid, normed_two = one
        nxt, active, slope = layer_forward_two(
            mid, normed_two, up_w, down_w, small, up_biases[layer]
        )
        saved.append((x, normed_one, qkv, attended, prob, mid, normed_two, active, slope))
        x = nxt

    out_keep, out_send, cls_rows = call(
        functools.partial(split_body, half, True),
        [crops_half, crops_half, sds((2 * half, D), F32)],
    )(place, x, lens)
    cot_send = lax.dynamic_slice_in_dim(cot_tokens, half * (1 - y), half, 0)
    cot_recv = swap(cot_send)
    chosen = (order_column == ids[None, :]).astype(BF16)
    grad_cls = dot(chosen, every_cot, 0, 0)
    dense_cls = jnp.dot(chosen, cls_rows.astype(BF16), preferred_element_type=F32).astype(BF16)
    g = call(functools.partial(top_body, half), sds((rows, D), F32))(
        place, cot_tokens, cot_recv, lens, grad_cls
    )
    out_recv = swap(out_send)
    block_out = call(
        functools.partial(join_body, half), sds((crop_count, SLOTS, D), BF16)
    )(place, out_keep, out_recv)

    step_value = step_count[0].astype(F32)
    fix = (1.0 - jnp.power(0.5, step_value)).reshape(1)
    gradients, reduced = [None] * LAYERS, []
    for layer in reversed(range(LAYERS)):
        xl, normed_one, qkv, attended, prob, mid, normed_two, active, slope = saved[layer]
        qkv_w, proj_w, up_w, down_w = matrices[layer]
        small = stacked[layer]
        g_mid, g_up, g_down, two = layer_backward_two(
            g, mid, normed_two, active, slope, up_w, down_w, small
        )
        if staged:
            reduced.append(reduce_chunk(REDUCED[2 * (1 - layer)], [g_up, g_down], place))
        g, g_qkv, g_proj, one = layer_backward_one(
            g_mid, xl, normed_one, qkv, attended, prob, qkv_w, proj_w, small
        )
        small_grad = small_gradient(two, one)
        gradients[layer] = (g_qkv, g_proj, g_up, g_down, small_grad)
        if staged and layer == 1:
            reduced.append(reduce_chunk(REDUCED[1], [g_qkv, g_proj, dense_cls], place))
        elif staged:
            both = jnp.concatenate([small_grad, gradients[1][4]], 1).astype(BF16)
            both = jnp.pad(both, ((0, 0), (0, SMALL - 24)))
            reduced.append(reduce_chunk(REDUCED[3], [g_qkv, g_proj, both], place))

    back_keep, back_send = call(
        functools.partial(split_body, half, False), [crops_half, crops_half]
    )(place, g, lens)
    back_recv = swap(back_send)
    patch_grad = call(
        functools.partial(scatter_body, half, patch_count), sds((crop_count, patch_count, D), F32)
    )(place, back_keep, back_recv, slots)

    results = [None] * 5

    def adam_call(chunks, names, kinds, parts, extra_shapes):
        flats = [item[kind] for kind in kinds for item in (masters, firsts, seconds)]
        shapes = [sds(f.shape, F32) for f in flats] + extra_shapes
        out = call(
            functools.partial(adam_body, (chunks, names)),
            shapes,
            scratch=[pltpu.VMEM(flats[3 * i].shape, F32) for i in range(len(names))],
            smem=2,
        )(place, fix, *[a for part in parts for a in part], *flats)
        for i, kind in enumerate(kinds):
            results[kind] = out[3 * i : 3 * i + 3]
        return out[3 * len(kinds) :]

    if staged:
        adam_call(
            [(REDUCED[0], 1), (REDUCED[2], 0)],
            ["up", "down"],
            [2, 3],
            [reduced[0], reduced[2]],
            [],
        )
        cls_own, small_own = adam_call(
            [(REDUCED[1], 1), (REDUCED[3], 0)],
            ["qkv", "proj"],
            [0, 1],
            [reduced[1], reduced[3]],
            [sds((ROWS, CLS), F32), sds((ROWS, SMALL), F32)],
        )
        cls_grouped = cls_own[:crop_count].astype(BF16)
        small_flat = jnp.transpose(small_own[:, :24].reshape(ROWS, 2, ROWS), (1, 0, 2))
        small_flat = small_flat.reshape(LAYERS, ROWS * ROWS)
        pending = [4]
        flat_grads = {4: small_flat}
    else:
        dense = lax.psum_scatter(dense_cls, AXES, scatter_dimension=0, tiled=True)
        cls_grouped = dense.astype(BF16)
        pending = range(5)
        flat_grads = {
            kind: jnp.stack(
                [
                    lax.psum_scatter(
                        gradients[layer][kind].reshape(-1).astype(F32),
                        AXES,
                        scatter_dimension=0,
                        tiled=True,
                    )
                    for layer in range(LAYERS)
                ]
            )
            for kind in range(5)
        }
    for kind in pending:
        results[kind] = adam_math(
            fix[0],
            masters[kind],
            firsts[kind],
            seconds[kind],
            flat_grads[kind],
            rate_small if kind == 4 else rate_matrix,
            0.0 if kind == 4 else decay_matrix,
        )
    return (
        (block_out, cls_grouped, patch_grad)
        + tuple(results[k][0] for k in range(5))
        + tuple(results[k][1] for k in range(5))
        + tuple(results[k][2] for k in range(5))
    )


def solution(mesh):
    crops = [P(AXES, None, None), P(AXES, None), P(AXES), P(AXES), P(AXES, None, None)]
    flat = P(None, AXES)
    return jax.shard_map(
        functools.partial(on_device, mesh.shape["crop"], mesh.shape["dp"]),
        mesh=mesh,
        in_specs=tuple(crops + [P(AXES, None), P()] + [flat] * 15),
        out_specs=(crops[0], crops[1], crops[0]) + (flat,) * 15,
        check_vma=False,
    )
```

```python
import functools

import jax
import jax.numpy as jnp
from jax import lax
from jax.experimental import pallas as pl
from jax.experimental.pallas import tpu as pltpu
from jax.sharding import PartitionSpec as P

D = 384
HEADS = 6
HEAD_DIM = 64
FF = 1536
LAYERS = 2
SLOTS = 144
FOCAL_SLOTS = 32
LEN_ROW = 143

eps_norm = 1e-06
neg_big = -1e30
adam_eps = 1e-08
rate_matrix = 0.04
decay_matrix = 0.05
rate_small = 0.4

F32 = jnp.float32
BF16 = jnp.bfloat16
VM = pl.BlockSpec(memory_space=pltpu.VMEM)
SM = pl.BlockSpec(memory_space=pltpu.SMEM)
AXES = ("crop", "dp")
VMEM_LIMIT = 20 * 1024 * 1024


def sds(shape, dtype):
    return jax.ShapeDtypeStruct(shape, dtype)


def call(body, out_shape, scratch=(), smem=1, cost=None):
    def run(*operands):
        moved = sum(a.size * a.dtype.itemsize for a in operands)
        moved += sum(a.size * a.dtype.itemsize for a in jax.tree.leaves(out_shape))
        return pl.pallas_call(
            body,
            out_shape=out_shape,
            in_specs=[SM] * smem + [VM] * (len(operands) - smem),
            out_specs=jax.tree.map(lambda _: VM, out_shape),
            scratch_shapes=list(scratch),
            compiler_params=pltpu.CompilerParams(vmem_limit_bytes=VMEM_LIMIT),
            cost_estimate=pl.CostEstimate(flops=cost or 0, bytes_accessed=moved, transcendentals=0),
        )(*operands)

    return run


def iota(shape, axis):
    return lax.broadcasted_iota(jnp.int32, shape, axis)


def dot(a, b, ca, cb):
    return lax.dot_general(a, b, (((ca,), (cb,)), ((), ())), preferred_element_type=F32)


def slot_onehot(slots, c, patch_count):
    row = slots[pl.ds(c, 1), :]
    return row, (iota((patch_count, SLOTS), 0) == row).astype(F32).astype(BF16)


def tokens_body(half, patch_count, place, patches, slots, keep, send):
    y = place[1]
    row_index = iota((SLOTS, D), 0)
    for i in range(half):
        for out, c in ((keep, half * y + i), (send, half * (1 - y) + i)):
            row, onehot = slot_onehot(slots, c, patch_count)
            count = jnp.sum((row >= 0).astype(F32), axis=1, keepdims=True) - 1.0
            picked = dot(onehot, patches[c], 0, 0)
            out[i] = jnp.where(row_index == LEN_ROW, count, picked).astype(BF16)


def arrange_body(half, place, keep, recv, x_ref, bias_ref, lens_ref):
    y = place[1]
    base = half * SLOTS
    used = half * FOCAL_SLOTS

    def run(v_src, f_src):
        k = iota((SLOTS, SLOTS), 0)
        q = iota((SLOTS, SLOTS), 1)
        row_index = iota((SLOTS, D), 0)
        for i in range(half):
            t = v_src[i].astype(F32)
            n = t[LEN_ROW : LEN_ROW + 1, 0:1]
            x_ref[SLOTS * i : SLOTS * (i + 1), :] = jnp.where(row_index == LEN_ROW, 0.0, t)
            bias_ref[i] = jnp.where(k.astype(F32) <= n, 0.0, neg_big)
            lens_ref[i : i + 1, :] = jnp.broadcast_to(n, (1, 128))
        limit = jnp.full((SLOTS, SLOTS), 1000.0, F32)
        for i in range(half):
            x_ref[base + FOCAL_SLOTS * i : base + FOCAL_SLOTS * (i + 1), :] = f_src[
                i, 0:FOCAL_SLOTS
            ].astype(F32)
            n = f_src[i, SLOTS - 16 : SLOTS].astype(F32)[15:16, 0:1]
            limit = jnp.where((k // FOCAL_SLOTS) == i, n, limit)
            lens_ref[half + i : half + i + 1, :] = jnp.broadcast_to(n, (1, 128))
        if used < SLOTS:
            x_ref[base + used : base + SLOTS, :] = jnp.zeros((SLOTS - used, D), F32)
        same = (q // FOCAL_SLOTS) == (k // FOCAL_SLOTS)
        inside = (k % FOCAL_SLOTS).astype(F32) <= limit
        bias_ref[half] = jnp.where(same & inside, 0.0, neg_big)

    @pl.when(y == 0)
    def _():
        run(keep, recv)

    @pl.when(y == 1)
    def _():
        run(recv, keep)


def turn_body(half, first_ids, place, x_ref, lens, cot, recv, order, every_cot, *outs):
    keep, send, g_ref, dense = outs
    y = place[1]
    base = half * SLOTS
    used = half * FOCAL_SLOTS
    views, focals = first_ids(place)
    index = iota((2 * half, 1), 0)
    ids = jnp.where(index < half, views + index, focals + index - half).astype(F32)
    chosen = (order[...] == ids).astype(F32).astype(BF16)
    top = dot(chosen, every_cot[...], 1, 0)

    def piece(values, n, row, rows):
        at = iota((rows, D), 0)
        masked = jnp.where(at.astype(F32) <= n, values, 0.0)
        return masked + jnp.where(at == 0, row, 0.0)

    def run(v_out, f_out, v_get, f_get):
        cls = []
        for i in range(half):
            n = lens[i : i + 1, 0:1]
            rows = slice(SLOTS * i, SLOTS * (i + 1))
            v = x_ref[rows, :]
            cls.append(v[0:1])
            v_out[i] = jnp.where(iota((SLOTS, D), 0).astype(F32) <= n, v, 0.0).astype(BF16)
            g_ref[rows, :] = piece(v_get(i).astype(F32), n, top[i : i + 1], SLOTS)
        for i in range(half):
            n = lens[half + i : half + i + 1, 0:1]
            rows = slice(base + FOCAL_SLOTS * i, base + FOCAL_SLOTS * (i + 1))
            f = x_ref[rows, :]
            cls.append(f[0:1])
            f = jnp.where(iota((FOCAL_SLOTS, D), 0).astype(F32) <= n, f, 0.0)
            f_out[i, 0:FOCAL_SLOTS] = f.astype(BF16)
            f_out[i, FOCAL_SLOTS:SLOTS] = jnp.zeros((SLOTS - FOCAL_SLOTS, D), BF16)
            g_ref[rows, :] = piece(
                f_get(i)[0:FOCAL_SLOTS].astype(F32), n, top[half + i : half + i + 1], FOCAL_SLOTS
            )
        if used < SLOTS:
            g_ref[base + used : base + SLOTS, :] = jnp.zeros((SLOTS - used, D), F32)
        dense[...] = dot(chosen, jnp.concatenate(cls, 0).astype(BF16), 0, 0)

    @pl.when(y == 0)
    def _():
        run(keep, send, lambda i: cot[i], lambda i: recv[i])

    @pl.when(y == 1)
    def _():
        run(send, keep, lambda i: recv[i], lambda i: cot[half + i])


def split_body(half, place, x_ref, keep, send):
    y = place[1]
    base = half * SLOTS

    def run(v_out, f_out):
        for i in range(half):
            v_out[i] = x_ref[SLOTS * i : SLOTS * (i + 1), :].astype(BF16)
            rows = slice(base + FOCAL_SLOTS * i, base + FOCAL_SLOTS * (i + 1))
            f_out[i, 0:FOCAL_SLOTS] = x_ref[rows, :].astype(BF16)
            f_out[i, FOCAL_SLOTS:SLOTS] = jnp.zeros((SLOTS - FOCAL_SLOTS, D), BF16)

    @pl.when(y == 0)
    def _():
        run(keep, send)

    @pl.when(y == 1)
    def _():
        run(send, keep)


def join_body(half, place, keep, recv, out):
    y = place[1]
    for i in range(half):
        out[half * y + i] = keep[i]
        out[half * (1 - y) + i] = recv[i]


def scatter_body(half, patch_count, place, keep, recv, slots, out):
    y = place[1]
    for i in range(half):
        for src, c in ((keep, half * y + i), (recv, half * (1 - y) + i)):
            _, onehot = slot_onehot(slots, c, patch_count)
            out[c] = dot(onehot, src[i], 1, 0)


def lane_mask(second, value):
    lane = iota((1, 128), 1)
    chosen = (lane >= HEAD_DIM) if second else (lane < HEAD_DIM)
    return jnp.where(chosen, value, 0.0).astype(BF16)


def attend_forward_body(qkv_ref, bias_ref, att_ref, prob_ref):
    bias = bias_ref[0]
    for pair in range(HEADS // 2):
        at = 128 * pair
        q = qkv_ref[:, at : at + 128]
        k = qkv_ref[:, D + at : D + at + 128]
        v = qkv_ref[:, 2 * D + at : 2 * D + at + 128]
        joined = None
        for h in range(2):
            s = dot(k * lane_mask(h, HEAD_DIM**-0.5), q, 1, 1) + bias
            e = jnp.exp(s - jnp.max(s, 0, keepdims=True))
            p = (e * (1.0 / jnp.sum(e, 0, keepdims=True))).astype(BF16)
            prob_ref[0, 2 * pair + h] = p
            o = dot(p, v * lane_mask(h, 1.0), 0, 0)
            joined = o if joined is None else joined + o
        att_ref[:, at : at + 128] = joined.astype(BF16)


def attend_backward_block(qkv_ref, prob_ref, grad_ref, out_ref, rows, b):
    for pair in range(HEADS // 2):
        at = 128 * pair
        q = qkv_ref[rows, at : at + 128]
        k = qkv_ref[rows, D + at : D + at + 128]
        v = qkv_ref[rows, 2 * D + at : 2 * D + at + 128]
        g = grad_ref[rows, at : at + 128]
        dq = dk = dv = None
        for h in range(2):
            pb = prob_ref[b, 2 * pair + h]
            p = pb.astype(F32)
            gh = g * lane_mask(h, 1.0)
            scaled = lane_mask(h, HEAD_DIM**-0.5)
            t = p * dot(v, gh, 1, 1)
            ds = (t - p * jnp.sum(t, 0, keepdims=True)).astype(BF16)
            parts = (dot(ds, k * scaled, 0, 0), dot(ds, q * scaled, 1, 0), dot(pb, gh, 1, 0))
            if dq is None:
                dq, dk, dv = parts
            else:
                dq, dk, dv = dq + parts[0], dk + parts[1], dv + parts[2]
        out_ref[rows, at : at + 128] = dq.astype(BF16)
        out_ref[rows, D + at : D + at + 128] = dk.astype(BF16)
        out_ref[rows, 2 * D + at : 2 * D + at + 128] = dv.astype(BF16)


def row_block(width):
    return pl.BlockSpec((SLOTS, width), lambda b: (b, 0))


def attend_forward(qkv, bias):
    blocks = bias.shape[0]
    return pl.pallas_call(
        attend_forward_body,
        grid=(blocks,),
        in_specs=[row_block(3 * D), pl.BlockSpec((1, SLOTS, SLOTS), lambda b: (b, 0, 0))],
        out_specs=[row_block(D), pl.BlockSpec((1, HEADS, SLOTS, SLOTS), lambda b: (b, 0, 0, 0))],
        out_shape=[
            sds((blocks * SLOTS, D), BF16),
            sds((blocks, HEADS, SLOTS, SLOTS), BF16),
        ],
        compiler_params=pltpu.CompilerParams(vmem_limit_bytes=VMEM_LIMIT),
        cost_estimate=pl.CostEstimate(
            flops=blocks * HEADS * SLOTS * SLOTS * 512,
            bytes_accessed=blocks * SLOTS * D * 16,
            transcendentals=blocks * HEADS * SLOTS * SLOTS,
        ),
    )(qkv, bias)


def total(values):
    return jnp.sum(values, 0, keepdims=True)


def normalized(values):
    centered = values - jnp.mean(values, -1, keepdims=True)
    scale = lax.rsqrt(jnp.mean(centered * centered, -1, keepdims=True) + eps_norm)
    return centered * scale, scale


def gelu_parts(v):
    c = 0.7978845608028654
    a = 0.044715
    square = v * v
    t = jnp.tanh(c * (v + a * v * square))
    value = 0.5 * v * (1.0 + t)
    slope = 0.5 * (1.0 + t) + 0.5 * v * (1.0 - t * t) * c * (1.0 + 3.0 * a * square)
    return value, slope


def layer_forward_one(x, bias, qkv_w, proj_w, small):
    unit, _ = normalized(x)
    normed_one = (unit * small[0:1] + small[1:2]).astype(BF16)
    qkv_bias = jnp.concatenate([small[2], jnp.zeros((D,), F32), small[3]])
    qkv = (jnp.dot(normed_one, qkv_w, preferred_element_type=F32) + qkv_bias).astype(BF16)
    attended, prob = attend_forward(qkv, bias)
    mid = x + jnp.dot(attended, proj_w, preferred_element_type=F32) + small[4]
    unit, _ = normalized(mid)
    normed_two = (unit * small[5] + small[6]).astype(BF16)
    return normed_one, qkv, attended, prob, mid, normed_two


def layer_forward_two(mid, normed_two, up_w, down_w, small, up_bias):
    hidden = jnp.dot(normed_two, up_w, preferred_element_type=F32) + up_bias
    value, slope = gelu_parts(hidden)
    active, slope = value.astype(BF16), slope.astype(BF16)
    out = mid + jnp.dot(active, down_w, preferred_element_type=F32) + small[7]
    return out, active, slope


def over_blocks(count, step):
    def body(b, _):
        step(pl.ds(pl.multiple_of(b * SLOTS, 16), SLOTS), b)
        return 0

    lax.fori_loop(0, count, body, 0)


def norm_back(grad, values, gain):
    unit, scale = normalized(values)
    inner = grad * gain
    mean, along = jnp.mean(inner, -1, keepdims=True), jnp.mean(inner * unit, -1, keepdims=True)
    return scale * (inner - mean - unit * along), unit


def mlp_weights_body(finish, place, g, normed, active, slope, down_w, *refs):
    outs, (branch, up, down) = refs[:-3], refs[-3:]
    g_hidden, bias_up = outs[-2:]
    branch[...] = g[...].astype(BF16)
    for c in range(FF // D):
        w = slice(c * D, (c + 1) * D)
        t = (dot(branch[...], down_w[w, :], 1, 1) * slope[:, w].astype(F32)).astype(BF16)
        g_hidden[:, w] = t
        bias_up[:, w] = total(t.astype(F32))
    for c in range(FF // D):
        w = slice(c * D, (c + 1) * D)
        down[w, :] = dot(active[:, w], branch[...], 0, 0)
    up[...] = dot(normed[...], g_hidden[...], 0, 0)
    finish(place, (up, down), outs[:-2])


def mlp_rows_body(g, g_hidden, mid, attended, up_w, proj_w, small, g_mid, g_proj, g_att, rows, work):
    rows[...] = jnp.zeros(rows.shape, F32)
    g_mid[...] = dot(g_hidden[...], up_w[...], 1, 1)

    def step(r, _):
        grad = g_mid[r, :]
        back, unit = norm_back(grad, mid[r, :], small[5:6])
        whole = back + g[r, :]
        g_mid[r, :] = whole
        rounded = whole.astype(BF16)
        work[r, :] = rounded
        rows[0:1] += total(grad * unit)
        rows[1:2] += total(grad)
        rows[2:3] += total(g[r, :].astype(BF16).astype(F32))
        rows[3:4] += total(rounded.astype(F32))

    over_blocks(g.shape[0] // SLOTS, step)
    g_att[...] = dot(work[...], proj_w[...], 1, 1).astype(BF16)
    g_proj[...] = dot(attended[...], work[...], 0, 0)


def qkv_weights_body(finish, extra_count, place, g_att, normed, qkv, prob, x, qkv_w, *refs):
    extra, outs, (g_qkv, weight) = refs[:extra_count], refs[extra_count:-2], refs[-2:]
    g_normed, rows = outs[-2:]
    rows[...] = jnp.zeros(rows.shape, F32)
    count = x.shape[0] // SLOTS
    over_blocks(count, lambda r, b: attend_backward_block(qkv, prob, g_att, g_qkv, r, b))
    g_normed[...] = dot(g_qkv[...], qkv_w[...], 1, 1)

    def step(r, _):
        unit, _ = normalized(x[r, :])
        grad = g_normed[r, :]
        rows[0:1] += total(grad * unit)
        rows[1:2] += total(grad)
        rows[2:3] += total(g_qkv[r, 0:D].astype(F32))
        rows[3:4] += total(g_qkv[r, 2 * D : 3 * D].astype(F32))

    over_blocks(count, step)
    weight[...] = dot(normed[...], g_qkv[...], 0, 0)
    finish(place, (weight,) + extra, outs[:-2], rows)


def norm_one_body(g_normed, x, g_mid, small, out):
    def step(r, _):
        out[r, :] = norm_back(g_normed[r, :], x[r, :], small[0:1])[0] + g_mid[r, :]

    over_blocks(x.shape[0] // SLOTS, step)


def mlp_weights(place, finish, shapes, g, normed, active, slope, down_w):
    rows = g.shape[0]
    return call(
        functools.partial(mlp_weights_body, finish),
        list(shapes) + [sds((rows, FF), BF16), sds((1, FF), F32)],
        scratch=[
            pltpu.VMEM((rows, D), BF16),
            pltpu.VMEM((D, FF), F32),
            pltpu.VMEM((FF, D), F32),
        ],
        cost=8 * rows * D * FF,
    )(place, g, normed, active, slope, down_w)


def mlp_rows(g, g_hidden, mid, attended, up_w, proj_w, small):
    rows = g.shape[0]
    return call(
        mlp_rows_body,
        [sds((rows, D), F32), sds((D, D), F32), sds((rows, D), BF16), sds((8, D), F32)],
        scratch=[pltpu.VMEM((rows, D), BF16)],
        smem=0,
        cost=4 * rows * D * FF,
    )(g, g_hidden, mid, attended, up_w, proj_w, small)


def qkv_weights(place, finish, shapes, extra, g_att, normed, qkv, prob, x, qkv_w):
    rows = x.shape[0]
    return call(
        functools.partial(qkv_weights_body, finish, len(extra)),
        list(shapes) + [sds((rows, D), F32), sds((8, D), F32)],
        scratch=[pltpu.VMEM((rows, 3 * D), BF16), pltpu.VMEM((D, 3 * D), F32)],
        cost=12 * rows * D * FF,
    )(place, g_att, normed, qkv, prob, x, qkv_w, *extra)


def norm_one(g_normed, x, g_mid, small):
    return call(norm_one_body, sds(x.shape, F32), smem=0)(g_normed, x, g_mid, small)


def small_table(groups):
    flat, wide = [], []
    lane = iota((1, FF), 1) % 4
    for rows_one, rows_two, bias_up in groups:
        flat += [rows_one[0:4, :], rows_two[3:4, :], rows_two[0:3, :], jnp.zeros((4, D), F32)]
        wide += [jnp.zeros((8, FF), F32)]
        wide += [jnp.where(lane == k, bias_up[...], 0.0) for k in range(4)]
    flat = jnp.concatenate(flat + [jnp.zeros((8, D), F32)], 0).astype(BF16)
    wide = jnp.concatenate(wide + [jnp.zeros((8, FF), F32)], 0).astype(BF16)
    same = (iota((D, D), 0) == iota((D, D), 1)).astype(F32).astype(BF16)
    spread = (iota((D, FF), 1) // 4 == iota((D, FF), 0)).astype(F32).astype(BF16)
    return dot(same, flat, 1, 1) + dot(spread, wide, 1, 1)


ROWS = 12
PAIR = 24
CHIPS = 16
QKV, PROJ, UP, SMALL, CLS, ORDER, PAD = 3 * D, D, FF, 128, D, 128, 128
CORE = (1, 1)
TABLES = ("small", "order")
GATHER_STAGES = ((4, 8), (8, 4), (2, 16), (16, 2))


class Chunk:
    def __init__(self, names, widths, down):
        self.names, self.widths, self.down = names, widths, down
        self.half = sum(widths) // 2
        self.width = self.half + (2 * D if down else 0)
        self.arrays = [n for n in names if n != "pad"] + (["down"] if down else [])
        self.layer = int(names[0][-1])

    def pieces(self, which):
        low, high, start, found = which * self.half, (which + 1) * self.half, 0, []
        for name, width in zip(self.names, self.widths):
            a, b = max(start, low), min(start + width, high)
            if a < b:
                found.append((name, a - start, a - low, b - a))
            start += width
        return found


GATHERED = (
    Chunk(("qkv0", "proj0", "up0", "small", "pad"), (QKV, PROJ, UP, SMALL, PAD), True),
    Chunk(("qkv1", "proj1", "cls", "order"), (QKV, PROJ, CLS, ORDER), False),
    Chunk(("up1",), (UP,), True),
)
MLP_SUMS = (Chunk(("up0",), (UP,), True), Chunk(("up1",), (UP,), True))
QKV_SUMS = (
    Chunk(("qkv0", "proj0", "small", "pad"), (QKV, PROJ, SMALL, PAD), False),
    Chunk(("qkv1", "proj1", "cls", "pad"), (QKV, PROJ, CLS, PAD), False),
)
FLAT = {"qkv": QKV, "proj": PROJ, "up": UP}


def by_core(place, run):
    for b in range(2):

        @pl.when((place[0] & 1) == b)
        def _(b=b):
            run(b)


def chip_of(place, core, bits):
    mask = 0
    for bit, stage in zip(bits, GATHER_STAGES):
        mask ^= stage[core] * bit
    return (place[0] ^ mask) >> 1


def bits_of(index, count=4):
    return [(index >> k) & 1 for k in range(count)]


def tie(*values):
    return lax.optimization_barrier(values)


def small_block(flat, layer):
    row = flat[layer : layer + 1, :].astype(BF16).astype(F32)
    width = ROWS * ROWS
    spread = jnp.where(iota((16, width), 1) // ROWS == iota((16, width), 0), row, 0.0).astype(BF16)
    at = iota((width, 128), 0) % ROWS + ROWS * layer
    chosen = (at == iota((width, 128), 1)).astype(F32).astype(BF16)
    return dot(spread, chosen, 1, 0)[0:ROWS]


def order_block(ref):
    count = ref.shape[1]
    row = ref[...].astype(F32)
    mine = iota((16, count), 0) == iota((16, count), 1)
    number = jnp.sum(jnp.where(mine, row, 0.0), 1, keepdims=True)
    number = jnp.where(iota((16, 1), 0) < count, number, -129.0)
    high = jnp.floor(number * (1.0 / 128.0))
    lane = iota((16, 128), 1)
    return jnp.where(lane == 0, high, number - 128.0 * high)[0:ROWS]


def pack_body(place, *refs):
    held, (keep, send, down_out), local, sem = refs[0:7], refs[7:10], refs[10:17], refs[17]
    copies = [
        pltpu.make_async_copy(src, dst, sem.at[i]) for i, (src, dst) in enumerate(zip(held, local))
    ]
    for copy in copies:
        copy.start()
    for copy in copies:
        copy.wait()
    source = dict(zip(("qkv", "proj", "up", "small", "cls", "order"), local))
    down = local[6]

    def run(b):
        base = 0
        for chunk in GATHERED:
            for out, which in ((keep, b), (send, 1 - b)):
                for name, column, at, width in chunk.pieces(which):
                    span = slice(base + at, base + at + width)
                    if name == "pad":
                        out[:, span] = jnp.zeros((ROWS, width), F32)
                    elif name == "small":
                        out[:, span] = small_block(source["small"], 0) + small_block(
                            source["small"], 1
                        )
                    elif name == "order":
                        out[:, span] = order_block(source["order"])
                    elif name == "cls":
                        count = source["cls"].shape[0]
                        out[:, span] = jnp.zeros((ROWS, width), F32)
                        out[0:count, span] = source["cls"][:, column : column + width].astype(F32)
                    else:
                        flat, full = source[name[:-1]], FLAT[name[:-1]]
                        for r in range(ROWS):
                            first = r * full + column
                            out[r : r + 1, span] = flat[
                                chunk.layer : chunk.layer + 1, first : first + width
                            ]
            base += chunk.half

    by_core(place, run)
    for layer in range(LAYERS):
        for r in range(2 * PAIR):
            first = (2 * layer + r // PAIR) * D
            down_out[r % PAIR : r % PAIR + 1, first : first + D] = down[
                layer : layer + 1, r * D : (r + 1) * D
            ]


def merge_body(place, keep, recv, down, first, second, work):
    def run(b):
        work[ROWS * b : ROWS * (b + 1), :] = keep[...]
        work[ROWS * (1 - b) : ROWS * (2 - b), :] = recv[...]

    by_core(place, run)
    source = target = 0
    for number, chunk in enumerate(GATHERED):
        out = second if number else first
        if number == 1:
            target = 0
        out[0, :, target : target + chunk.half] = work[:, source : source + chunk.half].astype(BF16)
        if chunk.down:
            at, first = target + chunk.half, 2 * D * chunk.layer
            out[0, :, at : at + 2 * D] = down[:, first : first + 2 * D].astype(BF16)
        source, target = source + chunk.half, target + chunk.width


def unpack_body(chunk, place, *refs):
    own, sib, outs = refs[0:2], refs[2:4], refs[4:]
    target = dict(zip([n for n in chunk.arrays if n not in TABLES], outs))
    if "small" in chunk.names:
        rows_out, up_out, target["small"] = outs[-3:]
    if "order" in chunk.names:
        order_out, target["order"] = outs[-2:]

    def run(b):
        for which in range(2):
            source = own if which == b else sib
            for received in range(2):
                block = source[received]

                def step(index, _, which=which, received=received, block=block):
                    chip = chip_of(place, which, bits_of(index, 3) + [received])
                    for name, column, at, width in chunk.pieces(which):
                        if name == "pad":
                            continue
                        values = block[index, :, at : at + width]
                        if name in TABLES:
                            values = values.astype(F32)
                        target[name][chip, :, column : column + width] = values
                    for part in range(2 if chunk.down else 0):
                        first = chunk.half + part * D
                        target["down"][chip * 4 + 2 * which + part] = block[
                            index, :, first : first + D
                        ]
                    return 0

                lax.fori_loop(0, CHIPS // 2, step, 0)

    by_core(place, run)
    if "order" in chunk.names:
        across = jnp.transpose(target["order"][...].reshape(D, ORDER))
        order_out[...] = across[0:1] * 128.0 + across[1:2]
    if "small" in chunk.names:
        across = jnp.transpose(target["small"][...].reshape(D, SMALL))
        rows_out[...] = across[0:24]
        ups = jnp.concatenate([across[8:12], across[20:24]], 0).astype(BF16)
        spread = (iota((D, FF), 1) // 4 == iota((D, FF), 0)).astype(F32).astype(BF16)
        wide = dot(ups, spread, 1, 0)
        lane = iota((1, FF), 1) % 4
        for layer in range(LAYERS):
            row = jnp.zeros((1, FF), F32)
            for k in range(4):
                row = jnp.where(lane == k, wide[4 * layer + k : 4 * layer + k + 1], row)
            up_out[layer : layer + 1, :] = row


def permute(x, masks):
    return lax.ppermute(x, AXES, [(i, i ^ masks[i & 1]) for i in range(2 * CHIPS)])


def unpack(chunk, pieces, sib, place):
    shapes = [
        sds((CHIPS, PAIR, width), BF16)
        for name, width in zip(chunk.names, chunk.widths)
        if name != "pad" and name not in TABLES
    ]
    if chunk.down:
        shapes.append(sds((4 * CHIPS, PAIR, D), BF16))
    count, scratch = len(shapes), []
    if "small" in chunk.names:
        shapes += [sds((24, D), F32), sds((LAYERS, FF), F32)]
        scratch = [pltpu.VMEM((CHIPS, PAIR, SMALL), F32)]
    if "order" in chunk.names:
        shapes += [sds((1, D), F32)]
        scratch = [pltpu.VMEM((CHIPS, PAIR, ORDER), F32)]
    out = call(functools.partial(unpack_body, chunk), shapes, scratch=scratch)(
        place, *pieces, *sib
    )
    return [b.reshape(-1, b.shape[2]) for b in out[:count]] + list(out[count:])


def arrange_sums(chunk, place, matrices, keep, send):
    source = dict(zip(chunk.arrays, matrices))

    def run(b):
        for out, which in ((keep, b), (send, 1 - b)):

            def step(index, _, out=out, which=which):
                chip = chip_of(place, which, bits_of(index))
                rows = pl.ds(pl.multiple_of(chip * PAIR, 8), PAIR)
                for name, column, at, width in chunk.pieces(which):
                    if name == "pad":
                        out[index, :, at : at + width] = jnp.zeros((PAIR, width), BF16)
                    else:
                        out[index, :, at : at + width] = source[name][
                            rows, column : column + width
                        ].astype(BF16)
                for part in range(2 if chunk.down else 0):
                    at = chunk.half + part * D
                    first = pl.multiple_of((chip * 4 + 2 * which + part) * PAIR, 8)
                    out[index, :, at : at + D] = source["down"][pl.ds(first, PAIR), :].astype(BF16)
                return 0

            lax.fori_loop(0, CHIPS, step, 0)

    by_core(place, run)


def sum_shapes(chunk):
    return [sds((CHIPS, PAIR, chunk.width), BF16)] * 2


def split_rows_body(chunk, place, own, recv, keep, send, *down_out):
    def run(b):
        whole = own[...] + recv[...].astype(F32)
        for out, core in ((keep, b), (send, 1 - b)):
            out[...] = whole[ROWS * core : ROWS * (core + 1), : chunk.half]
        if chunk.down:
            down_out[0][...] = whole[:, chunk.half :]

    by_core(place, run)


class Reduction:
    def __init__(self, chunk, keep, send, place):
        self.chunk, self.place, self.stage = chunk, place, 0
        self.keep, self.send = keep, send
        self.masks = (CORE,) + GATHER_STAGES[::-1] + (CORE,)

    def move(self):
        self.stage += 1
        return permute(self.send, self.masks[self.stage - 1])

    def absorb(self, recv):
        if self.stage <= 4:
            middle = recv.shape[0] // 2
            low = self.keep[:middle].astype(F32) + recv[:middle].astype(F32)
            high = self.keep[middle:].astype(F32) + recv[middle:].astype(F32)
            self.keep, self.send = low, high.astype(BF16)
        elif self.stage == 5:
            chunk = self.chunk
            shapes = [sds((ROWS, chunk.half), F32)] * 2
            if chunk.down:
                shapes.append(sds((PAIR, 2 * D), F32))
            self.keep, self.send, *self.rest = call(
                functools.partial(split_rows_body, chunk), shapes
            )(self.place, self.keep[0], recv[0])
        else:
            self.result = (self.keep, recv) + tuple(self.rest)


class Transfer:
    def __init__(self, swap, send):
        self.swap, self.send = swap, send

    def move(self):
        return self.swap(self.send)

    def absorb(self, recv):
        self.recv = recv


def beside(moving, run, *inputs):
    count = len(moving)
    tied = tie(*[m.send for m in moving], *inputs)
    for m, send in zip(moving, tied):
        m.send = send
    received = [m.move() for m in moving]
    out = run(*tied[count:])
    many = isinstance(out, (tuple, list))
    tied = tie(*received, *(out if many else (out,)))
    for m, recv in zip(moving, tied):
        m.absorb(recv)
    return tied[count:] if many else tied[count]


def adam_math(fix, master, first, second, grad, rate, decay):
    moment = 0.5 * first + 0.5 * grad
    square = 0.5 * second + 0.5 * grad * grad
    update = moment / fix / (jnp.sqrt(square / fix) + adam_eps) + decay * master
    return master - rate * update, moment, square


def adam_body(plan, place, fix_ref, *refs):
    chunks, names, extras = plan
    grads, at = [], 0
    for chunk, _ in chunks:
        size = 3 if chunk.down else 2
        grads.append(refs[at : at + size])
        at += size
    flats = refs[at : at + 3 * len(names)]
    outs = refs[at + 3 * len(names) : at + 6 * len(names)]
    rest = refs[at + 6 * len(names) :]
    extra = dict(zip(extras, rest))
    work = dict(zip(names, rest[len(extras) :]))

    def run(b):
        for (chunk, layer), parts in zip(chunks, grads):
            sides = (parts[0], parts[1]) if b == 0 else (parts[1], parts[0])
            for which in range(2):
                for name, column, first, width in chunk.pieces(which):
                    span = slice(first, first + width)
                    if name in extra:
                        extra[name][:, column : column + width] = sides[which][:, span]
                    elif name[:-1] in work:
                        full = FLAT[name[:-1]]
                        for r in range(ROWS):
                            to = r * full + column
                            work[name[:-1]][layer : layer + 1, to : to + width] = sides[which][
                                r : r + 1, span
                            ]
            if chunk.down and "down" in work:
                for r in range(2 * PAIR):
                    first = (r // PAIR) * D
                    work["down"][layer : layer + 1, r * D : (r + 1) * D] = parts[2][
                        r % PAIR : r % PAIR + 1, first : first + D
                    ]

    by_core(place, run)
    for i, name in enumerate(names):
        new = adam_math(
            fix_ref[0],
            flats[3 * i][...],
            flats[3 * i + 1][...],
            flats[3 * i + 2][...],
            work[name][...],
            rate_matrix,
            decay_matrix,
        )
        for k in range(3):
            outs[3 * i + k][...] = new[k]


class Step:
    def __init__(self, crop_devices, dp_devices, arguments):
        (
            self.patches,
            self.kept_index,
            self.lengths,
            self.source_order,
            self.cot_tokens,
            self.cot_cls,
            step_count,
        ) = arguments[:7]
        self.masters, self.firsts, self.seconds = arguments[7:12], arguments[12:17], arguments[17:22]
        self.crop_count, self.patch_count = self.patches.shape[:2]
        self.half = self.crop_count // 2
        self.dp_devices = dp_devices
        me = lax.axis_index(AXES)
        self.place = jnp.stack([me, me // dp_devices]).astype(jnp.int32)
        self.swap = functools.partial(lax.ppermute, axis_name="crop", perm=[(0, 1), (1, 0)])
        self.crops_half = sds((self.half, SLOTS, D), BF16)
        self.rows = (self.half + 1) * SLOTS
        self.fix = (1.0 - jnp.power(0.5, step_count[0].astype(F32))).reshape(1)

    def tokens(self):
        positions = jnp.arange(SLOTS, dtype=jnp.int32)[None, :]
        slots = jnp.pad(self.kept_index + 1, ((0, 0), (1, SLOTS - self.kept_index.shape[1] - 1)))
        self.slots = jnp.where(positions <= self.lengths[:, None], slots, -1)
        return call(
            functools.partial(tokens_body, self.half, self.patch_count), [self.crops_half] * 2
        )(self.place, self.patches, self.slots)

    def arrange(self, keep, recv):
        return call(
            functools.partial(arrange_body, self.half),
            [
                sds((self.rows, D), F32),
                sds((self.half + 1, SLOTS, SLOTS), F32),
                sds((2 * self.half, 128), F32),
            ],
        )(self.place, keep, recv)

    def first_ids(self, place):
        views = self.crop_count * (place[0] - place[1] * self.dp_devices) + self.half * place[1]
        return views, views + self.crop_count * self.dp_devices

    def cot_send(self):
        return lax.dynamic_slice_in_dim(
            self.cot_tokens, self.half * (1 - self.place[1]), self.half, 0
        )

    def turn(self, x, lens, cot_recv, order, every_cot):
        shapes = [self.crops_half] * 2 + [sds((self.rows, D), F32), sds(every_cot.shape, F32)]
        return call(functools.partial(turn_body, self.half, self.first_ids), shapes)(
            self.place, x, lens, self.cot_tokens, cot_recv, order, every_cot
        )

    def split(self, x):
        return call(functools.partial(split_body, self.half), [self.crops_half] * 2)(self.place, x)

    def join(self, keep, recv):
        return call(
            functools.partial(join_body, self.half), sds((self.crop_count, SLOTS, D), BF16)
        )(self.place, keep, recv)

    def scatter(self, keep, recv):
        return call(
            functools.partial(scatter_body, self.half, self.patch_count),
            sds((self.crop_count, self.patch_count, D), F32),
        )(self.place, keep, recv, self.slots)

    def adam_flat(self, kind, grad):
        return adam_math(
            self.fix[0],
            self.masters[kind],
            self.firsts[kind],
            self.seconds[kind],
            grad,
            rate_small if kind == 4 else rate_matrix,
            0.0 if kind == 4 else decay_matrix,
        )

    def adam_rows(self, fix, chunks, names, kinds, parts, extras):
        flats = [f[kind] for kind in kinds for f in (self.masters, self.firsts, self.seconds)]
        shapes = [sds(f.shape, F32) for f in flats] + [shape for _, shape in extras]
        plan = (chunks, names, [name for name, _ in extras])
        out = call(
            functools.partial(adam_body, plan),
            shapes,
            scratch=[pltpu.VMEM(flats[3 * i].shape, F32) for i in range(len(names))],
            smem=2,
        )(self.place, fix, *[a for part in parts for a in part], *flats)
        return [list(out[3 * i : 3 * i + 3]) for i in range(len(kinds))], out[3 * len(kinds) :]


def outputs(block_out, cls_grouped, patch_grad, results):
    return (block_out, cls_grouped, patch_grad) + tuple(
        results[kind][part] for part in range(3) for kind in range(5)
    )


def pack_call(place, operands, shapes):
    return pl.pallas_call(
        pack_body,
        in_specs=[SM] + [pl.BlockSpec(memory_space=pltpu.HBM)] * len(operands),
        out_specs=[VM] * len(shapes),
        out_shape=shapes,
        scratch_shapes=[pltpu.VMEM(a.shape, a.dtype) for a in operands]
        + [pltpu.SemaphoreType.DMA((len(operands),))],
        compiler_params=pltpu.CompilerParams(vmem_limit_bytes=VMEM_LIMIT),
    )(place, *operands)


def staged_step(step):
    place = step.place
    total_half = sum(c.half for c in GATHERED)
    rows_shape = sds((ROWS, total_half), F32)
    keep, send, downs = pack_call(
        place,
        step.masters[:3]
        + (step.masters[4], step.cot_cls, step.source_order[None, :], step.masters[3]),
        [rows_shape, rows_shape, sds((PAIR, 4 * D), F32)],
    )
    recv = permute(send, CORE)
    tok_keep, tok_send = step.tokens()
    width_a = GATHERED[0].width
    width_b = GATHERED[1].width
    a, b = call(
        merge_body,
        [sds((1, PAIR, width_a), BF16), sds((1, PAIR, width_b + GATHERED[2].width), BF16)],
        scratch=[pltpu.VMEM((PAIR, total_half), F32)],
    )(place, keep, recv, downs)

    a, b, tok_send = tie(a, b, tok_send)
    tok_recv = step.swap(tok_send)
    recv = permute(a, GATHER_STAGES[0])
    recv, b = tie(recv, b)
    a = jnp.concatenate([a, recv])
    recv = permute(a, GATHER_STAGES[1])
    b_recv = permute(b, GATHER_STAGES[0])
    recv, b_recv, tok_recv = tie(recv, b_recv, tok_recv)
    a = jnp.concatenate([a, recv])
    b = jnp.concatenate([b, b_recv])
    a_recv = permute(a, GATHER_STAGES[2])
    b_recv = permute(b, GATHER_STAGES[1])
    x, bias, lens = step.arrange(tok_keep, tok_recv)
    a_recv, b_recv, x = tie(a_recv, b_recv, x)
    a = jnp.concatenate([a, a_recv])
    c = jnp.concatenate([b[:, :, width_b:], b_recv[:, :, width_b:]])
    b = jnp.concatenate([b[:, :, :width_b], b_recv[:, :, :width_b]])
    a_recv = permute(a, GATHER_STAGES[3])
    b_recv = permute(b, GATHER_STAGES[2])
    cot_send = step.cot_send()
    a, a_recv, b_recv, c, cot_send = tie(a, a_recv, b_recv, c, cot_send)
    b = jnp.concatenate([b, b_recv])
    a_sib = (permute(a, CORE), permute(a_recv, CORE))
    b_recv = permute(b, GATHER_STAGES[3])
    c_recv = permute(c, GATHER_STAGES[2])
    cot_recv = step.swap(cot_send)
    qkv0, proj0, up0, down0, small, up_bias = unpack(GATHERED[0], (a, a_recv), a_sib, place)

    small0, small1 = small[0:12], small[12:24]
    n1_0, qkv_0, att_0, prob_0, mid_0, n2_0 = layer_forward_one(x, bias, qkv0, proj0, small0)
    mid_0, n2_0, b_recv, c_recv = tie(mid_0, n2_0, b_recv, c_recv)
    b_sib = (permute(b, CORE), permute(b_recv, CORE))
    c = jnp.concatenate([c, c_recv])
    c, mid_0 = tie(c, mid_0)
    c_recv = permute(c, GATHER_STAGES[3])
    x_1, act_0, slope_0 = layer_forward_two(mid_0, n2_0, up0, down0, small0, up_bias[0:1])
    qkv1, proj1, every_cot, order = unpack(GATHERED[1], (b, b_recv), b_sib, place)
    n1_1, qkv_1, att_1, prob_1, mid_1, n2_1 = layer_forward_one(x_1, bias, qkv1, proj1, small1)
    mid_1, n2_1, c_recv = tie(mid_1, n2_1, c_recv)
    c_sib = (permute(c, CORE), permute(c_recv, CORE))
    up1, down1 = unpack(GATHERED[2], (c, c_recv), c_sib, place)
    final, act_1, slope_1 = layer_forward_two(mid_1, n2_1, up1, down1, small1, up_bias[1:2])
    out_keep, out_send, g, dense_cls = step.turn(final, lens, cot_recv, order, every_cot)

    def mlp_finish(layer):
        def finish(place, matrices, outs):
            arrange_sums(MLP_SUMS[layer], place, matrices, outs[0], outs[1])

        return finish

    def qkv_finish(layer):
        def finish(place, matrices, outs, rows):
            matrices = list(matrices)
            if layer == 0:
                weight, proj, rows_one1, rows_two1, up1, rows_two0, up0 = matrices
                table = outs[2]
                table[...] = jnp.zeros(table.shape, F32)
                table[:, 0:32] = small_table(((rows, rows_two0, up0), (rows_one1, rows_two1, up1)))
                matrices = [weight, proj, table]
            arrange_sums(QKV_SUMS[layer], place, matrices, outs[0], outs[1])

        return finish

    out_swap = Transfer(step.swap, out_send)
    keep, send, g_hid, bias_up1 = beside(
        [out_swap],
        lambda g: mlp_weights(
            place, mlp_finish(1), sum_shapes(MLP_SUMS[1]), g, n2_1, act_1, slope_1, down1
        ),
        g,
    )
    m1 = Reduction(MLP_SUMS[1], keep, send, place)
    g_mid, g_proj, g_att, rows_two1 = beside(
        [m1], lambda g_hid: mlp_rows(g, g_hid, mid_1, att_1, up1, proj1, small1), g_hid
    )
    keep, send, g_nrm, rows_one1 = beside(
        [m1],
        lambda g_att: qkv_weights(
            place, qkv_finish(1), sum_shapes(QKV_SUMS[1]), (g_proj, dense_cls),
            g_att, n1_1, qkv_1, prob_1, x_1, qkv1,
        ),
        g_att,
    )
    q1 = Reduction(QKV_SUMS[1], keep, send, place)
    g = norm_one(g_nrm, x_1, g_mid, small1)

    keep, send, g_hid, bias_up0 = beside(
        [q1, m1],
        lambda g: mlp_weights(
            place, mlp_finish(0), sum_shapes(MLP_SUMS[0]), g, n2_0, act_0, slope_0, down0
        ),
        g,
    )
    m0 = Reduction(MLP_SUMS[0], keep, send, place)
    g_mid, g_proj, g_att, rows_two0 = beside(
        [m0, q1, m1], lambda g_hid: mlp_rows(g, g_hid, mid_0, att_0, up0, proj0, small0), g_hid
    )
    keep, send, _, g_nrm, _ = beside(
        [m0, q1, m1],
        lambda g_att: qkv_weights(
            place, qkv_finish(0), sum_shapes(QKV_SUMS[0]) + [sds((D, SMALL), F32)],
            (g_proj, rows_one1, rows_two1, bias_up1, rows_two0, bias_up0),
            g_att, n1_0, qkv_0, prob_0, x, qkv0,
        ),
        g_att,
    )
    q0 = Reduction(QKV_SUMS[0], keep, send, place)
    back_keep, back_send = beside(
        [q0, m0, q1], lambda g_nrm: step.split(norm_one(g_nrm, x, g_mid, small0)), g_nrm
    )
    back = Transfer(step.swap, back_send)
    block_out = beside(
        [q0, m0, q1], lambda keep, recv: step.join(keep, recv), out_keep, out_swap.recv
    )
    back_keep = beside([q0, m0, m1, back], lambda v: v, back_keep)
    patch_grad = beside([q0, m0, q1], step.scatter, back_keep, back.recv)

    def adam_mlp(fix):
        return sum(
            step.adam_rows(
                fix, [(MLP_SUMS[1], 1), (MLP_SUMS[0], 0)], ["up", "down"], [2, 3],
                [m1.result, m0.result], [],
            )[0],
            [],
        )

    new = beside([q0], adam_mlp, step.fix)
    new_up, new_down = new[:3], new[3:]
    q0.absorb(q0.move())
    (new_qkv, new_proj), (cls_own, small_own) = step.adam_rows(
        step.fix,
        [(QKV_SUMS[1], 1), (QKV_SUMS[0], 0)],
        ["qkv", "proj"],
        [0, 1],
        [q1.result, q0.result],
        [("cls", sds((ROWS, CLS), F32)), ("small", sds((ROWS, SMALL), F32))],
    )
    cls_grouped = cls_own[: step.crop_count].astype(BF16)
    small_flat = jnp.transpose(small_own[:, :24].reshape(ROWS, LAYERS, ROWS), (1, 0, 2))
    new_small = step.adam_flat(4, small_flat.reshape(LAYERS, ROWS * ROWS))
    return outputs(block_out, cls_grouped, patch_grad, (new_qkv, new_proj, new_up, new_down, new_small))


def plain_step(step):
    def gather(values):
        return lax.all_gather(values, AXES, axis=0, tiled=True)

    weights, smalls, up_biases = [], [], []
    for layer in range(LAYERS):
        flat = [gather(m[layer].astype(BF16)) for m in step.masters]
        small = flat[4].reshape(D, 8 + FF // D).astype(F32)
        weights.append(
            (
                flat[0].reshape(D, QKV),
                flat[1].reshape(D, D),
                flat[2].reshape(D, FF),
                flat[3].reshape(FF, D),
            )
        )
        smalls.append(jnp.transpose(small[:, :8]))
        up_biases.append(small[:, 8:].reshape(1, FF))
    keep, send = step.tokens()
    x, bias, lens = step.arrange(keep, step.swap(send))
    saved = []
    for layer in range(LAYERS):
        qkv_w, proj_w, up_w, down_w = weights[layer]
        one = layer_forward_one(x, bias, qkv_w, proj_w, smalls[layer])
        nxt, active, slope = layer_forward_two(
            one[4], one[5], up_w, down_w, smalls[layer], up_biases[layer]
        )
        saved.append((x,) + one + (active, slope))
        x = nxt
    order = gather(step.source_order).astype(F32)[None, :]
    out_keep, out_send, g, dense_cls = step.turn(
        x, lens, step.swap(step.cot_send()), order, gather(step.cot_cls)
    )
    block_out = step.join(out_keep, step.swap(out_send))
    gradients = [None] * LAYERS

    def two_out(place, matrices, outs, *_):
        for value, out in zip(matrices, outs):
            out[...] = value[...]

    for layer in reversed(range(LAYERS)):
        x, normed_one, qkv, attended, prob, mid, normed_two, active, slope = saved[layer]
        qkv_w, proj_w, up_w, down_w = weights[layer]
        g_up, g_down, g_hid, bias_up = mlp_weights(
            step.place, two_out, [sds((D, FF), F32), sds((FF, D), F32)],
            g, normed_two, active, slope, down_w,
        )
        g_mid, g_proj, g_att, two = mlp_rows(g, g_hid, mid, attended, up_w, proj_w, smalls[layer])
        g_qkv_w, g_nrm, one = qkv_weights(
            step.place, two_out, [sds((D, QKV), F32)], (),
            g_att, normed_one, qkv, prob, x, qkv_w,
        )
        g = norm_one(g_nrm, x, g_mid, smalls[layer])
        eight = jnp.concatenate([one[0:4], two[3:4], two[0:3]])
        table = jnp.concatenate([jnp.transpose(eight), bias_up.reshape(D, FF // D)], 1)
        gradients[layer] = (g_qkv_w, g_proj, g_up, g_down, table)
    back_keep, back_send = step.split(g)
    patch_grad = step.scatter(back_keep, step.swap(back_send))

    def scatter_sum(values):
        return lax.psum_scatter(values, AXES, scatter_dimension=0, tiled=True)

    results = []
    for kind in range(5):
        shares = [
            scatter_sum(gradients[layer][kind].reshape(-1).astype(F32)) for layer in range(LAYERS)
        ]
        results.append(step.adam_flat(kind, jnp.stack(shares)))
    cls_grouped = scatter_sum(dense_cls).astype(BF16)
    return outputs(block_out, cls_grouped, patch_grad, results)


def on_device(crop_devices, dp_devices, *arguments):
    step = Step(crop_devices, dp_devices, arguments)
    owned = step.masters[0].shape[1]
    staged = crop_devices * dp_devices == 2 * CHIPS and owned == ROWS * QKV
    if staged and step.crop_count <= ROWS:
        return staged_step(step)
    return plain_step(step)


def solution(mesh):
    crops = [P(AXES, None, None), P(AXES, None), P(AXES), P(AXES), P(AXES, None, None)]
    flat = P(None, AXES)
    return jax.shard_map(
        functools.partial(on_device, mesh.shape["crop"], mesh.shape["dp"]),
        mesh=mesh,
        in_specs=tuple(crops + [P(AXES, None), P()] + [flat] * 15),
        out_specs=(crops[0], crops[1], crops[0]) + (flat,) * 15,
        check_vma=False,
    )
```

```python
import functools

import jax
import jax.numpy as jnp
from jax import lax
from jax.experimental import pallas as pl
from jax.experimental.pallas import tpu as pltpu
from jax.sharding import PartitionSpec as P

D = 384
HEADS = 6
HEAD_DIM = 64
FF = 1536
LAYERS = 2
SLOTS = 144
FOCAL_SLOTS = 32
LEN_ROW = 143

eps_norm = 1e-06
neg_big = -1e30
adam_eps = 1e-08
rate_matrix = 0.04
decay_matrix = 0.05
rate_small = 0.4

F32 = jnp.float32
BF16 = jnp.bfloat16
VM = pl.BlockSpec(memory_space=pltpu.VMEM)
SM = pl.BlockSpec(memory_space=pltpu.SMEM)
AXES = ("crop", "dp")
VMEM_LIMIT = 12 * 1024 * 1024
NO_COST = pl.CostEstimate(flops=1, bytes_accessed=1, transcendentals=0)


def sds(shape, dtype):
    return jax.ShapeDtypeStruct(shape, dtype)


def call(body, out_shape, scratch=(), smem=1):
    def run(*operands):
        return pl.pallas_call(
            body,
            out_shape=out_shape,
            in_specs=[SM] * smem + [VM] * (len(operands) - smem),
            out_specs=jax.tree.map(lambda _: VM, out_shape),
            scratch_shapes=list(scratch),
            compiler_params=pltpu.CompilerParams(vmem_limit_bytes=VMEM_LIMIT),
            cost_estimate=NO_COST,
        )(*operands)

    return run


def iota(shape, axis):
    return lax.broadcasted_iota(jnp.int32, shape, axis)


def dot(a, b, ca, cb):
    return lax.dot_general(a, b, (((ca,), (cb,)), ((), ())), preferred_element_type=F32)


def slot_onehot(slots, c, patch_count):
    row = slots[pl.ds(c, 1), :]
    return row, (iota((patch_count, SLOTS), 0) == row).astype(F32).astype(BF16)


def tokens_body(half, patch_count, place, patches, slots, keep, send):
    y = place[1]
    row_index = iota((SLOTS, D), 0)
    for i in range(half):
        for out, c in ((keep, half * y + i), (send, half * (1 - y) + i)):
            row, onehot = slot_onehot(slots, c, patch_count)
            count = jnp.sum((row >= 0).astype(F32), axis=1, keepdims=True) - 1.0
            picked = dot(onehot, patches[c], 0, 0)
            out[i] = jnp.where(row_index == LEN_ROW, count, picked).astype(BF16)


class Halves:
    def __init__(self, first, second):
        self.parts, self.count = (first, second), first.shape[0]

    def __getitem__(self, key):
        i = key[0] if isinstance(key, tuple) else key
        rest = key[1:] if isinstance(key, tuple) else ()
        return self.parts[i // self.count][(i % self.count,) + tuple(rest)]


def arrange_body(half, place, keep, recv, x_ref, bias_ref, lens_ref):
    y = place[1]
    base = half * SLOTS
    used = half * FOCAL_SLOTS

    def run(v_src, f_src):
        k = iota((SLOTS, SLOTS), 0)
        q = iota((SLOTS, SLOTS), 1)
        row_index = iota((SLOTS, D), 0)
        for i in range(half):
            t = v_src[i].astype(F32)
            n = t[LEN_ROW : LEN_ROW + 1, 0:1]
            x_ref[SLOTS * i : SLOTS * (i + 1), :] = jnp.where(row_index == LEN_ROW, 0.0, t)
            bias_ref[i] = jnp.where(k.astype(F32) <= n, 0.0, neg_big)
            lens_ref[i : i + 1, :] = jnp.broadcast_to(n, (1, 128))
        limit = jnp.full((SLOTS, SLOTS), 1000.0, F32)
        for i in range(half):
            x_ref[base + FOCAL_SLOTS * i : base + FOCAL_SLOTS * (i + 1), :] = f_src[
                i, 0:FOCAL_SLOTS
            ].astype(F32)
            n = f_src[i, SLOTS - 16 : SLOTS].astype(F32)[15:16, 0:1]
            limit = jnp.where((k // FOCAL_SLOTS) == i, n, limit)
            lens_ref[half + i : half + i + 1, :] = jnp.broadcast_to(n, (1, 128))
        if used < SLOTS:
            x_ref[base + used : base + SLOTS, :] = jnp.zeros((SLOTS - used, D), F32)
        same = (q // FOCAL_SLOTS) == (k // FOCAL_SLOTS)
        inside = (k % FOCAL_SLOTS).astype(F32) <= limit
        bias_ref[half] = jnp.where(same & inside, 0.0, neg_big)

    @pl.when(y == 0)
    def _():
        run(keep, recv)

    @pl.when(y == 1)
    def _():
        run(recv, keep)


def turn_body(half, first_ids, place, x_ref, lens, cot, recv_a, recv_b, order, every_cot, *outs):
    keep, send, g_ref, dense = outs
    recv = Halves(recv_a, recv_b)
    y = place[1]
    base = half * SLOTS
    used = half * FOCAL_SLOTS
    views, focals = first_ids(place)
    index = iota((2 * half, 1), 0)
    ids = jnp.where(index < half, views + index, focals + index - half).astype(F32)
    chosen = (order[...] == ids).astype(F32).astype(BF16)
    top = dot(chosen, every_cot[...], 1, 0)

    def piece(values, n, row, rows):
        at = iota((rows, D), 0)
        masked = jnp.where(at.astype(F32) <= n, values, 0.0)
        return masked + jnp.where(at == 0, row, 0.0)

    def run(v_out, f_out, v_get, f_get):
        cls = []
        for i in range(half):
            n = lens[i : i + 1, 0:1]
            rows = slice(SLOTS * i, SLOTS * (i + 1))
            v = x_ref[rows, :]
            cls.append(v[0:1])
            v_out[i] = jnp.where(iota((SLOTS, D), 0).astype(F32) <= n, v, 0.0).astype(BF16)
            g_ref[rows, :] = piece(v_get(i).astype(F32), n, top[i : i + 1], SLOTS)
        for i in range(half):
            n = lens[half + i : half + i + 1, 0:1]
            rows = slice(base + FOCAL_SLOTS * i, base + FOCAL_SLOTS * (i + 1))
            f = x_ref[rows, :]
            cls.append(f[0:1])
            f = jnp.where(iota((FOCAL_SLOTS, D), 0).astype(F32) <= n, f, 0.0)
            f_out[i, 0:FOCAL_SLOTS] = f.astype(BF16)
            f_out[i, FOCAL_SLOTS:SLOTS] = jnp.zeros((SLOTS - FOCAL_SLOTS, D), BF16)
            g_ref[rows, :] = piece(
                f_get(i)[0:FOCAL_SLOTS].astype(F32), n, top[half + i : half + i + 1], FOCAL_SLOTS
            )
        if used < SLOTS:
            g_ref[base + used : base + SLOTS, :] = jnp.zeros((SLOTS - used, D), F32)
        dense[...] = dot(chosen, jnp.concatenate(cls, 0).astype(BF16), 0, 0)

    @pl.when(y == 0)
    def _():
        run(keep, send, lambda i: cot[i], lambda i: recv[i])

    @pl.when(y == 1)
    def _():
        run(send, keep, lambda i: recv[i], lambda i: cot[half + i])


def split_body(half, place, x_ref, keep, send):
    y = place[1]
    base = half * SLOTS

    def run(v_out, f_out):
        for i in range(half):
            v_out[i] = x_ref[SLOTS * i : SLOTS * (i + 1), :].astype(BF16)
            rows = slice(base + FOCAL_SLOTS * i, base + FOCAL_SLOTS * (i + 1))
            f_out[i, 0:FOCAL_SLOTS] = x_ref[rows, :].astype(BF16)
            f_out[i, FOCAL_SLOTS:SLOTS] = jnp.zeros((SLOTS - FOCAL_SLOTS, D), BF16)

    @pl.when(y == 0)
    def _():
        run(keep, send)

    @pl.when(y == 1)
    def _():
        run(send, keep)


def join_body(half, place, keep, recv, out):
    y = place[1]
    for i in range(half):
        out[half * y + i] = keep[i]
        out[half * (1 - y) + i] = recv[i]


def scatter_body(half, patch_count, place, keep, recv, slots, out):
    y = place[1]
    for i in range(half):
        for src, c in ((keep, half * y + i), (recv, half * (1 - y) + i)):
            _, onehot = slot_onehot(slots, c, patch_count)
            out[c] = dot(onehot, src[i], 1, 0)


def lane_mask(second, value):
    lane = iota((1, 128), 1)
    chosen = (lane >= HEAD_DIM) if second else (lane < HEAD_DIM)
    return jnp.where(chosen, value, 0.0).astype(BF16)


def attend_forward_block(qkv_ref, bias, att_ref, prob_ref, rows, b):
    for pair in range(HEADS // 2):
        at = 128 * pair
        q = qkv_ref[rows, at : at + 128]
        k = qkv_ref[rows, D + at : D + at + 128]
        v = qkv_ref[rows, 2 * D + at : 2 * D + at + 128]
        joined = None
        for h in range(2):
            s = dot(k * lane_mask(h, HEAD_DIM**-0.5), q, 1, 1) + bias
            e = jnp.exp(s - jnp.max(s, 0, keepdims=True))
            p = (e * (1.0 / jnp.sum(e, 0, keepdims=True))).astype(BF16)
            prob_ref[b, 2 * pair + h] = p
            o = dot(p, v * lane_mask(h, 1.0), 0, 0)
            joined = o if joined is None else joined + o
        att_ref[rows, at : at + 128] = joined.astype(BF16)


def attend_backward_block(qkv_ref, prob_ref, grad_ref, out_ref, rows, b):
    for pair in range(HEADS // 2):
        at = 128 * pair
        q = qkv_ref[rows, at : at + 128]
        k = qkv_ref[rows, D + at : D + at + 128]
        v = qkv_ref[rows, 2 * D + at : 2 * D + at + 128]
        g = grad_ref[rows, at : at + 128]
        dq = dk = dv = None
        for h in range(2):
            pb = prob_ref[b, 2 * pair + h]
            p = pb.astype(F32)
            gh = g * lane_mask(h, 1.0)
            scaled = lane_mask(h, HEAD_DIM**-0.5)
            t = p * dot(v, gh, 1, 1)
            ds = (t - p * jnp.sum(t, 0, keepdims=True)).astype(BF16)
            parts = (dot(ds, k * scaled, 0, 0), dot(ds, q * scaled, 1, 0), dot(pb, gh, 1, 0))
            if dq is None:
                dq, dk, dv = parts
            else:
                dq, dk, dv = dq + parts[0], dk + parts[1], dv + parts[2]
        out_ref[rows, at : at + 128] = dq.astype(BF16)
        out_ref[rows, D + at : D + at + 128] = dk.astype(BF16)
        out_ref[rows, 2 * D + at : 2 * D + at + 128] = dv.astype(BF16)


def total(values):
    return jnp.sum(values, 0, keepdims=True)


def normalized(values):
    centered = values - jnp.mean(values, -1, keepdims=True)
    scale = lax.rsqrt(jnp.mean(centered * centered, -1, keepdims=True) + eps_norm)
    return centered * scale, scale


def gelu_parts(v):
    c = 0.7978845608028654
    a = 0.044715
    square = v * v
    t = jnp.tanh(v * (c + (c * a) * square))
    h = 0.5 * v
    ht = h * t
    return h + ht, 0.5 * (1.0 + t) + (h - ht * t) * (c + (3.0 * a * c) * square)


def attention_body(x, bias, qkv_w, proj_w, small, *outs):
    unit_one, scale_one, unit_two, scale_two, normed_one, qkv, attended, prob, mid, normed_two = outs
    count = x.shape[0] // SLOTS

    def norm(values, r, unit_ref, scale_ref, normed_ref, first):
        unit, scale = normalized(values)
        unit_ref[r, :] = unit.astype(BF16)
        scale_ref[r, :] = scale
        normed_ref[r, :] = (unit * small[first : first + 1] + small[first + 1 : first + 2]).astype(
            BF16
        )

    over_blocks(count, lambda r, b: norm(x[r, :], r, unit_one, scale_one, normed_one, 0))
    for c in range(3):
        w = slice(c * D, (c + 1) * D)
        part = dot(normed_one[...], qkv_w[:, w], 1, 0)
        if c != 1:
            part = part + small[2 + c // 2 : 3 + c // 2]
        qkv[:, w] = part.astype(BF16)
    over_blocks(count, lambda r, b: attend_forward_block(qkv, bias[b], attended, prob, r, b))
    mid[...] = dot(attended[...], proj_w[...], 1, 0)

    def second(r, _):
        whole = x[r, :] + mid[r, :] + small[4:5]
        mid[r, :] = whole
        norm(whole, r, unit_two, scale_two, normed_two, 5)

    over_blocks(count, second)


def layer_forward_one(x, bias, qkv_w, proj_w, small):
    rows = x.shape[0]
    row = sds((rows, D), BF16)
    scale = sds((rows, 1), F32)
    out = call(
        attention_body,
        [
            row, scale, row, scale, row, sds((rows, 3 * D), BF16), row,
            sds((rows // SLOTS, HEADS, SLOTS, SLOTS), BF16), sds((rows, D), F32), row,
        ],
        smem=0,
    )(x, bias, qkv_w, proj_w, small)
    return (tuple(out[:4]),) + tuple(out[4:])


def feed_forward_body(mid, normed, up_w, down_w, small, up_bias, out, active, slope):
    for c in range(FF // 256):
        w = slice(c * 256, (c + 1) * 256)
        value, derivative = gelu_parts(dot(normed[...], up_w[:, w], 1, 0) + up_bias[:, w])
        active[:, w] = value.astype(BF16)
        slope[:, w] = derivative.astype(BF16)
    out[...] = dot(active[...], down_w[...], 1, 0) + mid[...] + small[7:8]


def layer_forward_two(mid, normed_two, up_w, down_w, small, up_bias):
    rows = mid.shape[0]
    return call(
        feed_forward_body,
        [sds((rows, D), F32), sds((rows, FF), BF16), sds((rows, FF), BF16)],
        smem=0,
    )(mid, normed_two, up_w, down_w, small, up_bias)


def over_blocks(count, step):
    def body(b, _):
        step(pl.ds(pl.multiple_of(b * SLOTS, 16), SLOTS), b)
        return 0

    lax.fori_loop(0, count, body, 0)


def norm_back(grad, unit, scale, gain):
    inner = grad * gain
    mean, along = jnp.mean(inner, -1, keepdims=True), jnp.mean(inner * unit, -1, keepdims=True)
    return scale * (inner - mean - unit * along)


def mlp_weights_body(finish, place, g, normed, active, slope, down_w, *refs):
    outs, (branch, up, down) = refs[:-3], refs[-3:]
    g_hidden, bias_up = outs[-2:]
    branch[...] = g[...].astype(BF16)
    for c in range(FF // D):
        w = slice(c * D, (c + 1) * D)
        t = (dot(branch[...], down_w[w, :], 1, 1) * slope[:, w].astype(F32)).astype(BF16)
        g_hidden[:, w] = t
        bias_up[:, w] = total(t.astype(F32))
    for c in range(FF // D):
        w = slice(c * D, (c + 1) * D)
        down[w, :] = dot(active[:, w], branch[...], 0, 0)
    up[...] = dot(normed[...], g_hidden[...], 0, 0)
    finish(place, (up, down), outs[:-2])


def mlp_rows_body(g, g_hidden, unit, scale, attended, up_w, proj_w, small, g_mid, g_proj, g_att, rows, work):
    rows[...] = jnp.zeros(rows.shape, F32)
    g_mid[...] = dot(g_hidden[...], up_w[...], 1, 1)

    def step(r, _):
        grad = g_mid[r, :]
        along = unit[r, :].astype(F32)
        whole = norm_back(grad, along, scale[r, :], small[5:6]) + g[r, :]
        g_mid[r, :] = whole
        rounded = whole.astype(BF16)
        work[r, :] = rounded
        rows[0:1] += total(grad * along)
        rows[1:2] += total(grad)
        rows[2:3] += total(g[r, :].astype(BF16).astype(F32))
        rows[3:4] += total(rounded.astype(F32))

    over_blocks(g.shape[0] // SLOTS, step)
    g_att[...] = dot(work[...], proj_w[...], 1, 1).astype(BF16)
    g_proj[...] = dot(attended[...], work[...], 0, 0)


def qkv_weights_body(finish, extra_count, place, g_att, normed, qkv, prob, unit, qkv_w, *refs):
    extra, outs, (g_qkv, weight) = refs[:extra_count], refs[extra_count:-2], refs[-2:]
    g_normed, rows = outs[-2:]
    rows[...] = jnp.zeros(rows.shape, F32)
    count = unit.shape[0] // SLOTS
    over_blocks(count, lambda r, b: attend_backward_block(qkv, prob, g_att, g_qkv, r, b))
    g_normed[...] = dot(g_qkv[...], qkv_w[...], 1, 1)

    def step(r, _):
        grad = g_normed[r, :]
        rows[0:1] += total(grad * unit[r, :].astype(F32))
        rows[1:2] += total(grad)
        rows[2:3] += total(g_qkv[r, 0:D].astype(F32))
        rows[3:4] += total(g_qkv[r, 2 * D : 3 * D].astype(F32))

    over_blocks(count, step)
    weight[...] = dot(normed[...], g_qkv[...], 0, 0)
    finish(place, (weight,) + extra, outs[:-2], rows)


def norm_one_body(g_normed, unit, scale, g_mid, small, out):
    def step(r, _):
        back = norm_back(g_normed[r, :], unit[r, :].astype(F32), scale[r, :], small[0:1])
        out[r, :] = back + g_mid[r, :]

    over_blocks(unit.shape[0] // SLOTS, step)


def mlp_weights(place, finish, shapes, g, normed, active, slope, down_w):
    rows = g.shape[0]
    return call(
        functools.partial(mlp_weights_body, finish),
        list(shapes) + [sds((rows, FF), BF16), sds((1, FF), F32)],
        scratch=[
            pltpu.VMEM((rows, D), BF16),
            pltpu.VMEM((D, FF), F32),
            pltpu.VMEM((FF, D), F32),
        ],
    )(place, g, normed, active, slope, down_w)


def mlp_rows(g, g_hidden, unit, scale, attended, up_w, proj_w, small):
    rows = g.shape[0]
    return call(
        mlp_rows_body,
        [sds((rows, D), F32), sds((D, D), F32), sds((rows, D), BF16), sds((8, D), F32)],
        scratch=[pltpu.VMEM((rows, D), BF16)],
        smem=0,
    )(g, g_hidden, unit, scale, attended, up_w, proj_w, small)


def qkv_weights(place, finish, shapes, extra, g_att, normed, qkv, prob, unit, qkv_w):
    rows = unit.shape[0]
    return call(
        functools.partial(qkv_weights_body, finish, len(extra)),
        list(shapes) + [sds((rows, D), F32), sds((8, D), F32)],
        scratch=[pltpu.VMEM((rows, 3 * D), BF16), pltpu.VMEM((D, 3 * D), F32)],
    )(place, g_att, normed, qkv, prob, unit, qkv_w, *extra)


def norm_one(g_normed, unit, scale, g_mid, small):
    return call(norm_one_body, sds(g_mid.shape, F32), smem=0)(g_normed, unit, scale, g_mid, small)


def small_table(groups):
    flat, wide = [], []
    lane = iota((1, FF), 1) % 4
    for rows_one, rows_two, bias_up in groups:
        flat += [rows_one[0:4, :], rows_two[3:4, :], rows_two[0:3, :], jnp.zeros((4, D), F32)]
        wide += [jnp.zeros((8, FF), F32)]
        wide += [jnp.where(lane == k, bias_up[...], 0.0) for k in range(4)]
    flat = jnp.concatenate(flat + [jnp.zeros((8, D), F32)], 0).astype(BF16)
    wide = jnp.concatenate(wide + [jnp.zeros((8, FF), F32)], 0).astype(BF16)
    same = (iota((D, D), 0) == iota((D, D), 1)).astype(F32).astype(BF16)
    spread = (iota((D, FF), 1) // 4 == iota((D, FF), 0)).astype(F32).astype(BF16)
    return dot(same, flat, 1, 1) + dot(spread, wide, 1, 1)


ROWS = 12
PAIR = 24
CHIPS = 16
QKV, PROJ, UP, SMALL, CLS, ORDER, PAD = 3 * D, D, FF, 128, D, 128, 128
CORE = (1, 1)
TABLES = ("small", "order")
GATHER_STAGES = ((4, 8), (8, 4), (2, 16), (16, 2))


class Chunk:
    def __init__(self, names, widths, down):
        self.names, self.widths, self.down = names, widths, down
        self.half = sum(widths) // 2
        self.width = self.half + (2 * D if down is not None else 0)
        self.arrays = [n for n in names if n != "pad"] + (["down"] if down is not None else [])

    def pieces(self, which):
        low, high, start, found = which * self.half, (which + 1) * self.half, 0, []
        for name, width in zip(self.names, self.widths):
            a, b = max(start, low), min(start + width, high)
            if a < b:
                found.append((name, a - start, a - low, b - a))
            start += width
        return found


GATHERED = (
    Chunk(("qkv0", "proj0", "up0", "small", "pad"), (QKV, PROJ, UP, SMALL, PAD), 0),
    Chunk(("qkv1", "proj1", "cls", "order"), (QKV, PROJ, CLS, ORDER), None),
    Chunk(("up1",), (UP,), 1),
)
MLP_SUMS = (Chunk(("up0",), (UP,), 0), Chunk(("up1",), (UP,), 1))
QKV_SUMS = (
    Chunk(("qkv0", "proj0", "small", "pad"), (QKV, PROJ, SMALL, PAD), None),
    Chunk(("qkv1", "proj1", "cls", "pad"), (QKV, PROJ, CLS, PAD), None),
)
FLAT = {"qkv": QKV, "proj": PROJ, "up": UP}


def by_core(place, run):
    for b in range(2):

        @pl.when((place[0] & 1) == b)
        def _(b=b):
            run(b)


def chip_of(place, core, bits):
    mask = 0
    for bit, stage in zip(bits, GATHER_STAGES):
        mask ^= stage[core] * bit
    return (place[0] ^ mask) >> 1


def bits_of(index, count=4):
    return [(index >> k) & 1 for k in range(count)]


def tie(*values):
    return lax.optimization_barrier(values)


def small_block(flat, layer):
    row = flat[layer : layer + 1, :].astype(BF16).astype(F32)
    width = ROWS * ROWS
    spread = jnp.where(iota((16, width), 1) // ROWS == iota((16, width), 0), row, 0.0).astype(BF16)
    at = iota((width, 128), 0) % ROWS + ROWS * layer
    chosen = (at == iota((width, 128), 1)).astype(F32).astype(BF16)
    return dot(spread, chosen, 1, 0)[0:ROWS]


def order_block(ref):
    count = ref.shape[1]
    row = ref[...].astype(F32)
    mine = iota((16, count), 0) == iota((16, count), 1)
    number = jnp.sum(jnp.where(mine, row, 0.0), 1, keepdims=True)
    number = jnp.where(iota((16, 1), 0) < count, number, -129.0)
    high = jnp.floor(number * (1.0 / 128.0))
    lane = iota((16, 128), 1)
    return jnp.where(lane == 0, high, number - 128.0 * high)[0:ROWS]


def pack_body(place, *refs):
    held, (keep, send, down_out), local, sem = refs[0:7], refs[7:10], refs[10:17], refs[17]
    copies = [
        pltpu.make_async_copy(src, dst, sem.at[i]) for i, (src, dst) in enumerate(zip(held, local))
    ]
    for copy in copies:
        copy.start()
    for copy in copies:
        copy.wait()
    source = dict(zip(("qkv", "proj", "up", "small", "cls", "order"), local))
    down = local[6]

    def run(b):
        base = 0
        for chunk in GATHERED:
            for out, which in ((keep, b), (send, 1 - b)):
                for name, column, at, width in chunk.pieces(which):
                    span = slice(base + at, base + at + width)
                    if name == "pad":
                        out[:, span] = jnp.zeros((ROWS, width), F32)
                    elif name == "small":
                        out[:, span] = small_block(source["small"], 0) + small_block(
                            source["small"], 1
                        )
                    elif name == "order":
                        out[:, span] = order_block(source["order"])
                    elif name == "cls":
                        count = source["cls"].shape[0]
                        out[:, span] = jnp.zeros((ROWS, width), F32)
                        out[0:count, span] = source["cls"][:, column : column + width].astype(F32)
                    else:
                        flat, full = source[name[:-1]], FLAT[name[:-1]]
                        for r in range(ROWS):
                            first = r * full + column
                            layer = int(name[-1])
                            out[r : r + 1, span] = flat[layer : layer + 1, first : first + width]
            base += chunk.half

    by_core(place, run)
    for layer in range(LAYERS):
        for r in range(2 * PAIR):
            first = (2 * layer + r // PAIR) * D
            down_out[r % PAIR : r % PAIR + 1, first : first + D] = down[
                layer : layer + 1, r * D : (r + 1) * D
            ]


def merge_body(place, keep, recv, down, *rest):
    outs, work = rest[:2], rest[2]

    def run(b):
        work[ROWS * b : ROWS * (b + 1), :] = keep[...]
        work[ROWS * (1 - b) : ROWS * (2 - b), :] = recv[...]

    by_core(place, run)
    source = target = 0
    for number, chunk in enumerate(GATHERED):
        out = outs[min(number, 1)]
        if number <= 1:
            target = 0
        out[0, :, target : target + chunk.half] = work[:, source : source + chunk.half].astype(BF16)
        if chunk.down is not None:
            at, first = target + chunk.half, 2 * D * chunk.down
            out[0, :, at : at + 2 * D] = down[:, first : first + 2 * D].astype(BF16)
        source, target = source + chunk.half, target + chunk.width


def unpack_body(chunk, base, pieces, place, *refs):
    own, sib, outs = refs[:pieces], refs[pieces : 2 * pieces], refs[2 * pieces :]
    low = 3 if pieces == 2 else 2
    target = dict(zip([n for n in chunk.arrays if n not in TABLES], outs))
    if "small" in chunk.names:
        rows_out, up_out, target["small"] = outs[-3:]
    if "order" in chunk.names:
        order_out, target["order"] = outs[-2:]

    def run(b):
        for which in range(2):
            source = own if which == b else sib
            for received in range(pieces):
                block = source[received]

                def step(index, _, which=which, received=received, block=block):
                    chip = chip_of(place, which, bits_of(index, low) + bits_of(received, 4 - low))
                    for name, column, at, width in chunk.pieces(which):
                        if name == "pad":
                            continue
                        values = block[index, :, base + at : base + at + width]
                        if name in TABLES:
                            values = values.astype(F32)
                        target[name][chip, :, column : column + width] = values
                    for part in range(0 if chunk.down is None else 2):
                        first = base + chunk.half + part * D
                        target["down"][chip * 4 + 2 * which + part] = block[
                            index, :, first : first + D
                        ]
                    return 0

                lax.fori_loop(0, CHIPS // pieces, step, 0)

    by_core(place, run)
    if "order" in chunk.names:
        across = jnp.transpose(target["order"][...].reshape(D, ORDER))
        order_out[...] = across[0:1] * 128.0 + across[1:2]
    if "small" in chunk.names:
        across = jnp.transpose(target["small"][...].reshape(D, SMALL))
        rows_out[...] = across[0:24]
        ups = jnp.concatenate([across[8:12], across[20:24]], 0).astype(BF16)
        spread = (iota((D, FF), 1) // 4 == iota((D, FF), 0)).astype(F32).astype(BF16)
        wide = dot(ups, spread, 1, 0)
        lane = iota((1, FF), 1) % 4
        for layer in range(LAYERS):
            row = jnp.zeros((1, FF), F32)
            for k in range(4):
                row = jnp.where(lane == k, wide[4 * layer + k : 4 * layer + k + 1], row)
            up_out[layer : layer + 1, :] = row


def permute(x, masks):
    return lax.ppermute(x, AXES, [(i, i ^ masks[i & 1]) for i in range(2 * CHIPS)])


def unpack(chunk, base, pieces, sib, place):
    shapes = [
        sds((CHIPS, PAIR, width), BF16)
        for name, width in zip(chunk.names, chunk.widths)
        if name != "pad" and name not in TABLES
    ]
    if chunk.down is not None:
        shapes.append(sds((4 * CHIPS, PAIR, D), BF16))
    count, scratch = len(shapes), []
    if "small" in chunk.names:
        shapes += [sds((24, D), F32), sds((LAYERS, FF), F32)]
        scratch = [pltpu.VMEM((CHIPS, PAIR, SMALL), F32)]
    if "order" in chunk.names:
        shapes += [sds((1, D), F32)]
        scratch = [pltpu.VMEM((CHIPS, PAIR, ORDER), F32)]
    out = call(functools.partial(unpack_body, chunk, base, len(pieces)), shapes, scratch=scratch)(
        place, *pieces, *sib
    )
    return [b.reshape(-1, b.shape[2]) for b in out[:count]] + list(out[count:])


def arrange_sums(chunk, place, matrices, keep, send):
    source = dict(zip(chunk.arrays, matrices))

    def run(b):
        for out, which in ((keep, b), (send, 1 - b)):

            def step(index, _, out=out, which=which):
                chip = chip_of(place, which, bits_of(index))
                rows = pl.ds(pl.multiple_of(chip * PAIR, 8), PAIR)
                for name, column, at, width in chunk.pieces(which):
                    if name == "pad":
                        out[index, :, at : at + width] = jnp.zeros((PAIR, width), BF16)
                    else:
                        out[index, :, at : at + width] = source[name][
                            rows, column : column + width
                        ].astype(BF16)
                for part in range(0 if chunk.down is None else 2):
                    at = chunk.half + part * D
                    first = pl.multiple_of((chip * 4 + 2 * which + part) * PAIR, 8)
                    out[index, :, at : at + D] = source["down"][pl.ds(first, PAIR), :].astype(BF16)
                return 0

            lax.fori_loop(0, CHIPS, step, 0)

    by_core(place, run)


def sum_shapes(chunk):
    return [sds((CHIPS, PAIR, chunk.width), BF16)] * 2


def split_rows_body(chunk, place, own, recv, keep, send, *down_out):
    def run(b):
        whole = own[...] + recv[...].astype(F32)
        for out, core in ((keep, b), (send, 1 - b)):
            out[...] = whole[ROWS * core : ROWS * (core + 1), : chunk.half]
        if chunk.down is not None:
            down_out[0][...] = whole[:, chunk.half :]

    by_core(place, run)


class Reduction:
    def __init__(self, chunk, keep, send, place):
        self.chunk, self.place, self.stage = chunk, place, 0
        self.keep, self.send = keep, send
        self.masks = (CORE,) + GATHER_STAGES[::-1] + (CORE,)

    def move(self):
        self.stage += 1
        return permute(self.send, self.masks[self.stage - 1])

    def absorb(self, recv):
        if self.stage <= 4:
            middle = recv.shape[0] // 2
            low = self.keep[:middle].astype(F32) + recv[:middle].astype(F32)
            high = self.keep[middle:].astype(F32) + recv[middle:].astype(F32)
            self.keep, self.send = low, high.astype(BF16)
        elif self.stage == 5:
            chunk = self.chunk
            shapes = [sds((ROWS, chunk.half), F32)] * 2
            if chunk.down is not None:
                shapes.append(sds((PAIR, 2 * D), F32))
            self.keep, self.send, *self.rest = call(
                functools.partial(split_rows_body, chunk), shapes
            )(self.place, self.keep[0], recv[0])
        else:
            self.result = (self.keep, recv) + tuple(self.rest)


class Transfer:
    def __init__(self, swap, send):
        self.swap, self.send = swap, send

    def move(self):
        return self.swap(self.send)

    def absorb(self, recv):
        self.recv = recv


def beside(moving, run, *inputs):
    count = len(moving)
    tied = tie(*[m.send for m in moving], *inputs)
    for m, send in zip(moving, tied):
        m.send = send
    received = [m.move() for m in moving]
    out = run(*tied[count:])
    many = isinstance(out, (tuple, list))
    tied = tie(*received, *(out if many else (out,)))
    for m, recv in zip(moving, tied):
        m.absorb(recv)
    return tied[count:] if many else tied[count]


def adam_math(fix, master, first, second, grad, rate, decay):
    moment = 0.5 * first + 0.5 * grad
    square = 0.5 * second + 0.5 * grad * grad
    update = moment / fix / (jnp.sqrt(square / fix) + adam_eps) + decay * master
    return master - rate * update, moment, square


def adam_body(plan, place, fix_ref, *refs):
    chunks, names, extras = plan
    grads, at = [], 0
    for chunk in chunks:
        size = 2 if chunk.down is None else 3
        grads.append(refs[at : at + size])
        at += size
    flats = refs[at : at + 3 * len(names)]
    outs = refs[at + 3 * len(names) : at + 6 * len(names)]
    rest = refs[at + 6 * len(names) :]
    extra = dict(zip(extras, rest))
    work = dict(zip(names, rest[len(extras) :]))

    def run(b):
        for chunk, parts in zip(chunks, grads):
            sides = (parts[0], parts[1]) if b == 0 else (parts[1], parts[0])
            for which in range(2):
                for name, column, first, width in chunk.pieces(which):
                    span = slice(first, first + width)
                    if name in extra:
                        out = extra[name]
                        out[:, column : column + width] = sides[which][
                            0 : out.shape[0], span
                        ].astype(out.dtype)
                    elif name[:-1] in work:
                        full, layer = FLAT[name[:-1]], int(name[-1])
                        for r in range(ROWS):
                            to = r * full + column
                            work[name[:-1]][layer : layer + 1, to : to + width] = sides[which][
                                r : r + 1, span
                            ]
            if chunk.down is not None and "down" in work:
                layer = chunk.down
                for r in range(2 * PAIR):
                    first = (r // PAIR) * D
                    work["down"][layer : layer + 1, r * D : (r + 1) * D] = parts[2][
                        r % PAIR : r % PAIR + 1, first : first + D
                    ]

    by_core(place, run)
    for i, name in enumerate(names):
        new = adam_math(
            fix_ref[0],
            flats[3 * i][...],
            flats[3 * i + 1][...],
            flats[3 * i + 2][...],
            work[name][...],
            rate_matrix,
            decay_matrix,
        )
        for k in range(3):
            outs[3 * i + k][...] = new[k]


class Step:
    def __init__(self, crop_devices, dp_devices, arguments):
        (
            self.patches,
            self.kept_index,
            self.lengths,
            self.source_order,
            self.cot_tokens,
            self.cot_cls,
            step_count,
        ) = arguments[:7]
        self.masters, self.firsts, self.seconds = arguments[7:12], arguments[12:17], arguments[17:22]
        self.crop_count, self.patch_count = self.patches.shape[:2]
        self.half = self.crop_count // 2
        self.dp_devices = dp_devices
        me = lax.axis_index(AXES)
        self.place = jnp.stack([me, me // dp_devices]).astype(jnp.int32)
        self.swap = functools.partial(lax.ppermute, axis_name="crop", perm=[(0, 1), (1, 0)])
        self.crops_half = sds((self.half, SLOTS, D), BF16)
        self.rows = (self.half + 1) * SLOTS
        self.fix = (1.0 - jnp.power(0.5, step_count[0].astype(F32))).reshape(1)

    def tokens(self):
        positions = jnp.arange(SLOTS, dtype=jnp.int32)[None, :]
        slots = jnp.pad(self.kept_index + 1, ((0, 0), (1, SLOTS - self.kept_index.shape[1] - 1)))
        self.slots = jnp.where(positions <= self.lengths[:, None], slots, -1)
        return call(
            functools.partial(tokens_body, self.half, self.patch_count),
            [self.crops_half] * 2,
        )(self.place, self.patches, self.slots)

    def arrange(self, keep, recv):
        return call(
            functools.partial(arrange_body, self.half),
            [
                sds((self.rows, D), F32),
                sds((self.half + 1, SLOTS, SLOTS), F32),
                sds((2 * self.half, 128), F32),
            ],
        )(self.place, keep, recv)

    def first_ids(self, place):
        views = self.crop_count * (place[0] - place[1] * self.dp_devices) + self.half * place[1]
        return views, views + self.crop_count * self.dp_devices

    def cot_send(self):
        start, count = self.half * (1 - self.place[1]), self.half // 2
        return [
            lax.dynamic_slice_in_dim(self.cot_tokens, start + i * count, count, 0) for i in range(2)
        ]

    def turn(self, x, lens, cot_a, cot_b, order, every_cot):
        shapes = [self.crops_half] * 2 + [sds((self.rows, D), F32), sds(every_cot.shape, F32)]
        return call(functools.partial(turn_body, self.half, self.first_ids), shapes)(
            self.place, x, lens, self.cot_tokens, cot_a, cot_b, order, every_cot
        )

    def split(self, x):
        return call(functools.partial(split_body, self.half), [self.crops_half] * 2)(self.place, x)

    def join(self, keep, recv):
        return call(
            functools.partial(join_body, self.half), sds((self.crop_count, SLOTS, D), BF16)
        )(self.place, keep, recv)

    def scatter(self, keep, recv):
        return call(
            functools.partial(scatter_body, self.half, self.patch_count),
            sds((self.crop_count, self.patch_count, D), F32),
        )(self.place, keep, recv, self.slots)

    def adam_flat(self, kind, grad):
        return adam_math(
            self.fix[0],
            self.masters[kind],
            self.firsts[kind],
            self.seconds[kind],
            grad,
            rate_small if kind == 4 else rate_matrix,
            0.0 if kind == 4 else decay_matrix,
        )

    def adam_rows(self, fix, chunks, names, kinds, parts, extras):
        flats = [f[kind] for kind in kinds for f in (self.masters, self.firsts, self.seconds)]
        shapes = [sds(f.shape, F32) for f in flats] + [shape for _, shape in extras]
        plan = (chunks, names, [name for name, _ in extras])
        out = call(
            functools.partial(adam_body, plan),
            shapes,
            scratch=[pltpu.VMEM(flats[3 * i].shape, F32) for i in range(len(names))],
            smem=2,
        )(self.place, fix, *[a for part in parts for a in part], *flats)
        return [list(out[3 * i : 3 * i + 3]) for i in range(len(kinds))], out[3 * len(kinds) :]


def outputs(block_out, cls_grouped, patch_grad, results):
    return (block_out, cls_grouped, patch_grad) + tuple(
        results[kind][part] for part in range(3) for kind in range(5)
    )


def pack_call(place, operands, shapes):
    return pl.pallas_call(
        pack_body,
        in_specs=[SM] + [pl.BlockSpec(memory_space=pltpu.HBM)] * len(operands),
        out_specs=[VM] * len(shapes),
        out_shape=shapes,
        scratch_shapes=[pltpu.VMEM(a.shape, a.dtype) for a in operands]
        + [pltpu.SemaphoreType.DMA((len(operands),))],
        compiler_params=pltpu.CompilerParams(vmem_limit_bytes=VMEM_LIMIT),
        cost_estimate=NO_COST,
    )(place, *[pltpu.with_memory_space_constraint(a, pltpu.HBM) for a in operands])


def staged_step(step):
    place = step.place
    total_half = sum(c.half for c in GATHERED)
    rows_shape = sds((ROWS, total_half), F32)
    keep, send, downs = pack_call(
        place,
        step.masters[:3]
        + (step.masters[4], step.cot_cls, step.source_order[None, :], step.masters[3]),
        [rows_shape, rows_shape, sds((PAIR, 4 * D), F32)],
    )
    recv = permute(send, CORE)
    tok_keep, tok_send = step.tokens()
    width = GATHERED[1].width
    a, b = call(
        merge_body,
        [
            sds((1, PAIR, GATHERED[0].width), BF16),
            sds((1, PAIR, width + GATHERED[2].width), BF16),
        ],
        scratch=[pltpu.VMEM((PAIR, total_half), F32)],
    )(place, keep, recv, downs)

    a, tok_send = tie(a, tok_send)
    tok_recv = step.swap(tok_send)
    a_recv = permute(a, GATHER_STAGES[0])
    a_recv, b = tie(a_recv, b)
    a = jnp.concatenate([a, a_recv])
    a_recv = permute(a, GATHER_STAGES[1])
    a_recv, tok_recv, b = tie(a_recv, tok_recv, b)
    a = jnp.concatenate([a, a_recv])
    a_recv = permute(a, GATHER_STAGES[2])
    b_recv = permute(b, GATHER_STAGES[0])
    x, bias, lens = step.arrange(tok_keep, tok_recv)
    a_recv, b_recv, x = tie(a_recv, b_recv, x)
    a = jnp.concatenate([a, a_recv])
    b = jnp.concatenate([b, b_recv])
    a_recv = permute(a, GATHER_STAGES[3])
    b_recv = permute(b, GATHER_STAGES[1])
    a_sib = permute(a, CORE)
    cot_a, cot_b = step.cot_send()
    a, a_recv, a_sib, b_recv, cot_a, cot_b = tie(a, a_recv, a_sib, b_recv, cot_a, cot_b)
    a_sib = (a_sib, permute(a_recv, CORE))
    b = jnp.concatenate([b, b_recv])
    b_near = permute(b, GATHER_STAGES[2])
    b_side = permute(b, GATHER_STAGES[3])
    qkv0, proj0, up0, down0, small, up_bias = unpack(GATHERED[0], 0, (a, a_recv), a_sib, place)

    small0, small1 = small[0:12], small[12:24]
    norms_0, n1_0, qkv_0, att_0, prob_0, mid_0, n2_0 = layer_forward_one(
        x, bias, qkv0, proj0, small0
    )
    mid_0, n2_0, b_near = tie(mid_0, n2_0, b_near)
    b_far = permute(b_near, GATHER_STAGES[3])
    x_1, act_0, slope_0 = layer_forward_two(mid_0, n2_0, up0, down0, small0, up_bias[0:1])
    x_1, b_side, b_far = tie(x_1, b_side, b_far)
    b_own = (b, b_near, b_side, b_far)
    b_sib = tuple(permute(item, CORE) for item in b_own)
    cot_a = step.swap(cot_a)
    qkv1, proj1, every_cot, order = unpack(GATHERED[1], 0, b_own, b_sib, place)
    norms_1, n1_1, qkv_1, att_1, prob_1, mid_1, n2_1 = layer_forward_one(
        x_1, bias, qkv1, proj1, small1
    )
    mid_1, n2_1, cot_a, cot_b = tie(mid_1, n2_1, cot_a, cot_b)
    cot_b = step.swap(cot_b)
    up1, down1 = unpack(GATHERED[2], width, b_own, b_sib, place)
    final, act_1, slope_1 = layer_forward_two(mid_1, n2_1, up1, down1, small1, up_bias[1:2])
    out_keep, out_send, g, dense_cls = step.turn(final, lens, cot_a, cot_b, order, every_cot)

    def mlp_finish(layer):
        def finish(place, matrices, outs):
            arrange_sums(MLP_SUMS[layer], place, matrices, outs[0], outs[1])

        return finish

    def qkv_finish(layer):
        def finish(place, matrices, outs, rows):
            matrices = list(matrices)
            if layer == 0:
                weight, proj, rows_one1, rows_two1, up1, rows_two0, up0 = matrices
                table = outs[2]
                table[...] = jnp.zeros(table.shape, F32)
                table[:, 0:32] = small_table(((rows, rows_two0, up0), (rows_one1, rows_two1, up1)))
                matrices = [weight, proj, table]
            arrange_sums(QKV_SUMS[layer], place, matrices, outs[0], outs[1])

        return finish

    out_swap = Transfer(step.swap, out_send)
    keep, send, g_hid, bias_up1 = beside(
        [out_swap],
        lambda g: mlp_weights(
            place, mlp_finish(1), sum_shapes(MLP_SUMS[1]), g, n2_1, act_1, slope_1, down1
        ),
        g,
    )
    m1 = Reduction(MLP_SUMS[1], keep, send, place)
    g_mid, g_proj, g_att, rows_two1 = beside(
        [m1],
        lambda g_hid: mlp_rows(g, g_hid, norms_1[2], norms_1[3], att_1, up1, proj1, small1),
        g_hid,
    )
    keep, send, g_nrm, rows_one1 = beside(
        [m1],
        lambda g_att: qkv_weights(
            place, qkv_finish(1), sum_shapes(QKV_SUMS[1]), (g_proj, dense_cls),
            g_att, n1_1, qkv_1, prob_1, norms_1[0], qkv1,
        ),
        g_att,
    )
    q1 = Reduction(QKV_SUMS[1], keep, send, place)
    g = norm_one(g_nrm, norms_1[0], norms_1[1], g_mid, small1)

    keep, send, g_hid, bias_up0 = beside(
        [q1, m1],
        lambda g: mlp_weights(
            place, mlp_finish(0), sum_shapes(MLP_SUMS[0]), g, n2_0, act_0, slope_0, down0
        ),
        g,
    )
    m0 = Reduction(MLP_SUMS[0], keep, send, place)
    g_mid, g_proj, g_att, rows_two0 = beside(
        [m0, q1, m1],
        lambda g_hid: mlp_rows(g, g_hid, norms_0[2], norms_0[3], att_0, up0, proj0, small0),
        g_hid,
    )
    keep, send, _, g_nrm, _ = beside(
        [m0, q1, m1],
        lambda g_att: qkv_weights(
            place, qkv_finish(0), sum_shapes(QKV_SUMS[0]) + [sds((D, SMALL), F32)],
            (g_proj, rows_one1, rows_two1, bias_up1, rows_two0, bias_up0),
            g_att, n1_0, qkv_0, prob_0, norms_0[0], qkv0,
        ),
        g_att,
    )
    q0 = Reduction(QKV_SUMS[0], keep, send, place)
    back_keep, back_send = beside(
        [q0, m0, q1],
        lambda g_nrm: step.split(norm_one(g_nrm, norms_0[0], norms_0[1], g_mid, small0)),
        g_nrm,
    )
    block_out = beside(
        [q0, m0, q1], lambda keep, recv: step.join(keep, recv), out_keep, out_swap.recv
    )
    back_send, q0.send = tie(back_send, q0.send)
    back_recv = step.swap(back_send)
    back_keep = beside([q0, m0, m1], lambda v: v, back_keep)
    back_keep = beside([q0, m0, q1], lambda v: v, back_keep)

    def adam_mlp(fix, keep, recv):
        new = step.adam_rows(
            fix, [MLP_SUMS[1], MLP_SUMS[0]], ["up", "down"], [2, 3], [m1.result, m0.result], []
        )[0]
        return new[0] + new[1] + [step.scatter(keep, recv)]

    new = beside([q0], adam_mlp, step.fix, back_keep, back_recv)
    new_up, new_down, patch_grad = new[:3], new[3:6], new[6]
    q0.absorb(q0.move())
    (new_qkv, new_proj), (cls_grouped, small_own) = step.adam_rows(
        step.fix,
        [QKV_SUMS[1], QKV_SUMS[0]],
        ["qkv", "proj"],
        [0, 1],
        [q1.result, q0.result],
        [("cls", sds((step.crop_count, CLS), BF16)), ("small", sds((ROWS, SMALL), F32))],
    )
    small_flat = jnp.transpose(small_own[:, :24].reshape(ROWS, LAYERS, ROWS), (1, 0, 2))
    new_small = step.adam_flat(4, small_flat.reshape(LAYERS, ROWS * ROWS))
    return outputs(block_out, cls_grouped, patch_grad, (new_qkv, new_proj, new_up, new_down, new_small))


def plain_step(step):
    def gather(values):
        return lax.all_gather(values, AXES, axis=0, tiled=True)

    weights, smalls, up_biases = [], [], []
    for layer in range(LAYERS):
        flat = [gather(m[layer].astype(BF16)) for m in step.masters]
        small = flat[4].reshape(D, 8 + FF // D).astype(F32)
        weights.append(
            (
                flat[0].reshape(D, QKV),
                flat[1].reshape(D, D),
                flat[2].reshape(D, FF),
                flat[3].reshape(FF, D),
            )
        )
        smalls.append(jnp.transpose(small[:, :8]))
        up_biases.append(small[:, 8:].reshape(1, FF))
    keep, send = step.tokens()
    x, bias, lens = step.arrange(keep, step.swap(send))
    saved = []
    for layer in range(LAYERS):
        qkv_w, proj_w, up_w, down_w = weights[layer]
        one = layer_forward_one(x, bias, qkv_w, proj_w, smalls[layer])
        x, active, slope = layer_forward_two(
            one[5], one[6], up_w, down_w, smalls[layer], up_biases[layer]
        )
        saved.append(one + (active, slope))
    order = gather(step.source_order).astype(F32)[None, :]
    out_keep, out_send, g, dense_cls = step.turn(
        x, lens, *[step.swap(item) for item in step.cot_send()], order, gather(step.cot_cls)
    )
    block_out = step.join(out_keep, step.swap(out_send))
    gradients = [None] * LAYERS

    def two_out(place, matrices, outs, *_):
        for value, out in zip(matrices, outs):
            out[...] = value[...]

    for layer in reversed(range(LAYERS)):
        norms, normed_one, qkv, attended, prob, _, normed_two, active, slope = saved[layer]
        qkv_w, proj_w, up_w, down_w = weights[layer]
        g_up, g_down, g_hid, bias_up = mlp_weights(
            step.place, two_out, [sds((D, FF), F32), sds((FF, D), F32)],
            g, normed_two, active, slope, down_w,
        )
        g_mid, g_proj, g_att, two = mlp_rows(
            g, g_hid, norms[2], norms[3], attended, up_w, proj_w, smalls[layer]
        )
        g_qkv_w, g_nrm, one = qkv_weights(
            step.place, two_out, [sds((D, QKV), F32)], (),
            g_att, normed_one, qkv, prob, norms[0], qkv_w,
        )
        g = norm_one(g_nrm, norms[0], norms[1], g_mid, smalls[layer])
        eight = jnp.concatenate([one[0:4], two[3:4], two[0:3]])
        table = jnp.concatenate([jnp.transpose(eight), bias_up.reshape(D, FF // D)], 1)
        gradients[layer] = (g_qkv_w, g_proj, g_up, g_down, table)
    back_keep, back_send = step.split(g)
    patch_grad = step.scatter(back_keep, step.swap(back_send))

    def scatter_sum(values):
        return lax.psum_scatter(values, AXES, scatter_dimension=0, tiled=True)

    results = []
    for kind in range(5):
        shares = [
            scatter_sum(gradients[layer][kind].reshape(-1).astype(F32)) for layer in range(LAYERS)
        ]
        results.append(step.adam_flat(kind, jnp.stack(shares)))
    cls_grouped = scatter_sum(dense_cls).astype(BF16)
    return outputs(block_out, cls_grouped, patch_grad, results)


def on_device(crop_devices, dp_devices, *arguments):
    step = Step(crop_devices, dp_devices, arguments)
    owned = step.masters[0].shape[1]
    staged = crop_devices * dp_devices == 2 * CHIPS and owned == ROWS * QKV
    if staged and step.crop_count <= ROWS:
        return staged_step(step)
    return plain_step(step)


def solution(mesh):
    crops = [P(AXES, None, None), P(AXES, None), P(AXES), P(AXES), P(AXES, None, None)]
    flat = P(None, AXES)
    return jax.shard_map(
        functools.partial(on_device, mesh.shape["crop"], mesh.shape["dp"]),
        mesh=mesh,
        in_specs=tuple(crops + [P(AXES, None), P()] + [flat] * 15),
        out_specs=(crops[0], crops[1], crops[0]) + (flat,) * 15,
        check_vma=False,
    )
```

```python
import functools

import jax
import jax.numpy as jnp
from jax import lax
from jax.experimental import pallas as pl
from jax.experimental.pallas import tpu as pltpu
from jax.sharding import PartitionSpec as P

D = 384
HEADS = 6
HEAD_DIM = 64
FF = 1536
LAYERS = 2
SLOTS = 144
FOCAL_SLOTS = 32
LEN_ROW = 143

eps_norm = 1e-06
neg_big = -1e30
adam_eps = 1e-08
rate_matrix = 0.04
decay_matrix = 0.05
rate_small = 0.4

F32 = jnp.float32
BF16 = jnp.bfloat16
VM = pl.BlockSpec(memory_space=pltpu.VMEM)
SM = pl.BlockSpec(memory_space=pltpu.SMEM)
AXES = ("crop", "dp")
VMEM_LIMIT = 12 * 1024 * 1024
NO_COST = pl.CostEstimate(flops=1, bytes_accessed=1, transcendentals=0)


def sds(shape, dtype):
    return jax.ShapeDtypeStruct(shape, dtype)


def call(body, out_shape, scratch=(), smem=1):
    def run(*operands):
        return pl.pallas_call(
            body,
            out_shape=out_shape,
            in_specs=[SM] * smem + [VM] * (len(operands) - smem),
            out_specs=jax.tree.map(lambda _: VM, out_shape),
            scratch_shapes=list(scratch),
            compiler_params=pltpu.CompilerParams(vmem_limit_bytes=VMEM_LIMIT),
            cost_estimate=NO_COST,
        )(*operands)

    return run


def iota(shape, axis):
    return lax.broadcasted_iota(jnp.int32, shape, axis)


def dot(a, b, ca, cb):
    return lax.dot_general(a, b, (((ca,), (cb,)), ((), ())), preferred_element_type=F32)


def slot_onehot(slots, c, patch_count):
    row = slots[pl.ds(c, 1), :]
    return row, (iota((patch_count, SLOTS), 0) == row).astype(F32).astype(BF16)


def tokens_body(half, patch_count, place, patches, slots, keep, send):
    y = place[1]
    row_index = iota((SLOTS, D), 0)
    for i in range(half):
        for out, c in ((keep, half * y + i), (send, half * (1 - y) + i)):
            row, onehot = slot_onehot(slots, c, patch_count)
            count = jnp.sum((row >= 0).astype(F32), axis=1, keepdims=True) - 1.0
            picked = dot(onehot, patches[c], 0, 0)
            out[i] = jnp.where(row_index == LEN_ROW, count, picked).astype(BF16)


class Halves:
    def __init__(self, first, second):
        self.parts, self.count = (first, second), first.shape[0]

    def __getitem__(self, key):
        i = key[0] if isinstance(key, tuple) else key
        rest = key[1:] if isinstance(key, tuple) else ()
        return self.parts[i // self.count][(i % self.count,) + tuple(rest)]


def arrange_body(half, place, keep, recv, x_ref, bias_ref, lens_ref):
    y = place[1]
    base = half * SLOTS
    used = half * FOCAL_SLOTS

    def run(v_src, f_src):
        k = iota((SLOTS, 2 * SLOTS), 0)
        q = iota((SLOTS, 2 * SLOTS), 1) % SLOTS
        row_index = iota((SLOTS, D), 0)
        for i in range(half):
            t = v_src[i].astype(F32)
            n = t[LEN_ROW : LEN_ROW + 1, 0:1]
            x_ref[SLOTS * i : SLOTS * (i + 1), :] = jnp.where(row_index == LEN_ROW, 0.0, t)
            bias_ref[i] = jnp.where(k.astype(F32) <= n, 0.0, neg_big)
            lens_ref[i : i + 1, :] = jnp.broadcast_to(n, (1, 128))
        limit = jnp.full((SLOTS, 2 * SLOTS), 1000.0, F32)
        for i in range(half):
            x_ref[base + FOCAL_SLOTS * i : base + FOCAL_SLOTS * (i + 1), :] = f_src[
                i, 0:FOCAL_SLOTS
            ].astype(F32)
            n = f_src[i, SLOTS - 16 : SLOTS].astype(F32)[15:16, 0:1]
            limit = jnp.where((k // FOCAL_SLOTS) == i, n, limit)
            lens_ref[half + i : half + i + 1, :] = jnp.broadcast_to(n, (1, 128))
        if used < SLOTS:
            x_ref[base + used : base + SLOTS, :] = jnp.zeros((SLOTS - used, D), F32)
        same = (q // FOCAL_SLOTS) == (k // FOCAL_SLOTS)
        inside = (k % FOCAL_SLOTS).astype(F32) <= limit
        bias_ref[half] = jnp.where(same & inside, 0.0, neg_big)

    @pl.when(y == 0)
    def _():
        run(keep, recv)

    @pl.when(y == 1)
    def _():
        run(recv, keep)


def turn_body(half, first_ids, place, x_ref, lens, cot, recv_a, recv_b, order, every_cot, *outs):
    keep, send, g_ref, dense = outs
    recv = Halves(recv_a, recv_b)
    y = place[1]
    base = half * SLOTS
    used = half * FOCAL_SLOTS
    views, focals = first_ids(place)
    index = iota((2 * half, 1), 0)
    ids = jnp.where(index < half, views + index, focals + index - half).astype(F32)
    chosen = (order[...] == ids).astype(F32).astype(BF16)
    top = dot(chosen, every_cot[...], 1, 0)

    def piece(values, n, row, rows):
        at = iota((rows, D), 0)
        masked = jnp.where(at.astype(F32) <= n, values, 0.0)
        return masked + jnp.where(at == 0, row, 0.0)

    def run(v_out, f_out, v_get, f_get):
        cls = []
        for i in range(half):
            n = lens[i : i + 1, 0:1]
            rows = slice(SLOTS * i, SLOTS * (i + 1))
            v = x_ref[rows, :]
            cls.append(v[0:1])
            v_out[i] = jnp.where(iota((SLOTS, D), 0).astype(F32) <= n, v, 0.0).astype(BF16)
            g_ref[rows, :] = piece(v_get(i).astype(F32), n, top[i : i + 1], SLOTS)
        for i in range(half):
            n = lens[half + i : half + i + 1, 0:1]
            rows = slice(base + FOCAL_SLOTS * i, base + FOCAL_SLOTS * (i + 1))
            f = x_ref[rows, :]
            cls.append(f[0:1])
            f = jnp.where(iota((FOCAL_SLOTS, D), 0).astype(F32) <= n, f, 0.0)
            f_out[i, 0:FOCAL_SLOTS] = f.astype(BF16)
            f_out[i, FOCAL_SLOTS:SLOTS] = jnp.zeros((SLOTS - FOCAL_SLOTS, D), BF16)
            g_ref[rows, :] = piece(
                f_get(i)[0:FOCAL_SLOTS].astype(F32), n, top[half + i : half + i + 1], FOCAL_SLOTS
            )
        if used < SLOTS:
            g_ref[base + used : base + SLOTS, :] = jnp.zeros((SLOTS - used, D), F32)
        dense[...] = dot(chosen, jnp.concatenate(cls, 0).astype(BF16), 0, 0)

    @pl.when(y == 0)
    def _():
        run(keep, send, lambda i: cot[i], lambda i: recv[i])

    @pl.when(y == 1)
    def _():
        run(send, keep, lambda i: recv[i], lambda i: cot[half + i])


def split_body(half, place, x_ref, keep, send):
    y = place[1]
    base = half * SLOTS

    def run(v_out, f_out):
        for i in range(half):
            v_out[i] = x_ref[SLOTS * i : SLOTS * (i + 1), :].astype(BF16)
            rows = slice(base + FOCAL_SLOTS * i, base + FOCAL_SLOTS * (i + 1))
            f_out[i, 0:FOCAL_SLOTS] = x_ref[rows, :].astype(BF16)
            f_out[i, FOCAL_SLOTS:SLOTS] = jnp.zeros((SLOTS - FOCAL_SLOTS, D), BF16)

    @pl.when(y == 0)
    def _():
        run(keep, send)

    @pl.when(y == 1)
    def _():
        run(send, keep)


def join_body(half, place, keep, recv, out):
    y = place[1]
    for i in range(half):
        out[half * y + i] = keep[i]
        out[half * (1 - y) + i] = recv[i]


def scatter_body(half, patch_count, place, keep, recv, slots, out, *work):
    y = place[1]
    stride = work[0].shape[0] // (2 * half)
    for i in range(half):
        for src, c in ((keep, half * y + i), (recv, half * (1 - y) + i)):
            _, onehot = slot_onehot(slots, c, patch_count)
            first = pl.multiple_of(c * stride, 8)
            rows = dot(onehot, src[i], 1, 0)
            for t, part in enumerate(work):
                part[pl.ds(first, patch_count), :] = rows[:, 128 * t : 128 * (t + 1)]

    def copy(p):
        for t, part in enumerate(work):
            out[p, :, 128 * t : 128 * (t + 1)] = part[pl.ds(p, 2 * half, stride=stride), :]

    group = 8

    def step(i, _):
        for j in range(group):
            copy(i * group + j)
        return 0

    lax.fori_loop(0, patch_count // group, step, 0)
    for p in range(patch_count // group * group, patch_count):
        copy(p)


def lane_mask(second, value):
    lane = iota((1, 128), 1)
    chosen = (lane >= HEAD_DIM) if second else (lane < HEAD_DIM)
    return jnp.where(chosen, value, 0.0).astype(BF16)


def pair_rows(values, scale):
    return jnp.concatenate([values * lane_mask(0, scale), values * lane_mask(1, scale)], 0)


def pair_lanes(values):
    own = iota((SLOTS, 128), 1) < HEAD_DIM
    return jnp.where(own, values[:SLOTS], values[SLOTS:])


def heads_at(part, pair):
    return slice(part * D + 128 * pair, part * D + 128 * (pair + 1))


PAIRS = HEADS // 2
HEAD_SCALE = HEAD_DIM**-0.5


def attend_forward_block(qkv, bias, attended, prob, r, b):
    for i in range(PAIRS):
        queries = pair_rows(qkv[r, heads_at(0, i)], HEAD_SCALE)
        s = dot(qkv[r, heads_at(1, i)], queries, 1, 1) + bias
        e = jnp.exp(s - jnp.max(s, 0, keepdims=True))
        prob[b, i] = (e * (1.0 / jnp.sum(e, 0, keepdims=True))).astype(BF16)
    for i in range(PAIRS):
        out = dot(prob[b, i], qkv[r, heads_at(2, i)], 0, 0)
        attended[r, heads_at(0, i)] = pair_lanes(out).astype(BF16)


def attend_backward_block(qkv, prob, grad, out, r, b):
    grads = [pair_rows(grad[r, heads_at(0, i)], 1.0) for i in range(PAIRS)]
    inner = [dot(qkv[r, heads_at(2, i)], grads[i], 1, 1) for i in range(PAIRS)]
    for i in range(PAIRS):
        out[r, heads_at(2, i)] = dot(prob[b, i], grads[i], 1, 0).astype(BF16)
    scores = []
    for i in range(PAIRS):
        p = prob[b, i].astype(F32)
        t = p * inner[i]
        scores.append((t - p * jnp.sum(t, 0, keepdims=True)).astype(BF16))
    for i in range(PAIRS):
        queries = pair_rows(qkv[r, heads_at(0, i)], HEAD_SCALE)
        out[r, heads_at(1, i)] = dot(scores[i], queries, 1, 0).astype(BF16)
    for i in range(PAIRS):
        back = pair_lanes(dot(scores[i], qkv[r, heads_at(1, i)], 0, 0))
        out[r, heads_at(0, i)] = (back * HEAD_SCALE).astype(BF16)


def total(values):
    return jnp.sum(values, 0, keepdims=True)


def normalized(values):
    centered = values - jnp.mean(values, -1, keepdims=True)
    scale = lax.rsqrt(jnp.mean(centered * centered, -1, keepdims=True) + eps_norm)
    return centered * scale, scale


def gelu_parts(v):
    c = 0.7978845608028654
    a = 0.044715
    square = v * v
    t = jnp.tanh(v * (c + (c * a) * square))
    h = 0.5 * v
    ht = h * t
    return h + ht, 0.5 * (1.0 + t) + (h - ht * t) * (c + (3.0 * a * c) * square)


def attention_body(x, bias, qkv_w, proj_w, small, *outs):
    unit_one, scale_one, unit_two, scale_two, normed_one, qkv, attended, prob, mid, normed_two = outs
    count = x.shape[0] // SLOTS

    def norm(values, r, unit_ref, scale_ref, normed_ref, first):
        unit, scale = normalized(values)
        unit_ref[r, :] = unit.astype(BF16)
        scale_ref[r, :] = scale
        normed_ref[r, :] = (unit * small[first : first + 1] + small[first + 1 : first + 2]).astype(
            BF16
        )

    over_blocks(count, lambda r, b: norm(x[r, :], r, unit_one, scale_one, normed_one, 0))
    for c in range(3):
        w = slice(c * D, (c + 1) * D)
        part = dot(normed_one[...], qkv_w[:, w], 1, 0)
        if c != 1:
            part = part + small[2 + c // 2 : 3 + c // 2]
        qkv[:, w] = part.astype(BF16)
    over_blocks(count, lambda r, b: attend_forward_block(qkv, bias[b], attended, prob, r, b))
    mid[...] = dot(attended[...], proj_w[...], 1, 0)

    def second(r, _):
        whole = x[r, :] + mid[r, :] + small[4:5]
        mid[r, :] = whole
        norm(whole, r, unit_two, scale_two, normed_two, 5)

    over_blocks(count, second)


def layer_forward_one(x, bias, qkv_w, proj_w, small):
    rows = x.shape[0]
    row = sds((rows, D), BF16)
    scale = sds((rows, 1), F32)
    out = call(
        attention_body,
        [
            row, scale, row, scale, row, sds((rows, 3 * D), BF16), row,
            sds((rows // SLOTS, PAIRS, SLOTS, 2 * SLOTS), BF16), sds((rows, D), F32), row,
        ],
        smem=0,
    )(x, bias, qkv_w, proj_w, small)
    return (tuple(out[:4]),) + tuple(out[4:])


def feed_forward_body(mid, normed, up_w, down_w, small, up_bias, out, active, slope):
    for c in range(FF // 256):
        w = slice(c * 256, (c + 1) * 256)
        value, derivative = gelu_parts(dot(normed[...], up_w[:, w], 1, 0) + up_bias[:, w])
        active[:, w] = value.astype(BF16)
        slope[:, w] = derivative.astype(BF16)
    out[...] = dot(active[...], down_w[...], 1, 0) + mid[...] + small[7:8]


def layer_forward_two(mid, normed_two, up_w, down_w, small, up_bias):
    rows = mid.shape[0]
    return call(
        feed_forward_body,
        [sds((rows, D), F32), sds((rows, FF), BF16), sds((rows, FF), BF16)],
        smem=0,
    )(mid, normed_two, up_w, down_w, small, up_bias)


def over_blocks(count, step):
    def body(b, _):
        step(pl.ds(pl.multiple_of(b * SLOTS, 16), SLOTS), b)
        return 0

    lax.fori_loop(0, count, body, 0)


def norm_back(grad, unit, scale, gain):
    inner = grad * gain
    mean, along = jnp.mean(inner, -1, keepdims=True), jnp.mean(inner * unit, -1, keepdims=True)
    return scale * (inner - mean - unit * along)


def mlp_weights_body(finish, place, g, normed, active, slope, down_w, *refs):
    outs, (branch, up, down) = refs[:-3], refs[-3:]
    g_hidden, bias_up = outs[-2:]
    branch[...] = g[...].astype(BF16)
    for c in range(FF // D):
        w = slice(c * D, (c + 1) * D)
        t = (dot(branch[...], down_w[w, :], 1, 1) * slope[:, w].astype(F32)).astype(BF16)
        g_hidden[:, w] = t
        bias_up[:, w] = total(t.astype(F32))
    for c in range(FF // D):
        w = slice(c * D, (c + 1) * D)
        down[w, :] = dot(active[:, w], branch[...], 0, 0)
    up[...] = dot(normed[...], g_hidden[...], 0, 0)
    finish(place, (up, down), outs[:-2])


def mlp_rows_body(g, g_hidden, unit, scale, attended, up_w, proj_w, small, g_mid, g_proj, g_att, rows, work):
    rows[...] = jnp.zeros(rows.shape, F32)
    g_mid[...] = dot(g_hidden[...], up_w[...], 1, 1)

    def step(r, _):
        grad = g_mid[r, :]
        along = unit[r, :].astype(F32)
        whole = norm_back(grad, along, scale[r, :], small[5:6]) + g[r, :]
        g_mid[r, :] = whole
        rounded = whole.astype(BF16)
        work[r, :] = rounded
        rows[0:1] += total(grad * along)
        rows[1:2] += total(grad)
        rows[2:3] += total(g[r, :].astype(BF16).astype(F32))
        rows[3:4] += total(rounded.astype(F32))

    over_blocks(g.shape[0] // SLOTS, step)
    g_att[...] = dot(work[...], proj_w[...], 1, 1).astype(BF16)
    g_proj[...] = dot(attended[...], work[...], 0, 0)


def qkv_weights_body(finish, extra_count, place, g_att, normed, qkv, prob, unit, qkv_w, *refs):
    extra, outs, (g_qkv, weight) = refs[:extra_count], refs[extra_count:-2], refs[-2:]
    g_normed, rows = outs[-2:]
    rows[...] = jnp.zeros(rows.shape, F32)
    count = unit.shape[0] // SLOTS
    over_blocks(count, lambda r, b: attend_backward_block(qkv, prob, g_att, g_qkv, r, b))
    g_normed[...] = dot(g_qkv[...], qkv_w[...], 1, 1)

    def step(r, _):
        grad = g_normed[r, :]
        rows[0:1] += total(grad * unit[r, :].astype(F32))
        rows[1:2] += total(grad)
        rows[2:3] += total(g_qkv[r, 0:D].astype(F32))
        rows[3:4] += total(g_qkv[r, 2 * D : 3 * D].astype(F32))

    over_blocks(count, step)
    weight[...] = dot(normed[...], g_qkv[...], 0, 0)
    finish(place, (weight,) + extra, outs[:-2], rows)


def norm_one_body(g_normed, unit, scale, g_mid, small, out):
    def step(r, _):
        back = norm_back(g_normed[r, :], unit[r, :].astype(F32), scale[r, :], small[0:1])
        out[r, :] = back + g_mid[r, :]

    over_blocks(unit.shape[0] // SLOTS, step)


def mlp_weights(place, finish, shapes, g, normed, active, slope, down_w):
    rows = g.shape[0]
    return call(
        functools.partial(mlp_weights_body, finish),
        list(shapes) + [sds((rows, FF), BF16), sds((1, FF), F32)],
        scratch=[
            pltpu.VMEM((rows, D), BF16),
            pltpu.VMEM((D, FF), F32),
            pltpu.VMEM((FF, D), F32),
        ],
    )(place, g, normed, active, slope, down_w)


def mlp_rows(g, g_hidden, unit, scale, attended, up_w, proj_w, small):
    rows = g.shape[0]
    return call(
        mlp_rows_body,
        [sds((rows, D), F32), sds((D, D), F32), sds((rows, D), BF16), sds((8, D), F32)],
        scratch=[pltpu.VMEM((rows, D), BF16)],
        smem=0,
    )(g, g_hidden, unit, scale, attended, up_w, proj_w, small)


def qkv_weights(place, finish, shapes, extra, g_att, normed, qkv, prob, unit, qkv_w):
    rows = unit.shape[0]
    return call(
        functools.partial(qkv_weights_body, finish, len(extra)),
        list(shapes) + [sds((rows, D), F32), sds((8, D), F32)],
        scratch=[pltpu.VMEM((rows, 3 * D), BF16), pltpu.VMEM((D, 3 * D), F32)],
    )(place, g_att, normed, qkv, prob, unit, qkv_w, *extra)


def norm_one(g_normed, unit, scale, g_mid, small):
    return call(norm_one_body, sds(g_mid.shape, F32), smem=0)(g_normed, unit, scale, g_mid, small)


def small_table(groups):
    flat, wide = [], []
    lane = iota((1, FF), 1) % 4
    for rows_one, rows_two, bias_up in groups:
        flat += [rows_one[0:4, :], rows_two[3:4, :], rows_two[0:3, :], jnp.zeros((4, D), F32)]
        wide += [jnp.zeros((8, FF), F32)]
        wide += [jnp.where(lane == k, bias_up[...], 0.0) for k in range(4)]
    flat = jnp.concatenate(flat + [jnp.zeros((8, D), F32)], 0).astype(BF16)
    wide = jnp.concatenate(wide + [jnp.zeros((8, FF), F32)], 0).astype(BF16)
    same = (iota((D, D), 0) == iota((D, D), 1)).astype(F32).astype(BF16)
    spread = (iota((D, FF), 1) // 4 == iota((D, FF), 0)).astype(F32).astype(BF16)
    return dot(same, flat, 1, 1) + dot(spread, wide, 1, 1)


ROWS = 12
PAIR = 24
CHIPS = 16
QKV, PROJ, UP, SMALL, CLS, ORDER, PAD = 3 * D, D, FF, 128, D, 128, 128
CORE = (1, 1)
TABLES = ("small", "order")
GATHER_STAGES = ((4, 8), (8, 4), (2, 16), (16, 2))


class Chunk:
    def __init__(self, names, widths, down):
        self.names, self.widths, self.down = names, widths, down
        self.half = sum(widths) // 2
        self.width = self.half + (2 * D if down is not None else 0)
        self.arrays = [n for n in names if n != "pad"] + (["down"] if down is not None else [])

    def pieces(self, which):
        low, high, start, found = which * self.half, (which + 1) * self.half, 0, []
        for name, width in zip(self.names, self.widths):
            a, b = max(start, low), min(start + width, high)
            if a < b:
                found.append((name, a - start, a - low, b - a))
            start += width
        return found


GATHERED = (
    Chunk(("qkv0", "proj0", "up0", "small", "pad"), (QKV, PROJ, UP, SMALL, PAD), 0),
    Chunk(("qkv1", "proj1", "cls", "order"), (QKV, PROJ, CLS, ORDER), None),
    Chunk(("up1",), (UP,), 1),
)
MLP_SUMS = (Chunk(("up0",), (UP,), 0), Chunk(("up1",), (UP,), 1))
QKV_SUMS = (
    Chunk(("qkv0", "proj0", "small", "pad"), (QKV, PROJ, SMALL, PAD), None),
    Chunk(("qkv1", "proj1", "cls", "pad"), (QKV, PROJ, CLS, PAD), None),
)
FLAT = {"qkv": QKV, "proj": PROJ, "up": UP}


def by_core(place, run):
    for b in range(2):

        @pl.when((place[0] & 1) == b)
        def _(b=b):
            run(b)


def chip_of(place, core, bits):
    mask = 0
    for bit, stage in zip(bits, GATHER_STAGES):
        mask ^= stage[core] * bit
    return (place[0] ^ mask) >> 1


def bits_of(index, count=4):
    return [(index >> k) & 1 for k in range(count)]


def tie(*values):
    return lax.optimization_barrier(values)


def small_block(flat, layer):
    row = flat[layer : layer + 1, :].astype(BF16).astype(F32)
    width = ROWS * ROWS
    spread = jnp.where(iota((16, width), 1) // ROWS == iota((16, width), 0), row, 0.0).astype(BF16)
    at = iota((width, 128), 0) % ROWS + ROWS * layer
    chosen = (at == iota((width, 128), 1)).astype(F32).astype(BF16)
    return dot(spread, chosen, 1, 0)[0:ROWS]


def order_block(ref):
    count = ref.shape[1]
    row = ref[...].astype(F32)
    mine = iota((16, count), 0) == iota((16, count), 1)
    number = jnp.sum(jnp.where(mine, row, 0.0), 1, keepdims=True)
    number = jnp.where(iota((16, 1), 0) < count, number, -129.0)
    high = jnp.floor(number * (1.0 / 128.0))
    lane = iota((16, 128), 1)
    return jnp.where(lane == 0, high, number - 128.0 * high)[0:ROWS]


def pack_body(place, *refs):
    held, (keep, send, down_out), local, sem = refs[0:7], refs[7:10], refs[10:17], refs[17]
    copies = [
        pltpu.make_async_copy(src, dst, sem.at[i]) for i, (src, dst) in enumerate(zip(held, local))
    ]
    for copy in copies:
        copy.start()
    for copy in copies:
        copy.wait()
    source = dict(zip(("qkv", "proj", "up", "small", "cls", "order"), local))
    down = local[6]

    def run(b):
        base = 0
        for chunk in GATHERED:
            for out, which in ((keep, b), (send, 1 - b)):
                for name, column, at, width in chunk.pieces(which):
                    span = slice(base + at, base + at + width)
                    if name == "pad":
                        out[:, span] = jnp.zeros((ROWS, width), F32)
                    elif name == "small":
                        out[:, span] = small_block(source["small"], 0) + small_block(
                            source["small"], 1
                        )
                    elif name == "order":
                        out[:, span] = order_block(source["order"])
                    elif name == "cls":
                        count = source["cls"].shape[0]
                        out[:, span] = jnp.zeros((ROWS, width), F32)
                        out[0:count, span] = source["cls"][:, column : column + width].astype(F32)
                    else:
                        flat, full = source[name[:-1]], FLAT[name[:-1]]
                        for r in range(ROWS):
                            first = r * full + column
                            layer = int(name[-1])
                            out[r : r + 1, span] = flat[layer : layer + 1, first : first + width]
            base += chunk.half

    by_core(place, run)
    for layer in range(LAYERS):
        for r in range(2 * PAIR):
            first = (2 * layer + r // PAIR) * D
            down_out[r % PAIR : r % PAIR + 1, first : first + D] = down[
                layer : layer + 1, r * D : (r + 1) * D
            ]


def merge_body(place, keep, recv, down, *rest):
    outs, work = rest[:2], rest[2]

    def run(b):
        work[ROWS * b : ROWS * (b + 1), :] = keep[...]
        work[ROWS * (1 - b) : ROWS * (2 - b), :] = recv[...]

    by_core(place, run)
    source = target = 0
    for number, chunk in enumerate(GATHERED):
        out = outs[min(number, 1)]
        if number <= 1:
            target = 0
        out[0, :, target : target + chunk.half] = work[:, source : source + chunk.half].astype(BF16)
        if chunk.down is not None:
            at, first = target + chunk.half, 2 * D * chunk.down
            out[0, :, at : at + 2 * D] = down[:, first : first + 2 * D].astype(BF16)
        source, target = source + chunk.half, target + chunk.width


def unpack_body(chunk, base, pieces, place, *refs):
    own, sib, outs = refs[:pieces], refs[pieces : 2 * pieces], refs[2 * pieces :]
    low = 3 if pieces == 2 else 2
    target = dict(zip([n for n in chunk.arrays if n not in TABLES], outs))
    if "small" in chunk.names:
        rows_out, up_out, target["small"] = outs[-3:]
    if "order" in chunk.names:
        order_out, target["order"] = outs[-2:]

    def run(b):
        for which in range(2):
            source = own if which == b else sib
            for received in range(pieces):
                block = source[received]

                def step(index, _, which=which, received=received, block=block):
                    chip = chip_of(place, which, bits_of(index, low) + bits_of(received, 4 - low))
                    for name, column, at, width in chunk.pieces(which):
                        if name == "pad":
                            continue
                        values = block[index, :, base + at : base + at + width]
                        if name in TABLES:
                            values = values.astype(F32)
                        target[name][chip, :, column : column + width] = values
                    for part in range(0 if chunk.down is None else 2):
                        first = base + chunk.half + part * D
                        target["down"][chip * 4 + 2 * which + part] = block[
                            index, :, first : first + D
                        ]
                    return 0

                lax.fori_loop(0, CHIPS // pieces, step, 0)

    by_core(place, run)
    if "order" in chunk.names:
        across = jnp.transpose(target["order"][...].reshape(D, ORDER))
        order_out[...] = across[0:1] * 128.0 + across[1:2]
    if "small" in chunk.names:
        across = jnp.transpose(target["small"][...].reshape(D, SMALL))
        rows_out[...] = across[0:24]
        ups = jnp.concatenate([across[8:12], across[20:24]], 0).astype(BF16)
        spread = (iota((D, FF), 1) // 4 == iota((D, FF), 0)).astype(F32).astype(BF16)
        wide = dot(ups, spread, 1, 0)
        lane = iota((1, FF), 1) % 4
        for layer in range(LAYERS):
            row = jnp.zeros((1, FF), F32)
            for k in range(4):
                row = jnp.where(lane == k, wide[4 * layer + k : 4 * layer + k + 1], row)
            up_out[layer : layer + 1, :] = row


def permute(x, masks):
    return lax.ppermute(x, AXES, [(i, i ^ masks[i & 1]) for i in range(2 * CHIPS)])


def unpack(chunk, base, pieces, sib, place):
    shapes = [
        sds((CHIPS, PAIR, width), BF16)
        for name, width in zip(chunk.names, chunk.widths)
        if name != "pad" and name not in TABLES
    ]
    if chunk.down is not None:
        shapes.append(sds((4 * CHIPS, PAIR, D), BF16))
    count, scratch = len(shapes), []
    if "small" in chunk.names:
        shapes += [sds((24, D), F32), sds((LAYERS, FF), F32)]
        scratch = [pltpu.VMEM((CHIPS, PAIR, SMALL), F32)]
    if "order" in chunk.names:
        shapes += [sds((1, D), F32)]
        scratch = [pltpu.VMEM((CHIPS, PAIR, ORDER), F32)]
    out = call(functools.partial(unpack_body, chunk, base, len(pieces)), shapes, scratch=scratch)(
        place, *pieces, *sib
    )
    return [b.reshape(-1, b.shape[2]) for b in out[:count]] + list(out[count:])


def arrange_sums(chunk, place, matrices, keep, send):
    source = dict(zip(chunk.arrays, matrices))

    def run(b):
        for out, which in ((keep, b), (send, 1 - b)):

            def step(index, _, out=out, which=which):
                chip = chip_of(place, which, bits_of(index))
                rows = pl.ds(pl.multiple_of(chip * PAIR, 8), PAIR)
                for name, column, at, width in chunk.pieces(which):
                    if name == "pad":
                        out[index, :, at : at + width] = jnp.zeros((PAIR, width), BF16)
                    else:
                        out[index, :, at : at + width] = source[name][
                            rows, column : column + width
                        ].astype(BF16)
                for part in range(0 if chunk.down is None else 2):
                    at = chunk.half + part * D
                    first = pl.multiple_of((chip * 4 + 2 * which + part) * PAIR, 8)
                    out[index, :, at : at + D] = source["down"][pl.ds(first, PAIR), :].astype(BF16)
                return 0

            lax.fori_loop(0, CHIPS, step, 0)

    by_core(place, run)


def sum_shapes(chunk):
    return [sds((CHIPS, PAIR, chunk.width), BF16)] * 2


def split_rows_body(chunk, place, own, recv, keep, send, *down_out):
    def run(b):
        whole = own[...] + recv[...].astype(F32)
        for out, core in ((keep, b), (send, 1 - b)):
            out[...] = whole[ROWS * core : ROWS * (core + 1), : chunk.half]
        if chunk.down is not None:
            down_out[0][...] = whole[:, chunk.half :]

    by_core(place, run)


class Reduction:
    def __init__(self, chunk, keep, send, place, direct=False):
        self.chunk, self.place, self.stage = chunk, place, 0
        self.keep, self.send = keep, [send]
        z_one, z_two, near, far = GATHER_STAGES
        across = [[near, far, (near[0] ^ far[0],) * 2]] if direct else [[far], [near]]
        self.routes = [[CORE]] + across + [[z_two], [z_one], [CORE]]

    def move(self):
        self.stage += 1
        return [permute(s, mask) for s, mask in zip(self.send, self.routes[self.stage - 1])]

    def absorb(self, received):
        if self.stage == len(self.routes):
            self.result = (self.keep, received[0]) + tuple(self.rest)
            return
        if self.stage == len(self.routes) - 1:
            chunk = self.chunk
            shapes = [sds((ROWS, chunk.half), F32)] * 2
            if chunk.down is not None:
                shapes.append(sds((PAIR, 2 * D), F32))
            self.keep, send, *self.rest = call(functools.partial(split_rows_body, chunk), shapes)(
                self.place, self.keep[0], received[0][0]
            )
            self.send = [send]
            return
        parts = len(self.routes[self.stage]) + 1
        count = self.keep.shape[0] // parts

        def part(i):
            span = slice(i * count, (i + 1) * count)
            return sum([r[span].astype(F32) for r in received], self.keep[span].astype(F32))

        self.send = [part(i).astype(BF16) for i in range(1, parts)]
        self.keep = part(0)


class Transfer:
    def __init__(self, swap, send):
        self.swap, self.send = swap, [send]

    def move(self):
        return [self.swap(self.send[0])]

    def absorb(self, received):
        self.recv = received[0]


def beside(moving, run, *inputs):
    sends, inputs = lax.optimization_barrier(([m.send for m in moving], inputs))
    for m, send in zip(moving, sends):
        m.send = send
    received = [m.move() for m in moving]
    received, out = lax.optimization_barrier((received, run(*inputs)))
    for m, got in zip(moving, received):
        m.absorb(got)
    return out


def adam_math(fix, master, first, second, grad, rate, decay):
    moment = 0.5 * first + 0.5 * grad
    square = 0.5 * second + 0.5 * grad * grad
    update = moment / fix / (jnp.sqrt(square / fix) + adam_eps) + decay * master
    return master - rate * update, moment, square


def small_flat(table):
    width = ROWS * ROWS
    row, column = iota((ROWS, width), 1) // ROWS, iota((ROWS, width), 1) % ROWS
    at = iota((ROWS, width), 0)
    rows = []
    for layer in range(LAYERS):
        mine = table[:, ROWS * layer : ROWS * (layer + 1)]
        spread = jnp.zeros((ROWS, width), F32)
        for j in range(ROWS):
            spread = jnp.where(column == j, mine[:, j : j + 1], spread)
        rows.append(jnp.sum(jnp.where(row == at, spread, 0.0), 0, keepdims=True))
    return jnp.concatenate(rows, 0)


def adam_body(plan, place, fix_ref, *refs):
    chunks, names, extras = plan
    grads, at = [], 0
    for chunk in chunks:
        size = 2 if chunk.down is None else 3
        grads.append(refs[at : at + size])
        at += size
    flats = refs[at : at + 3 * len(names)]
    outs = refs[at + 3 * len(names) : at + 6 * len(names)]
    rest = refs[at + 6 * len(names) :]
    extra = dict(zip(extras, rest))
    work = dict(zip(names, rest[len(extras) :]))

    def run(b):
        for chunk, parts in zip(chunks, grads):
            sides = (parts[0], parts[1]) if b == 0 else (parts[1], parts[0])
            for which in range(2):
                for name, column, first, width in chunk.pieces(which):
                    span = slice(first, first + width)
                    if name in extra:
                        out = extra[name]
                        out[:, column : column + width] = sides[which][
                            0 : out.shape[0], span
                        ].astype(out.dtype)
                    elif name == "small" and name in work:
                        work[name][:, column : column + width] = sides[which][:, span]
                    elif name[:-1] in work:
                        full, layer = FLAT[name[:-1]], int(name[-1])
                        for r in range(ROWS):
                            to = r * full + column
                            work[name[:-1]][layer : layer + 1, to : to + width] = sides[which][
                                r : r + 1, span
                            ]
            if chunk.down is not None and "down" in work:
                layer = chunk.down
                for r in range(2 * PAIR):
                    first = (r // PAIR) * D
                    work["down"][layer : layer + 1, r * D : (r + 1) * D] = parts[2][
                        r % PAIR : r % PAIR + 1, first : first + D
                    ]

    by_core(place, run)
    for i, name in enumerate(names):
        new = adam_math(
            fix_ref[0],
            flats[3 * i][...],
            flats[3 * i + 1][...],
            flats[3 * i + 2][...],
            small_flat(work[name][...]) if name == "small" else work[name][...],
            rate_small if name == "small" else rate_matrix,
            0.0 if name == "small" else decay_matrix,
        )
        for k in range(3):
            outs[3 * i + k][...] = new[k]


class Step:
    def __init__(self, crop_devices, dp_devices, arguments):
        (
            self.patches,
            self.kept_index,
            self.lengths,
            self.source_order,
            self.cot_tokens,
            self.cot_cls,
            step_count,
        ) = arguments[:7]
        self.masters, self.firsts, self.seconds = arguments[7:12], arguments[12:17], arguments[17:22]
        self.crop_count, self.patch_count = self.patches.shape[:2]
        self.half = self.crop_count // 2
        self.dp_devices = dp_devices
        me = lax.axis_index(AXES)
        self.place = jnp.stack([me, me // dp_devices]).astype(jnp.int32)
        self.swap = functools.partial(lax.ppermute, axis_name="crop", perm=[(0, 1), (1, 0)])
        self.crops_half = sds((self.half, SLOTS, D), BF16)
        self.rows = (self.half + 1) * SLOTS
        self.fix = (1.0 - jnp.power(0.5, step_count[0].astype(F32))).reshape(1)

    def tokens(self):
        positions = jnp.arange(SLOTS, dtype=jnp.int32)[None, :]
        rest = SLOTS - self.kept_index.shape[1] - 1
        slots = jnp.pad(self.kept_index, ((0, 0), (1, rest)), constant_values=-1)
        self.slots = jnp.where(positions <= self.lengths[:, None], slots + 1, -1)
        return call(
            functools.partial(tokens_body, self.half, self.patch_count),
            [self.crops_half] * 2,
        )(self.place, self.patches, self.slots)

    def arrange(self, keep, recv):
        return call(
            functools.partial(arrange_body, self.half),
            [
                sds((self.rows, D), F32),
                sds((self.half + 1, SLOTS, 2 * SLOTS), F32),
                sds((2 * self.half, 128), F32),
            ],
        )(self.place, keep, recv)

    def first_ids(self, place):
        views = self.crop_count * (place[0] - place[1] * self.dp_devices) + self.half * place[1]
        return views, views + self.crop_count * self.dp_devices

    def cot_send(self):
        start, count = self.half * (1 - self.place[1]), self.half // 2
        return [
            lax.dynamic_slice_in_dim(self.cot_tokens, start + i * count, count, 0) for i in range(2)
        ]

    def turn(self, x, lens, cot_a, cot_b, order, every_cot):
        shapes = [self.crops_half] * 2 + [sds((self.rows, D), F32), sds(every_cot.shape, F32)]
        return call(functools.partial(turn_body, self.half, self.first_ids), shapes)(
            self.place, x, lens, self.cot_tokens, cot_a, cot_b, order, every_cot
        )

    def split(self, x):
        return call(functools.partial(split_body, self.half), [self.crops_half] * 2)(self.place, x)

    def join(self, keep, recv):
        return call(
            functools.partial(join_body, self.half), sds((self.crop_count, SLOTS, D), BF16)
        )(self.place, keep, recv)

    def scatter(self, keep, recv):
        stride = -(-self.patch_count // 8) * 8
        out = call(
            functools.partial(scatter_body, self.half, self.patch_count),
            sds((self.patch_count, self.crop_count, D), F32),
            scratch=[pltpu.VMEM((self.crop_count * stride, 128), F32)] * (D // 128),
        )(self.place, keep, recv, self.slots)
        return jnp.transpose(out, (1, 0, 2))

    def adam_flat(self, kind, grad):
        return adam_math(
            self.fix[0],
            self.masters[kind],
            self.firsts[kind],
            self.seconds[kind],
            grad,
            rate_small if kind == 4 else rate_matrix,
            0.0 if kind == 4 else decay_matrix,
        )

    def adam_rows(self, fix, chunks, names, kinds, parts, extras, small=False):
        names, kinds = names + ["small"] * small, kinds + [4] * small
        flats = [f[kind] for kind in kinds for f in (self.masters, self.firsts, self.seconds)]
        shapes = [sds(f.shape, F32) for f in flats] + [shape for _, shape in extras]
        plan = (chunks, names, [name for name, _ in extras])
        out = call(
            functools.partial(adam_body, plan),
            shapes,
            scratch=[
                pltpu.VMEM((ROWS, SMALL) if name == "small" else flats[3 * i].shape, F32)
                for i, name in enumerate(names)
            ],
            smem=2,
        )(self.place, fix, *[a for part in parts for a in part], *flats)
        return [list(out[3 * i : 3 * i + 3]) for i in range(len(kinds))], out[3 * len(kinds) :]


def outputs(block_out, cls_grouped, patch_grad, results):
    return (block_out, cls_grouped, patch_grad) + tuple(
        results[kind][part] for part in range(3) for kind in range(5)
    )


def pack_call(place, operands, shapes):
    return pl.pallas_call(
        pack_body,
        in_specs=[SM] + [pl.BlockSpec(memory_space=pltpu.HBM)] * len(operands),
        out_specs=[VM] * len(shapes),
        out_shape=shapes,
        scratch_shapes=[pltpu.VMEM(a.shape, a.dtype) for a in operands]
        + [pltpu.SemaphoreType.DMA((len(operands),))],
        compiler_params=pltpu.CompilerParams(vmem_limit_bytes=VMEM_LIMIT),
        cost_estimate=NO_COST,
    )(place, *[pltpu.with_memory_space_constraint(a, pltpu.HBM) for a in operands])


def staged_step(step):
    place = step.place
    total_half = sum(c.half for c in GATHERED)
    rows_shape = sds((ROWS, total_half), F32)
    keep, send, downs = pack_call(
        place,
        step.masters[:3]
        + (step.masters[4], step.cot_cls, step.source_order[None, :], step.masters[3]),
        [rows_shape, rows_shape, sds((PAIR, 4 * D), F32)],
    )
    recv = permute(send, CORE)
    width = GATHERED[1].width
    a, b = call(
        merge_body,
        [
            sds((1, PAIR, GATHERED[0].width), BF16),
            sds((1, PAIR, width + GATHERED[2].width), BF16),
        ],
        scratch=[pltpu.VMEM((PAIR, total_half), F32)],
    )(place, keep, recv, downs)

    step.kept_index, step.patches, a = tie(step.kept_index, step.patches, a)
    a_recv = permute(a, GATHER_STAGES[0])
    tok_keep, tok_send = step.tokens()
    tok_recv = step.swap(tok_send)
    a_recv, b = tie(a_recv, b)
    a = jnp.concatenate([a, a_recv])
    a_recv = permute(a, GATHER_STAGES[1])
    a_recv, tok_recv, b = tie(a_recv, tok_recv, b)
    a = jnp.concatenate([a, a_recv])
    a_recv = permute(a, GATHER_STAGES[2])
    b_recv = permute(b, GATHER_STAGES[0])
    x, bias, lens = step.arrange(tok_keep, tok_recv)
    a_recv, b_recv, x = tie(a_recv, b_recv, x)
    a = jnp.concatenate([a, a_recv])
    b = jnp.concatenate([b, b_recv])
    a_recv = permute(a, GATHER_STAGES[3])
    b_recv = permute(b, GATHER_STAGES[1])
    a_sib = permute(a, CORE)
    cot_a, cot_b = step.cot_send()
    a, a_recv, a_sib, b_recv, cot_a, cot_b = tie(a, a_recv, a_sib, b_recv, cot_a, cot_b)
    a_sib = (a_sib, permute(a_recv, CORE))
    b = jnp.concatenate([b, b_recv])
    b_near = permute(b, GATHER_STAGES[2])
    b_side = permute(b, GATHER_STAGES[3])
    qkv0, proj0, up0, down0, small, up_bias = unpack(GATHERED[0], 0, (a, a_recv), a_sib, place)

    small0, small1 = small[0:12], small[12:24]
    norms_0, n1_0, qkv_0, att_0, prob_0, mid_0, n2_0 = layer_forward_one(
        x, bias, qkv0, proj0, small0
    )
    mid_0, n2_0, b_near = tie(mid_0, n2_0, b_near)
    b_far = permute(b_near, GATHER_STAGES[3])
    x_1, act_0, slope_0 = layer_forward_two(mid_0, n2_0, up0, down0, small0, up_bias[0:1])
    x_1, b_side, b_far = tie(x_1, b_side, b_far)
    b_own = (b, b_near, b_side, b_far)
    b_sib = tuple(permute(item, CORE) for item in b_own)
    cot_a = step.swap(cot_a)
    qkv1, proj1, every_cot, order = unpack(GATHERED[1], 0, b_own, b_sib, place)
    norms_1, n1_1, qkv_1, att_1, prob_1, mid_1, n2_1 = layer_forward_one(
        x_1, bias, qkv1, proj1, small1
    )
    mid_1, n2_1, cot_a, cot_b = tie(mid_1, n2_1, cot_a, cot_b)
    cot_b = step.swap(cot_b)
    up1, down1 = unpack(GATHERED[2], width, b_own, b_sib, place)
    final, act_1, slope_1 = layer_forward_two(mid_1, n2_1, up1, down1, small1, up_bias[1:2])
    out_keep, out_send, g, dense_cls = step.turn(final, lens, cot_a, cot_b, order, every_cot)

    def mlp_finish(layer):
        def finish(place, matrices, outs):
            arrange_sums(MLP_SUMS[layer], place, matrices, outs[0], outs[1])

        return finish

    def qkv_finish(layer):
        def finish(place, matrices, outs, rows):
            matrices = list(matrices)
            if layer == 0:
                weight, proj, rows_one1, rows_two1, up1, rows_two0, up0 = matrices
                table = outs[2]
                table[...] = jnp.zeros(table.shape, F32)
                table[:, 0:32] = small_table(((rows, rows_two0, up0), (rows_one1, rows_two1, up1)))
                matrices = [weight, proj, table]
            arrange_sums(QKV_SUMS[layer], place, matrices, outs[0], outs[1])

        return finish

    out_swap = Transfer(step.swap, out_send)
    keep, send, g_hid, bias_up1 = beside(
        [out_swap],
        lambda g: mlp_weights(
            place, mlp_finish(1), sum_shapes(MLP_SUMS[1]), g, n2_1, act_1, slope_1, down1
        ),
        g,
    )
    m1 = Reduction(MLP_SUMS[1], keep, send, place)
    g_mid, g_proj, g_att, rows_two1 = beside(
        [m1],
        lambda g_hid: mlp_rows(g, g_hid, norms_1[2], norms_1[3], att_1, up1, proj1, small1),
        g_hid,
    )
    keep, send, g_nrm, rows_one1 = beside(
        [m1],
        lambda g_att: qkv_weights(
            place, qkv_finish(1), sum_shapes(QKV_SUMS[1]), (g_proj, dense_cls),
            g_att, n1_1, qkv_1, prob_1, norms_1[0], qkv1,
        ),
        g_att,
    )
    q1 = Reduction(QKV_SUMS[1], keep, send, place)
    g = norm_one(g_nrm, norms_1[0], norms_1[1], g_mid, small1)

    keep, send, g_hid, bias_up0 = beside(
        [q1, m1],
        lambda g: mlp_weights(
            place, mlp_finish(0), sum_shapes(MLP_SUMS[0]), g, n2_0, act_0, slope_0, down0
        ),
        g,
    )
    m0 = Reduction(MLP_SUMS[0], keep, send, place)
    g_mid, g_proj, g_att, rows_two0 = beside(
        [m0, q1, m1],
        lambda g_hid: mlp_rows(g, g_hid, norms_0[2], norms_0[3], att_0, up0, proj0, small0),
        g_hid,
    )
    keep, send, _, g_nrm, _ = beside(
        [m0, q1, m1],
        lambda g_att: qkv_weights(
            place, qkv_finish(0), sum_shapes(QKV_SUMS[0]) + [sds((D, SMALL), F32)],
            (g_proj, rows_one1, rows_two1, bias_up1, rows_two0, bias_up0),
            g_att, n1_0, qkv_0, prob_0, norms_0[0], qkv0,
        ),
        g_att,
    )
    q0 = Reduction(QKV_SUMS[0], keep, send, place, direct=True)
    back_keep, back_send = beside(
        [q0, m0, q1],
        lambda g_nrm: step.split(norm_one(g_nrm, norms_0[0], norms_0[1], g_mid, small0)),
        g_nrm,
    )
    block_out = beside(
        [q0, m0, q1], lambda keep, recv: step.join(keep, recv), out_keep, out_swap.recv
    )
    back_send, q0.send = tie(back_send, q0.send)
    back_recv = step.swap(back_send)
    back_keep = beside([q0, m0, q1, m1], lambda v: v, back_keep)
    patch_grad = beside([q0, m0], lambda keep: step.scatter(keep, back_recv), back_keep)

    def adam_mlp(fix):
        new, _ = step.adam_rows(
            fix, [MLP_SUMS[1], MLP_SUMS[0]], ["up", "down"], [2, 3], [m1.result, m0.result], []
        )
        return new[0] + new[1]

    new = beside([q0], adam_mlp, step.fix)
    new_up, new_down = new[:3], new[3:]
    (new_qkv, new_proj, new_small), (cls_grouped,) = step.adam_rows(
        step.fix,
        [QKV_SUMS[1], QKV_SUMS[0]],
        ["qkv", "proj"],
        [0, 1],
        [q1.result, q0.result],
        [("cls", sds((step.crop_count, CLS), BF16))],
        small=True,
    )
    return outputs(block_out, cls_grouped, patch_grad, (new_qkv, new_proj, new_up, new_down, new_small))


def plain_step(step):
    def gather(values):
        return lax.all_gather(values, AXES, axis=0, tiled=True)

    weights, smalls, up_biases = [], [], []
    for layer in range(LAYERS):
        flat = [gather(m[layer].astype(BF16)) for m in step.masters]
        small = flat[4].reshape(D, 8 + FF // D).astype(F32)
        weights.append(
            (
                flat[0].reshape(D, QKV),
                flat[1].reshape(D, D),
                flat[2].reshape(D, FF),
                flat[3].reshape(FF, D),
            )
        )
        smalls.append(jnp.transpose(small[:, :8]))
        up_biases.append(small[:, 8:].reshape(1, FF))
    keep, send = step.tokens()
    x, bias, lens = step.arrange(keep, step.swap(send))
    saved = []
    for layer in range(LAYERS):
        qkv_w, proj_w, up_w, down_w = weights[layer]
        one = layer_forward_one(x, bias, qkv_w, proj_w, smalls[layer])
        x, active, slope = layer_forward_two(
            one[5], one[6], up_w, down_w, smalls[layer], up_biases[layer]
        )
        saved.append(one + (active, slope))
    order = gather(step.source_order).astype(F32)[None, :]
    out_keep, out_send, g, dense_cls = step.turn(
        x, lens, *[step.swap(item) for item in step.cot_send()], order, gather(step.cot_cls)
    )
    block_out = step.join(out_keep, step.swap(out_send))
    gradients = [None] * LAYERS

    def two_out(place, matrices, outs, *_):
        for value, out in zip(matrices, outs):
            out[...] = value[...]

    for layer in reversed(range(LAYERS)):
        norms, normed_one, qkv, attended, prob, _, normed_two, active, slope = saved[layer]
        qkv_w, proj_w, up_w, down_w = weights[layer]
        g_up, g_down, g_hid, bias_up = mlp_weights(
            step.place, two_out, [sds((D, FF), F32), sds((FF, D), F32)],
            g, normed_two, active, slope, down_w,
        )
        g_mid, g_proj, g_att, two = mlp_rows(
            g, g_hid, norms[2], norms[3], attended, up_w, proj_w, smalls[layer]
        )
        g_qkv_w, g_nrm, one = qkv_weights(
            step.place, two_out, [sds((D, QKV), F32)], (),
            g_att, normed_one, qkv, prob, norms[0], qkv_w,
        )
        g = norm_one(g_nrm, norms[0], norms[1], g_mid, smalls[layer])
        eight = jnp.concatenate([one[0:4], two[3:4], two[0:3]])
        table = jnp.concatenate([jnp.transpose(eight), bias_up.reshape(D, FF // D)], 1)
        gradients[layer] = (g_qkv_w, g_proj, g_up, g_down, table)
    back_keep, back_send = step.split(g)
    patch_grad = step.scatter(back_keep, step.swap(back_send))

    def scatter_sum(values):
        return lax.psum_scatter(values, AXES, scatter_dimension=0, tiled=True)

    results = []
    for kind in range(5):
        shares = [
            scatter_sum(gradients[layer][kind].reshape(-1).astype(F32)) for layer in range(LAYERS)
        ]
        results.append(step.adam_flat(kind, jnp.stack(shares)))
    cls_grouped = scatter_sum(dense_cls).astype(BF16)
    return outputs(block_out, cls_grouped, patch_grad, results)


def on_device(crop_devices, dp_devices, *arguments):
    step = Step(crop_devices, dp_devices, arguments)
    owned = step.masters[0].shape[1]
    staged = crop_devices * dp_devices == 2 * CHIPS and owned == ROWS * QKV
    if staged and step.crop_count <= ROWS:
        return staged_step(step)
    return plain_step(step)


def solution(mesh):
    crops = [P(AXES, None, None), P(AXES, None), P(AXES), P(AXES), P(AXES, None, None)]
    flat = P(None, AXES)
    return jax.shard_map(
        functools.partial(on_device, mesh.shape["crop"], mesh.shape["dp"]),
        mesh=mesh,
        in_specs=tuple(crops + [P(AXES, None), P()] + [flat] * 15),
        out_specs=(crops[0], crops[1], crops[0]) + (flat,) * 15,
        check_vma=False,
    )
```

```python
import functools

import jax
import jax.numpy as jnp
from jax import lax
from jax.experimental import pallas as pl
from jax.experimental.pallas import tpu as pltpu
from jax.sharding import PartitionSpec as P

D = 384
HEADS = 6
HEAD_DIM = 64
FF = 1536
LAYERS = 2
SLOTS = 144
FOCAL_SLOTS = 32
LEN_ROW = 143

eps_norm = 1e-06
neg_big = -1e30
adam_eps = 1e-08
rate_matrix = 0.04
decay_matrix = 0.05
rate_small = 0.4

F32 = jnp.float32
BF16 = jnp.bfloat16
VM = pl.BlockSpec(memory_space=pltpu.VMEM)
SM = pl.BlockSpec(memory_space=pltpu.SMEM)
AXES = ("crop", "dp")
VMEM_LIMIT = 12 * 1024 * 1024
NO_COST = pl.CostEstimate(flops=1, bytes_accessed=1, transcendentals=0)


def sds(shape, dtype):
    return jax.ShapeDtypeStruct(shape, dtype)


def call(body, out_shape, scratch=(), smem=1):
    def run(*operands):
        return pl.pallas_call(
            body,
            out_shape=out_shape,
            in_specs=[SM] * smem + [VM] * (len(operands) - smem),
            out_specs=jax.tree.map(lambda _: VM, out_shape),
            scratch_shapes=list(scratch),
            compiler_params=pltpu.CompilerParams(vmem_limit_bytes=VMEM_LIMIT),
            cost_estimate=NO_COST,
        )(*operands)

    return run


def iota(shape, axis):
    return lax.broadcasted_iota(jnp.int32, shape, axis)


def dot(a, b, ca, cb):
    return lax.dot_general(a, b, (((ca,), (cb,)), ((), ())), preferred_element_type=F32)


def slot_onehot(slots, c, patch_count):
    row = slots[pl.ds(c, 1), :]
    return row, (iota((patch_count, SLOTS), 0) == row).astype(F32).astype(BF16)


def tokens_body(half, patch_count, place, patches, slots, keep, send):
    y = place[1]
    row_index = iota((SLOTS, D), 0)
    for i in range(half):
        for out, c in ((keep, half * y + i), (send, half * (1 - y) + i)):
            row, onehot = slot_onehot(slots, c, patch_count)
            count = jnp.sum((row >= 0).astype(F32), axis=1, keepdims=True) - 1.0
            picked = dot(onehot, patches[c], 0, 0)
            out[i] = jnp.where(row_index == LEN_ROW, count, picked).astype(BF16)


class Halves:
    def __init__(self, first, second):
        self.parts, self.count = (first, second), first.shape[0]

    def __getitem__(self, key):
        i = key[0] if isinstance(key, tuple) else key
        rest = key[1:] if isinstance(key, tuple) else ()
        return self.parts[i // self.count][(i % self.count,) + tuple(rest)]


def arrange_body(half, place, keep, recv, x_ref, bias_ref, lens_ref):
    y = place[1]
    base = half * SLOTS
    used = half * FOCAL_SLOTS

    def run(v_src, f_src):
        k = iota((SLOTS, 2 * SLOTS), 0)
        q = iota((SLOTS, 2 * SLOTS), 1) % SLOTS
        row_index = iota((SLOTS, D), 0)
        for i in range(half):
            t = v_src[i].astype(F32)
            n = t[LEN_ROW : LEN_ROW + 1, 0:1]
            x_ref[SLOTS * i : SLOTS * (i + 1), :] = jnp.where(row_index == LEN_ROW, 0.0, t)
            bias_ref[i] = jnp.where(k.astype(F32) <= n, 0.0, neg_big)
            lens_ref[i : i + 1, :] = jnp.broadcast_to(n, (1, 128))
        limit = jnp.full((SLOTS, 2 * SLOTS), 1000.0, F32)
        for i in range(half):
            x_ref[base + FOCAL_SLOTS * i : base + FOCAL_SLOTS * (i + 1), :] = f_src[
                i, 0:FOCAL_SLOTS
            ].astype(F32)
            n = f_src[i, SLOTS - 16 : SLOTS].astype(F32)[15:16, 0:1]
            limit = jnp.where((k // FOCAL_SLOTS) == i, n, limit)
            lens_ref[half + i : half + i + 1, :] = jnp.broadcast_to(n, (1, 128))
        if used < SLOTS:
            x_ref[base + used : base + SLOTS, :] = jnp.zeros((SLOTS - used, D), F32)
        same = (q // FOCAL_SLOTS) == (k // FOCAL_SLOTS)
        inside = (k % FOCAL_SLOTS).astype(F32) <= limit
        bias_ref[half] = jnp.where(same & inside, 0.0, neg_big)

    @pl.when(y == 0)
    def _():
        run(keep, recv)

    @pl.when(y == 1)
    def _():
        run(recv, keep)


def turn_body(half, first_ids, place, x_ref, lens, cot, recv_a, recv_b, order, every_cot, *outs):
    keep, send, g_ref, dense = outs
    recv = Halves(recv_a, recv_b)
    y = place[1]
    base = half * SLOTS
    used = half * FOCAL_SLOTS
    views, focals = first_ids(place)
    index = iota((2 * half, 1), 0)
    ids = jnp.where(index < half, views + index, focals + index - half).astype(F32)
    chosen = (order[...] == ids).astype(F32).astype(BF16)
    top = dot(chosen, every_cot[...], 1, 0)

    def piece(values, n, row, rows):
        at = iota((rows, D), 0)
        masked = jnp.where(at.astype(F32) <= n, values, 0.0)
        return masked + jnp.where(at == 0, row, 0.0)

    def run(v_out, f_out, v_get, f_get):
        cls = []
        for i in range(half):
            n = lens[i : i + 1, 0:1]
            rows = slice(SLOTS * i, SLOTS * (i + 1))
            v = x_ref[rows, :]
            cls.append(v[0:1])
            v_out[i] = jnp.where(iota((SLOTS, D), 0).astype(F32) <= n, v, 0.0).astype(BF16)
            g_ref[rows, :] = piece(v_get(i).astype(F32), n, top[i : i + 1], SLOTS)
        for i in range(half):
            n = lens[half + i : half + i + 1, 0:1]
            rows = slice(base + FOCAL_SLOTS * i, base + FOCAL_SLOTS * (i + 1))
            f = x_ref[rows, :]
            cls.append(f[0:1])
            f = jnp.where(iota((FOCAL_SLOTS, D), 0).astype(F32) <= n, f, 0.0)
            f_out[i, 0:FOCAL_SLOTS] = f.astype(BF16)
            f_out[i, FOCAL_SLOTS:SLOTS] = jnp.zeros((SLOTS - FOCAL_SLOTS, D), BF16)
            g_ref[rows, :] = piece(
                f_get(i)[0:FOCAL_SLOTS].astype(F32), n, top[half + i : half + i + 1], FOCAL_SLOTS
            )
        if used < SLOTS:
            g_ref[base + used : base + SLOTS, :] = jnp.zeros((SLOTS - used, D), F32)
        dense[...] = dot(chosen, jnp.concatenate(cls, 0).astype(BF16), 0, 0)

    @pl.when(y == 0)
    def _():
        run(keep, send, lambda i: cot[i], lambda i: recv[i])

    @pl.when(y == 1)
    def _():
        run(send, keep, lambda i: recv[i], lambda i: cot[half + i])


def split_body(half, place, x_ref, keep, send):
    y = place[1]
    base = half * SLOTS

    def run(v_out, f_out):
        for i in range(half):
            v_out[i] = x_ref[SLOTS * i : SLOTS * (i + 1), :].astype(BF16)
            rows = slice(base + FOCAL_SLOTS * i, base + FOCAL_SLOTS * (i + 1))
            f_out[i, 0:FOCAL_SLOTS] = x_ref[rows, :].astype(BF16)
            f_out[i, FOCAL_SLOTS:SLOTS] = jnp.zeros((SLOTS - FOCAL_SLOTS, D), BF16)

    @pl.when(y == 0)
    def _():
        run(keep, send)

    @pl.when(y == 1)
    def _():
        run(send, keep)


def join_body(half, place, keep, recv, out):
    y = place[1]
    for i in range(half):
        out[half * y + i] = keep[i]
        out[half * (1 - y) + i] = recv[i]


def scatter_body(half, patch_count, place, keep, recv, slots, out, *work):
    y = place[1]
    stride = work[0].shape[0] // (2 * half)
    for i in range(half):
        for src, c in ((keep, half * y + i), (recv, half * (1 - y) + i)):
            _, onehot = slot_onehot(slots, c, patch_count)
            first = pl.multiple_of(c * stride, 8)
            rows = dot(onehot, src[i], 1, 0)
            for t, part in enumerate(work):
                part[pl.ds(first, patch_count), :] = rows[:, 128 * t : 128 * (t + 1)]

    def copy(p):
        for t, part in enumerate(work):
            out[p, :, 128 * t : 128 * (t + 1)] = part[pl.ds(p, 2 * half, stride=stride), :]

    group = 8

    def step(i, _):
        for j in range(group):
            copy(i * group + j)
        return 0

    lax.fori_loop(0, patch_count // group, step, 0)
    for p in range(patch_count // group * group, patch_count):
        copy(p)


def lane_mask(second, value):
    lane = iota((1, 128), 1)
    chosen = (lane >= HEAD_DIM) if second else (lane < HEAD_DIM)
    return jnp.where(chosen, value, 0.0).astype(BF16)


def pair_rows(values, scale):
    return jnp.concatenate([values * lane_mask(0, scale), values * lane_mask(1, scale)], 0)


def pair_lanes(values):
    own = iota((SLOTS, 128), 1) < HEAD_DIM
    return jnp.where(own, values[:SLOTS], values[SLOTS:])


def heads_at(part, pair):
    return slice(part * D + 128 * pair, part * D + 128 * (pair + 1))


PAIRS = HEADS // 2
HEAD_SCALE = HEAD_DIM**-0.5


def block_rows(b):
    return slice(b * SLOTS, (b + 1) * SLOTS)


def attend_scores(qkv, bias, prob, r, b):
    for i in range(PAIRS):
        queries = pair_rows(qkv[r, heads_at(0, i)], HEAD_SCALE)
        s = dot(qkv[r, heads_at(1, i)], queries, 1, 1) + bias
        e = jnp.exp(s - jnp.max(s, 0, keepdims=True))
        prob[b, i] = (e * (1.0 / jnp.sum(e, 0, keepdims=True))).astype(BF16)


def attend_values(qkv, attended, prob, r, b):
    for i in range(PAIRS):
        out = dot(prob[b, i], qkv[r, heads_at(2, i)], 0, 0)
        attended[r, heads_at(0, i)] = pair_lanes(out).astype(BF16)


def attend_backward_block(qkv, prob, grad, out, r, b):
    grads = [pair_rows(grad[r, heads_at(0, i)], 1.0) for i in range(PAIRS)]
    inner = [dot(qkv[r, heads_at(2, i)], grads[i], 1, 1) for i in range(PAIRS)]
    for i in range(PAIRS):
        out[r, heads_at(2, i)] = dot(prob[b, i], grads[i], 1, 0).astype(BF16)
    scores = []
    for i in range(PAIRS):
        p = prob[b, i].astype(F32)
        t = p * inner[i]
        scores.append((t - p * jnp.sum(t, 0, keepdims=True)).astype(BF16))
    for i in range(PAIRS):
        queries = pair_rows(qkv[r, heads_at(0, i)], HEAD_SCALE)
        out[r, heads_at(1, i)] = dot(scores[i], queries, 1, 0).astype(BF16)
    for i in range(PAIRS):
        back = pair_lanes(dot(scores[i], qkv[r, heads_at(1, i)], 0, 0))
        out[r, heads_at(0, i)] = (back * HEAD_SCALE).astype(BF16)


def total(values):
    return jnp.sum(values, 0, keepdims=True)


def normalized(values):
    centered = values - jnp.mean(values, -1, keepdims=True)
    scale = lax.rsqrt(jnp.mean(centered * centered, -1, keepdims=True) + eps_norm)
    return centered * scale, scale


def gelu_parts(v):
    c = 0.7978845608028654
    a = 0.044715
    square = v * v
    t = jnp.tanh(v * (c + (c * a) * square))
    h = 0.5 * v
    ht = h * t
    return h + ht, 0.5 * (1.0 + t) + (h - ht * t) * (c + (3.0 * a * c) * square)


def attention_body(x, bias, qkv_w, proj_w, small, *outs):
    unit_one, scale_one, unit_two, scale_two, normed_one, qkv, attended, prob, mid, normed_two = outs
    count = x.shape[0] // SLOTS

    def norm(values, unit_ref, scale_ref, normed_ref, first):
        unit, scale = normalized(values)
        unit_ref[...] = unit.astype(BF16)
        scale_ref[...] = scale
        normed_ref[...] = (unit * small[first : first + 1] + small[first + 1 : first + 2]).astype(
            BF16
        )

    norm(x[...], unit_one, scale_one, normed_one, 0)
    for c in range(3):
        w = slice(c * D, (c + 1) * D)
        part = dot(normed_one[...], qkv_w[:, w], 1, 0)
        if c != 1:
            part = part + small[2 + c // 2 : 3 + c // 2]
        qkv[:, w] = part.astype(BF16)
    for b in range(count + 1):
        if b < count:
            attend_scores(qkv, bias[b], prob, block_rows(b), b)
        if b > 0:
            attend_values(qkv, attended, prob, block_rows(b - 1), b - 1)
    whole = x[...] + dot(attended[...], proj_w[...], 1, 0) + small[4:5]
    mid[...] = whole
    norm(whole, unit_two, scale_two, normed_two, 5)


def layer_forward_one(x, bias, qkv_w, proj_w, small):
    rows = x.shape[0]
    row = sds((rows, D), BF16)
    scale = sds((rows, 1), F32)
    out = call(
        attention_body,
        [
            row, scale, row, scale, row, sds((rows, 3 * D), BF16), row,
            sds((rows // SLOTS, PAIRS, SLOTS, 2 * SLOTS), BF16), sds((rows, D), F32), row,
        ],
        smem=0,
    )(x, bias, qkv_w, proj_w, small)
    return (tuple(out[:4]),) + tuple(out[4:])


def feed_forward_body(mid, normed, up_w, down_w, small, up_bias, out, active, slope):
    for c in range(FF // 256):
        w = slice(c * 256, (c + 1) * 256)
        value, derivative = gelu_parts(dot(normed[...], up_w[:, w], 1, 0) + up_bias[:, w])
        active[:, w] = value.astype(BF16)
        slope[:, w] = derivative.astype(BF16)
    out[...] = dot(active[...], down_w[...], 1, 0) + mid[...] + small[7:8]


def layer_forward_two(mid, normed_two, up_w, down_w, small, up_bias):
    rows = mid.shape[0]
    return call(
        feed_forward_body,
        [sds((rows, D), F32), sds((rows, FF), BF16), sds((rows, FF), BF16)],
        smem=0,
    )(mid, normed_two, up_w, down_w, small, up_bias)


def norm_back(grad, unit, scale, gain):
    inner = grad * gain
    mean, along = jnp.mean(inner, -1, keepdims=True), jnp.mean(inner * unit, -1, keepdims=True)
    return scale * (inner - mean - unit * along)


def mlp_weights_body(finish, place, g, normed, active, slope, down_w, *refs):
    outs, (branch, up, down) = refs[:-3], refs[-3:]
    g_hidden, bias_up = outs[-2:]
    branch[...] = g[...].astype(BF16)
    for c in range(FF // D):
        w = slice(c * D, (c + 1) * D)
        t = (dot(branch[...], down_w[w, :], 1, 1) * slope[:, w].astype(F32)).astype(BF16)
        g_hidden[:, w] = t
        bias_up[:, w] = total(t.astype(F32))
    for c in range(FF // D):
        w = slice(c * D, (c + 1) * D)
        down[w, :] = dot(active[:, w], branch[...], 0, 0)
    up[...] = dot(normed[...], g_hidden[...], 0, 0)
    finish(place, (up, down), outs[:-2])


def mlp_rows_body(g, g_hidden, unit, scale, attended, up_w, proj_w, small, g_mid, g_proj, g_att, rows, work):
    grad = dot(g_hidden[...], up_w[...], 1, 1)
    along = unit[...].astype(F32)
    rows[...] = jnp.zeros(rows.shape, F32)
    rows[0:1] = total(grad * along)
    rows[1:2] = total(grad)
    rows[2:3] = total(g[...].astype(BF16).astype(F32))
    whole = norm_back(grad, along, scale[...], small[5:6]) + g[...]
    g_mid[...] = whole
    work[...] = whole.astype(BF16)
    rows[3:4] = total(work[...].astype(F32))
    g_att[...] = dot(work[...], proj_w[...], 1, 1).astype(BF16)
    g_proj[...] = dot(attended[...], work[...], 0, 0)


def qkv_weights_body(finish, extra_count, place, g_att, normed, qkv, prob, unit, qkv_w, *refs):
    extra, outs, (g_qkv, weight) = refs[:extra_count], refs[extra_count:-2], refs[-2:]
    g_normed, rows = outs[-2:]
    for b in range(unit.shape[0] // SLOTS):
        attend_backward_block(qkv, prob, g_att, g_qkv, block_rows(b), b)
    grad = dot(g_qkv[...], qkv_w[...], 1, 1)
    g_normed[...] = grad
    rows[...] = jnp.zeros(rows.shape, F32)
    rows[0:1] = total(grad * unit[...].astype(F32))
    rows[1:2] = total(grad)
    rows[2:3] = total(g_qkv[:, 0:D].astype(F32))
    rows[3:4] = total(g_qkv[:, 2 * D : 3 * D].astype(F32))
    weight[...] = dot(normed[...], g_qkv[...], 0, 0)
    finish(place, (weight,) + extra, outs[:-2], rows)


def norm_one_body(g_normed, unit, scale, g_mid, small, out):
    back = norm_back(g_normed[...], unit[...].astype(F32), scale[...], small[0:1])
    out[...] = back + g_mid[...]


def mlp_weights(place, finish, shapes, g, normed, active, slope, down_w):
    rows = g.shape[0]
    return call(
        functools.partial(mlp_weights_body, finish),
        list(shapes) + [sds((rows, FF), BF16), sds((1, FF), F32)],
        scratch=[
            pltpu.VMEM((rows, D), BF16),
            pltpu.VMEM((D, FF), F32),
            pltpu.VMEM((FF, D), F32),
        ],
    )(place, g, normed, active, slope, down_w)


def mlp_rows(g, g_hidden, unit, scale, attended, up_w, proj_w, small):
    rows = g.shape[0]
    return call(
        mlp_rows_body,
        [sds((rows, D), F32), sds((D, D), F32), sds((rows, D), BF16), sds((8, D), F32)],
        scratch=[pltpu.VMEM((rows, D), BF16)],
        smem=0,
    )(g, g_hidden, unit, scale, attended, up_w, proj_w, small)


def qkv_weights(place, finish, shapes, extra, g_att, normed, qkv, prob, unit, qkv_w):
    rows = unit.shape[0]
    return call(
        functools.partial(qkv_weights_body, finish, len(extra)),
        list(shapes) + [sds((rows, D), F32), sds((8, D), F32)],
        scratch=[pltpu.VMEM((rows, 3 * D), BF16), pltpu.VMEM((D, 3 * D), F32)],
    )(place, g_att, normed, qkv, prob, unit, qkv_w, *extra)


def norm_one(g_normed, unit, scale, g_mid, small):
    return call(norm_one_body, sds(g_mid.shape, F32), smem=0)(g_normed, unit, scale, g_mid, small)


def small_table(groups):
    flat, wide = [], []
    lane = iota((1, FF), 1) % 4
    for rows_one, rows_two, bias_up in groups:
        flat += [rows_one[0:4, :], rows_two[3:4, :], rows_two[0:3, :], jnp.zeros((4, D), F32)]
        wide += [jnp.zeros((8, FF), F32)]
        wide += [jnp.where(lane == k, bias_up[...], 0.0) for k in range(4)]
    flat = jnp.concatenate(flat + [jnp.zeros((8, D), F32)], 0).astype(BF16)
    wide = jnp.concatenate(wide + [jnp.zeros((8, FF), F32)], 0).astype(BF16)
    same = (iota((D, D), 0) == iota((D, D), 1)).astype(F32).astype(BF16)
    spread = (iota((D, FF), 1) // 4 == iota((D, FF), 0)).astype(F32).astype(BF16)
    return dot(same, flat, 1, 1) + dot(spread, wide, 1, 1)


ROWS = 12
PAIR = 24
CHIPS = 16
QKV, PROJ, UP, SMALL, CLS, ORDER, PAD = 3 * D, D, FF, 128, D, 128, 128
CORE = (1, 1)
TABLES = ("small", "order")
GATHER_STAGES = ((4, 8), (8, 4), (2, 16), (16, 2))


class Chunk:
    def __init__(self, names, widths, down):
        self.names, self.widths, self.down = names, widths, down
        self.half = sum(widths) // 2
        self.width = self.half + (2 * D if down is not None else 0)
        self.arrays = [n for n in names if n != "pad"] + (["down"] if down is not None else [])

    def pieces(self, which):
        low, high, start, found = which * self.half, (which + 1) * self.half, 0, []
        for name, width in zip(self.names, self.widths):
            a, b = max(start, low), min(start + width, high)
            if a < b:
                found.append((name, a - start, a - low, b - a))
            start += width
        return found


GATHERED = (
    Chunk(("qkv0", "proj0", "up0", "small", "pad"), (QKV, PROJ, UP, SMALL, PAD), 0),
    Chunk(("qkv1", "proj1", "cls", "order"), (QKV, PROJ, CLS, ORDER), None),
    Chunk(("up1",), (UP,), 1),
)
MLP_SUMS = (Chunk(("up0",), (UP,), 0), Chunk(("up1",), (UP,), 1))
QKV_SUMS = (
    Chunk(("qkv0", "proj0", "small", "pad"), (QKV, PROJ, SMALL, PAD), None),
    Chunk(("qkv1", "proj1", "cls", "pad"), (QKV, PROJ, CLS, PAD), None),
)
FLAT = {"qkv": QKV, "proj": PROJ, "up": UP}


def by_core(place, run):
    for b in range(2):

        @pl.when((place[0] & 1) == b)
        def _(b=b):
            run(b)


def chip_of(place, core, bits):
    mask = 0
    for bit, stage in zip(bits, GATHER_STAGES):
        mask ^= stage[core] * bit
    return (place[0] ^ mask) >> 1


def bits_of(index, count=4):
    return [(index >> k) & 1 for k in range(count)]


def tie(*values):
    return lax.optimization_barrier(values)


def small_block(flat, layer):
    row = flat[layer : layer + 1, :].astype(BF16).astype(F32)
    width = ROWS * ROWS
    spread = jnp.where(iota((16, width), 1) // ROWS == iota((16, width), 0), row, 0.0).astype(BF16)
    at = iota((width, 128), 0) % ROWS + ROWS * layer
    chosen = (at == iota((width, 128), 1)).astype(F32).astype(BF16)
    return dot(spread, chosen, 1, 0)[0:ROWS]


def order_block(ref):
    count = ref.shape[1]
    row = ref[...].astype(F32)
    mine = iota((16, count), 0) == iota((16, count), 1)
    number = jnp.sum(jnp.where(mine, row, 0.0), 1, keepdims=True)
    number = jnp.where(iota((16, 1), 0) < count, number, -129.0)
    high = jnp.floor(number * (1.0 / 128.0))
    lane = iota((16, 128), 1)
    return jnp.where(lane == 0, high, number - 128.0 * high)[0:ROWS]


def pack_body(place, *refs):
    held, (keep, send, down_out), local, sem = refs[0:7], refs[7:10], refs[10:17], refs[17]
    copies = [
        pltpu.make_async_copy(src, dst, sem.at[i]) for i, (src, dst) in enumerate(zip(held, local))
    ]
    for copy in copies:
        copy.start()
    for copy in copies:
        copy.wait()
    source = dict(zip(("qkv", "proj", "up", "small", "cls", "order"), local))
    down = local[6]

    def run(b):
        base = 0
        for chunk in GATHERED:
            for out, which in ((keep, b), (send, 1 - b)):
                for name, column, at, width in chunk.pieces(which):
                    span = slice(base + at, base + at + width)
                    if name == "pad":
                        out[:, span] = jnp.zeros((ROWS, width), F32)
                    elif name == "small":
                        out[:, span] = small_block(source["small"], 0) + small_block(
                            source["small"], 1
                        )
                    elif name == "order":
                        out[:, span] = order_block(source["order"])
                    elif name == "cls":
                        count = source["cls"].shape[0]
                        out[:, span] = jnp.zeros((ROWS, width), F32)
                        out[0:count, span] = source["cls"][:, column : column + width].astype(F32)
                    else:
                        flat, full = source[name[:-1]], FLAT[name[:-1]]
                        for r in range(ROWS):
                            first = r * full + column
                            layer = int(name[-1])
                            out[r : r + 1, span] = flat[layer : layer + 1, first : first + width]
            base += chunk.half

    by_core(place, run)
    for layer in range(LAYERS):
        for r in range(2 * PAIR):
            first = (2 * layer + r // PAIR) * D
            down_out[r % PAIR : r % PAIR + 1, first : first + D] = down[
                layer : layer + 1, r * D : (r + 1) * D
            ]


def merge_body(place, keep, recv, down, *rest):
    outs, work = rest[:2], rest[2]

    def run(b):
        work[ROWS * b : ROWS * (b + 1), :] = keep[...]
        work[ROWS * (1 - b) : ROWS * (2 - b), :] = recv[...]

    by_core(place, run)
    source = target = 0
    for number, chunk in enumerate(GATHERED):
        out = outs[min(number, 1)]
        if number <= 1:
            target = 0
        out[0, :, target : target + chunk.half] = work[:, source : source + chunk.half].astype(BF16)
        if chunk.down is not None:
            at, first = target + chunk.half, 2 * D * chunk.down
            out[0, :, at : at + 2 * D] = down[:, first : first + 2 * D].astype(BF16)
        source, target = source + chunk.half, target + chunk.width


def unpack_body(chunk, base, pieces, place, *refs):
    own, sib, outs = refs[:pieces], refs[pieces : 2 * pieces], refs[2 * pieces :]
    low = 3 if pieces == 2 else 2
    target = dict(zip([n for n in chunk.arrays if n not in TABLES], outs))
    if "small" in chunk.names:
        rows_out, up_out, target["small"] = outs[-3:]
    if "order" in chunk.names:
        order_out, target["order"] = outs[-2:]

    def run(b):
        for which in range(2):
            source = own if which == b else sib
            for received in range(pieces):
                block = source[received]

                def step(index, _, which=which, received=received, block=block):
                    chip = chip_of(place, which, bits_of(index, low) + bits_of(received, 4 - low))
                    for name, column, at, width in chunk.pieces(which):
                        if name == "pad":
                            continue
                        values = block[index, :, base + at : base + at + width]
                        if name in TABLES:
                            values = values.astype(F32)
                        target[name][chip, :, column : column + width] = values
                    for part in range(0 if chunk.down is None else 2):
                        first = base + chunk.half + part * D
                        target["down"][chip * 4 + 2 * which + part] = block[
                            index, :, first : first + D
                        ]
                    return 0

                lax.fori_loop(0, CHIPS // pieces, step, 0)

    by_core(place, run)
    if "order" in chunk.names:
        across = jnp.transpose(target["order"][...].reshape(D, ORDER))
        order_out[...] = across[0:1] * 128.0 + across[1:2]
    if "small" in chunk.names:
        across = jnp.transpose(target["small"][...].reshape(D, SMALL))
        rows_out[...] = across[0:24]
        ups = jnp.concatenate([across[8:12], across[20:24]], 0).astype(BF16)
        spread = (iota((D, FF), 1) // 4 == iota((D, FF), 0)).astype(F32).astype(BF16)
        wide = dot(ups, spread, 1, 0)
        lane = iota((1, FF), 1) % 4
        for layer in range(LAYERS):
            row = jnp.zeros((1, FF), F32)
            for k in range(4):
                row = jnp.where(lane == k, wide[4 * layer + k : 4 * layer + k + 1], row)
            up_out[layer : layer + 1, :] = row


def permute(x, masks):
    return lax.ppermute(x, AXES, [(i, i ^ masks[i & 1]) for i in range(2 * CHIPS)])


def unpack(chunk, base, pieces, sib, place):
    shapes = [
        sds((CHIPS, PAIR, width), BF16)
        for name, width in zip(chunk.names, chunk.widths)
        if name != "pad" and name not in TABLES
    ]
    if chunk.down is not None:
        shapes.append(sds((4 * CHIPS, PAIR, D), BF16))
    count, scratch = len(shapes), []
    if "small" in chunk.names:
        shapes += [sds((24, D), F32), sds((LAYERS, FF), F32)]
        scratch = [pltpu.VMEM((CHIPS, PAIR, SMALL), F32)]
    if "order" in chunk.names:
        shapes += [sds((1, D), F32)]
        scratch = [pltpu.VMEM((CHIPS, PAIR, ORDER), F32)]
    out = call(functools.partial(unpack_body, chunk, base, len(pieces)), shapes, scratch=scratch)(
        place, *pieces, *sib
    )
    return [b.reshape(-1, b.shape[2]) for b in out[:count]] + list(out[count:])


def arrange_sums(chunk, place, matrices, keep, send):
    source = dict(zip(chunk.arrays, matrices))

    def run(b):
        for out, which in ((keep, b), (send, 1 - b)):

            def step(index, _, out=out, which=which):
                chip = chip_of(place, which, bits_of(index))
                rows = pl.ds(pl.multiple_of(chip * PAIR, 8), PAIR)
                for name, column, at, width in chunk.pieces(which):
                    if name == "pad":
                        out[index, :, at : at + width] = jnp.zeros((PAIR, width), BF16)
                    else:
                        out[index, :, at : at + width] = source[name][
                            rows, column : column + width
                        ].astype(BF16)
                for part in range(0 if chunk.down is None else 2):
                    at = chunk.half + part * D
                    first = pl.multiple_of((chip * 4 + 2 * which + part) * PAIR, 8)
                    out[index, :, at : at + D] = source["down"][pl.ds(first, PAIR), :].astype(BF16)
                return 0

            lax.fori_loop(0, CHIPS, step, 0)

    by_core(place, run)


def sum_shapes(chunk):
    return [sds((CHIPS, PAIR, chunk.width), BF16)] * 2


def split_rows_body(chunk, place, own, recv, keep, send, *down_out):
    def run(b):
        whole = own[...] + recv[...].astype(F32)
        for out, core in ((keep, b), (send, 1 - b)):
            out[...] = whole[ROWS * core : ROWS * (core + 1), : chunk.half]
        if chunk.down is not None:
            down_out[0][...] = whole[:, chunk.half :]

    by_core(place, run)


class Reduction:
    def __init__(self, chunk, keep, send, place, direct=False):
        self.chunk, self.place, self.stage = chunk, place, 0
        self.keep, self.send = keep, [send]
        z_one, z_two, near, far = GATHER_STAGES
        across = [[near, far, (near[0] ^ far[0],) * 2]] if direct else [[far], [near]]
        self.routes = [[CORE]] + across + [[z_two], [z_one], [CORE]]

    def move(self):
        self.stage += 1
        return [permute(s, mask) for s, mask in zip(self.send, self.routes[self.stage - 1])]

    def absorb(self, received):
        if self.stage == len(self.routes):
            self.result = (self.keep, received[0]) + tuple(self.rest)
            return
        if self.stage == len(self.routes) - 1:
            chunk = self.chunk
            shapes = [sds((ROWS, chunk.half), F32)] * 2
            if chunk.down is not None:
                shapes.append(sds((PAIR, 2 * D), F32))
            self.keep, send, *self.rest = call(functools.partial(split_rows_body, chunk), shapes)(
                self.place, self.keep[0], received[0][0]
            )
            self.send = [send]
            return
        parts = len(self.routes[self.stage]) + 1
        count = self.keep.shape[0] // parts

        def part(i):
            span = slice(i * count, (i + 1) * count)
            return sum([r[span].astype(F32) for r in received], self.keep[span].astype(F32))

        self.send = [part(i).astype(BF16) for i in range(1, parts)]
        self.keep = part(0)


class Transfer:
    def __init__(self, swap, send):
        self.swap, self.send = swap, [send]

    def move(self):
        return [self.swap(self.send[0])]

    def absorb(self, received):
        self.recv = received[0]


def beside(moving, run, *inputs):
    sends, inputs = lax.optimization_barrier(([m.send for m in moving], inputs))
    for m, send in zip(moving, sends):
        m.send = send
    received = [m.move() for m in moving]
    received, out = lax.optimization_barrier((received, run(*inputs)))
    for m, got in zip(moving, received):
        m.absorb(got)
    return out


def adam_math(fix, master, first, second, grad, rate, decay):
    moment = 0.5 * first + 0.5 * grad
    square = 0.5 * second + 0.5 * grad * grad
    update = moment / fix / (jnp.sqrt(square / fix) + adam_eps) + decay * master
    return master - rate * update, moment, square


def small_flat(table):
    width = ROWS * ROWS
    row, column = iota((ROWS, width), 1) // ROWS, iota((ROWS, width), 1) % ROWS
    at = iota((ROWS, width), 0)
    rows = []
    for layer in range(LAYERS):
        mine = table[:, ROWS * layer : ROWS * (layer + 1)]
        spread = jnp.zeros((ROWS, width), F32)
        for j in range(ROWS):
            spread = jnp.where(column == j, mine[:, j : j + 1], spread)
        rows.append(jnp.sum(jnp.where(row == at, spread, 0.0), 0, keepdims=True))
    return jnp.concatenate(rows, 0)


def adam_body(plan, place, fix_ref, *refs):
    chunks, names, extras = plan
    grads, at = [], 0
    for chunk in chunks:
        size = 2 if chunk.down is None else 3
        grads.append(refs[at : at + size])
        at += size
    flats = refs[at : at + 3 * len(names)]
    outs = refs[at + 3 * len(names) : at + 6 * len(names)]
    rest = refs[at + 6 * len(names) :]
    extra = dict(zip(extras, rest))
    work = dict(zip(names, rest[len(extras) :]))

    def run(b):
        for chunk, parts in zip(chunks, grads):
            sides = (parts[0], parts[1]) if b == 0 else (parts[1], parts[0])
            for which in range(2):
                for name, column, first, width in chunk.pieces(which):
                    span = slice(first, first + width)
                    if name in extra:
                        out = extra[name]
                        out[:, column : column + width] = sides[which][
                            0 : out.shape[0], span
                        ].astype(out.dtype)
                    elif name == "small" and name in work:
                        work[name][:, column : column + width] = sides[which][:, span]
                    elif name[:-1] in work:
                        full, layer = FLAT[name[:-1]], int(name[-1])
                        for r in range(ROWS):
                            to = r * full + column
                            work[name[:-1]][layer : layer + 1, to : to + width] = sides[which][
                                r : r + 1, span
                            ]
            if chunk.down is not None and "down" in work:
                layer = chunk.down
                for r in range(2 * PAIR):
                    first = (r // PAIR) * D
                    work["down"][layer : layer + 1, r * D : (r + 1) * D] = parts[2][
                        r % PAIR : r % PAIR + 1, first : first + D
                    ]

    by_core(place, run)
    for i, name in enumerate(names):
        new = adam_math(
            fix_ref[0],
            flats[3 * i][...],
            flats[3 * i + 1][...],
            flats[3 * i + 2][...],
            small_flat(work[name][...]) if name == "small" else work[name][...],
            rate_small if name == "small" else rate_matrix,
            0.0 if name == "small" else decay_matrix,
        )
        for k in range(3):
            outs[3 * i + k][...] = new[k]


class Step:
    def __init__(self, crop_devices, dp_devices, arguments):
        (
            self.patches,
            self.kept_index,
            self.lengths,
            self.source_order,
            self.cot_tokens,
            self.cot_cls,
            step_count,
        ) = arguments[:7]
        self.masters, self.firsts, self.seconds = arguments[7:12], arguments[12:17], arguments[17:22]
        self.crop_count, self.patch_count = self.patches.shape[:2]
        self.half = self.crop_count // 2
        self.dp_devices = dp_devices
        me = lax.axis_index(AXES)
        self.place = jnp.stack([me, me // dp_devices]).astype(jnp.int32)
        self.swap = functools.partial(lax.ppermute, axis_name="crop", perm=[(0, 1), (1, 0)])
        self.crops_half = sds((self.half, SLOTS, D), BF16)
        self.rows = (self.half + 1) * SLOTS
        self.fix = (1.0 - jnp.power(0.5, step_count[0].astype(F32))).reshape(1)

    def tokens(self):
        positions = jnp.arange(SLOTS, dtype=jnp.int32)[None, :]
        rest = SLOTS - self.kept_index.shape[1] - 1
        slots = jnp.pad(self.kept_index, ((0, 0), (1, rest)), constant_values=-1)
        self.slots = jnp.where(positions <= self.lengths[:, None], slots + 1, -1)
        return call(
            functools.partial(tokens_body, self.half, self.patch_count),
            [self.crops_half] * 2,
        )(self.place, self.patches, self.slots)

    def arrange(self, keep, recv):
        return call(
            functools.partial(arrange_body, self.half),
            [
                sds((self.rows, D), F32),
                sds((self.half + 1, SLOTS, 2 * SLOTS), F32),
                sds((2 * self.half, 128), F32),
            ],
        )(self.place, keep, recv)

    def first_ids(self, place):
        views = self.crop_count * (place[0] - place[1] * self.dp_devices) + self.half * place[1]
        return views, views + self.crop_count * self.dp_devices

    def cot_send(self):
        start, count = self.half * (1 - self.place[1]), self.half // 2
        return [
            lax.dynamic_slice_in_dim(self.cot_tokens, start + i * count, count, 0) for i in range(2)
        ]

    def turn(self, x, lens, cot_a, cot_b, order, every_cot):
        shapes = [self.crops_half] * 2 + [sds((self.rows, D), F32), sds(every_cot.shape, F32)]
        return call(functools.partial(turn_body, self.half, self.first_ids), shapes)(
            self.place, x, lens, self.cot_tokens, cot_a, cot_b, order, every_cot
        )

    def split(self, x):
        return call(functools.partial(split_body, self.half), [self.crops_half] * 2)(self.place, x)

    def join(self, keep, recv):
        return call(
            functools.partial(join_body, self.half), sds((self.crop_count, SLOTS, D), BF16)
        )(self.place, keep, recv)

    def scatter(self, keep, recv):
        stride = -(-self.patch_count // 8) * 8
        out = call(
            functools.partial(scatter_body, self.half, self.patch_count),
            sds((self.patch_count, self.crop_count, D), F32),
            scratch=[pltpu.VMEM((self.crop_count * stride, 128), F32)] * (D // 128),
        )(self.place, keep, recv, self.slots)
        return jnp.transpose(out, (1, 0, 2))

    def adam_flat(self, kind, grad):
        return adam_math(
            self.fix[0],
            self.masters[kind],
            self.firsts[kind],
            self.seconds[kind],
            grad,
            rate_small if kind == 4 else rate_matrix,
            0.0 if kind == 4 else decay_matrix,
        )

    def adam_rows(self, fix, chunks, names, kinds, parts, extras, small=False):
        names, kinds = names + ["small"] * small, kinds + [4] * small
        flats = [f[kind] for kind in kinds for f in (self.masters, self.firsts, self.seconds)]
        shapes = [sds(f.shape, F32) for f in flats] + [shape for _, shape in extras]
        plan = (chunks, names, [name for name, _ in extras])
        out = call(
            functools.partial(adam_body, plan),
            shapes,
            scratch=[
                pltpu.VMEM((ROWS, SMALL) if name == "small" else flats[3 * i].shape, F32)
                for i, name in enumerate(names)
            ],
            smem=2,
        )(self.place, fix, *[a for part in parts for a in part], *flats)
        return [list(out[3 * i : 3 * i + 3]) for i in range(len(kinds))], out[3 * len(kinds) :]


def outputs(block_out, cls_grouped, patch_grad, results):
    return (block_out, cls_grouped, patch_grad) + tuple(
        results[kind][part] for part in range(3) for kind in range(5)
    )


def pack_call(place, operands, shapes):
    return pl.pallas_call(
        pack_body,
        in_specs=[SM] + [pl.BlockSpec(memory_space=pltpu.HBM)] * len(operands),
        out_specs=[VM] * len(shapes),
        out_shape=shapes,
        scratch_shapes=[pltpu.VMEM(a.shape, a.dtype) for a in operands]
        + [pltpu.SemaphoreType.DMA((len(operands),))],
        compiler_params=pltpu.CompilerParams(vmem_limit_bytes=VMEM_LIMIT),
        cost_estimate=NO_COST,
    )(place, *[pltpu.with_memory_space_constraint(a, pltpu.HBM) for a in operands])


def staged_step(step):
    place = step.place
    total_half = sum(c.half for c in GATHERED)
    rows_shape = sds((ROWS, total_half), F32)
    keep, send, downs = pack_call(
        place,
        step.masters[:3]
        + (step.masters[4], step.cot_cls, step.source_order[None, :], step.masters[3]),
        [rows_shape, rows_shape, sds((PAIR, 4 * D), F32)],
    )
    recv = permute(send, CORE)
    width = GATHERED[1].width
    a, b = call(
        merge_body,
        [
            sds((1, PAIR, GATHERED[0].width), BF16),
            sds((1, PAIR, width + GATHERED[2].width), BF16),
        ],
        scratch=[pltpu.VMEM((PAIR, total_half), F32)],
    )(place, keep, recv, downs)

    step.kept_index, step.patches, a = tie(step.kept_index, step.patches, a)
    a_recv = permute(a, GATHER_STAGES[0])
    tok_keep, tok_send = step.tokens()
    tok_recv = step.swap(tok_send)
    a_recv, b = tie(a_recv, b)
    a = jnp.concatenate([a, a_recv])
    a_recv = permute(a, GATHER_STAGES[1])
    a_recv, tok_recv, b = tie(a_recv, tok_recv, b)
    a = jnp.concatenate([a, a_recv])
    a_recv = permute(a, GATHER_STAGES[2])
    b_recv = permute(b, GATHER_STAGES[0])
    x, bias, lens = step.arrange(tok_keep, tok_recv)
    a_recv, b_recv, x = tie(a_recv, b_recv, x)
    a = jnp.concatenate([a, a_recv])
    b = jnp.concatenate([b, b_recv])
    a_recv = permute(a, GATHER_STAGES[3])
    b_recv = permute(b, GATHER_STAGES[1])
    a_sib = permute(a, CORE)
    cot_a, cot_b = step.cot_send()
    a, a_recv, a_sib, b_recv, cot_a, cot_b = tie(a, a_recv, a_sib, b_recv, cot_a, cot_b)
    a_sib = (a_sib, permute(a_recv, CORE))
    b = jnp.concatenate([b, b_recv])
    b_near = permute(b, GATHER_STAGES[2])
    b_side = permute(b, GATHER_STAGES[3])
    qkv0, proj0, up0, down0, small, up_bias = unpack(GATHERED[0], 0, (a, a_recv), a_sib, place)

    small0, small1 = small[0:12], small[12:24]
    norms_0, n1_0, qkv_0, att_0, prob_0, mid_0, n2_0 = layer_forward_one(
        x, bias, qkv0, proj0, small0
    )
    mid_0, n2_0, b_near = tie(mid_0, n2_0, b_near)
    b_far = permute(b_near, GATHER_STAGES[3])
    x_1, act_0, slope_0 = layer_forward_two(mid_0, n2_0, up0, down0, small0, up_bias[0:1])
    x_1, b_side, b_far = tie(x_1, b_side, b_far)
    b_own = (b, b_near, b_side, b_far)
    b_sib = tuple(permute(item, CORE) for item in b_own)
    cot_a = step.swap(cot_a)
    qkv1, proj1, every_cot, order = unpack(GATHERED[1], 0, b_own, b_sib, place)
    norms_1, n1_1, qkv_1, att_1, prob_1, mid_1, n2_1 = layer_forward_one(
        x_1, bias, qkv1, proj1, small1
    )
    mid_1, n2_1, cot_a, cot_b = tie(mid_1, n2_1, cot_a, cot_b)
    cot_b = step.swap(cot_b)
    up1, down1 = unpack(GATHERED[2], width, b_own, b_sib, place)
    final, act_1, slope_1 = layer_forward_two(mid_1, n2_1, up1, down1, small1, up_bias[1:2])
    out_keep, out_send, g, dense_cls = step.turn(final, lens, cot_a, cot_b, order, every_cot)

    def mlp_finish(layer):
        def finish(place, matrices, outs):
            arrange_sums(MLP_SUMS[layer], place, matrices, outs[0], outs[1])

        return finish

    def qkv_finish(layer):
        def finish(place, matrices, outs, rows):
            matrices = list(matrices)
            if layer == 0:
                weight, proj, rows_one1, rows_two1, up1, rows_two0, up0 = matrices
                table = outs[2]
                table[...] = jnp.zeros(table.shape, F32)
                table[:, 0:32] = small_table(((rows, rows_two0, up0), (rows_one1, rows_two1, up1)))
                matrices = [weight, proj, table]
            arrange_sums(QKV_SUMS[layer], place, matrices, outs[0], outs[1])

        return finish

    out_swap = Transfer(step.swap, out_send)
    keep, send, g_hid, bias_up1 = beside(
        [out_swap],
        lambda g: mlp_weights(
            place, mlp_finish(1), sum_shapes(MLP_SUMS[1]), g, n2_1, act_1, slope_1, down1
        ),
        g,
    )
    m1 = Reduction(MLP_SUMS[1], keep, send, place)
    g_mid, g_proj, g_att, rows_two1 = beside(
        [m1],
        lambda g_hid: mlp_rows(g, g_hid, norms_1[2], norms_1[3], att_1, up1, proj1, small1),
        g_hid,
    )
    keep, send, g_nrm, rows_one1 = beside(
        [m1],
        lambda g_att: qkv_weights(
            place, qkv_finish(1), sum_shapes(QKV_SUMS[1]), (g_proj, dense_cls),
            g_att, n1_1, qkv_1, prob_1, norms_1[0], qkv1,
        ),
        g_att,
    )
    q1 = Reduction(QKV_SUMS[1], keep, send, place)
    g = norm_one(g_nrm, norms_1[0], norms_1[1], g_mid, small1)

    keep, send, g_hid, bias_up0 = beside(
        [q1, m1],
        lambda g: mlp_weights(
            place, mlp_finish(0), sum_shapes(MLP_SUMS[0]), g, n2_0, act_0, slope_0, down0
        ),
        g,
    )
    m0 = Reduction(MLP_SUMS[0], keep, send, place)
    g_mid, g_proj, g_att, rows_two0 = beside(
        [m0, q1, m1],
        lambda g_hid: mlp_rows(g, g_hid, norms_0[2], norms_0[3], att_0, up0, proj0, small0),
        g_hid,
    )
    keep, send, _, g_nrm, _ = beside(
        [m0, q1, m1],
        lambda g_att: qkv_weights(
            place, qkv_finish(0), sum_shapes(QKV_SUMS[0]) + [sds((D, SMALL), F32)],
            (g_proj, rows_one1, rows_two1, bias_up1, rows_two0, bias_up0),
            g_att, n1_0, qkv_0, prob_0, norms_0[0], qkv0,
        ),
        g_att,
    )
    q0 = Reduction(QKV_SUMS[0], keep, send, place, direct=True)
    back_keep, back_send = beside(
        [q0, m0, q1],
        lambda g_nrm: step.split(norm_one(g_nrm, norms_0[0], norms_0[1], g_mid, small0)),
        g_nrm,
    )
    block_out = beside(
        [q0, m0, q1], lambda keep, recv: step.join(keep, recv), out_keep, out_swap.recv
    )
    back_send, q0.send = tie(back_send, q0.send)
    back_recv = step.swap(back_send)
    back_keep = beside([q0, m0, q1, m1], lambda v: v, back_keep)
    patch_grad = beside([q0, m0], lambda keep: step.scatter(keep, back_recv), back_keep)

    def adam_mlp(fix):
        new, _ = step.adam_rows(
            fix, [MLP_SUMS[1], MLP_SUMS[0]], ["up", "down"], [2, 3], [m1.result, m0.result], []
        )
        return new[0] + new[1]

    new = beside([q0], adam_mlp, step.fix)
    new_up, new_down = new[:3], new[3:]
    (new_qkv, new_proj, new_small), (cls_grouped,) = step.adam_rows(
        step.fix,
        [QKV_SUMS[1], QKV_SUMS[0]],
        ["qkv", "proj"],
        [0, 1],
        [q1.result, q0.result],
        [("cls", sds((step.crop_count, CLS), BF16))],
        small=True,
    )
    return outputs(block_out, cls_grouped, patch_grad, (new_qkv, new_proj, new_up, new_down, new_small))


def plain_step(step):
    def gather(values):
        return lax.all_gather(values, AXES, axis=0, tiled=True)

    weights, smalls, up_biases = [], [], []
    for layer in range(LAYERS):
        flat = [gather(m[layer].astype(BF16)) for m in step.masters]
        small = flat[4].reshape(D, 8 + FF // D).astype(F32)
        weights.append(
            (
                flat[0].reshape(D, QKV),
                flat[1].reshape(D, D),
                flat[2].reshape(D, FF),
                flat[3].reshape(FF, D),
            )
        )
        smalls.append(jnp.transpose(small[:, :8]))
        up_biases.append(small[:, 8:].reshape(1, FF))
    keep, send = step.tokens()
    x, bias, lens = step.arrange(keep, step.swap(send))
    saved = []
    for layer in range(LAYERS):
        qkv_w, proj_w, up_w, down_w = weights[layer]
        one = layer_forward_one(x, bias, qkv_w, proj_w, smalls[layer])
        x, active, slope = layer_forward_two(
            one[5], one[6], up_w, down_w, smalls[layer], up_biases[layer]
        )
        saved.append(one + (active, slope))
    order = gather(step.source_order).astype(F32)[None, :]
    out_keep, out_send, g, dense_cls = step.turn(
        x, lens, *[step.swap(item) for item in step.cot_send()], order, gather(step.cot_cls)
    )
    block_out = step.join(out_keep, step.swap(out_send))
    gradients = [None] * LAYERS

    def two_out(place, matrices, outs, *_):
        for value, out in zip(matrices, outs):
            out[...] = value[...]

    for layer in reversed(range(LAYERS)):
        norms, normed_one, qkv, attended, prob, _, normed_two, active, slope = saved[layer]
        qkv_w, proj_w, up_w, down_w = weights[layer]
        g_up, g_down, g_hid, bias_up = mlp_weights(
            step.place, two_out, [sds((D, FF), F32), sds((FF, D), F32)],
            g, normed_two, active, slope, down_w,
        )
        g_mid, g_proj, g_att, two = mlp_rows(
            g, g_hid, norms[2], norms[3], attended, up_w, proj_w, smalls[layer]
        )
        g_qkv_w, g_nrm, one = qkv_weights(
            step.place, two_out, [sds((D, QKV), F32)], (),
            g_att, normed_one, qkv, prob, norms[0], qkv_w,
        )
        g = norm_one(g_nrm, norms[0], norms[1], g_mid, smalls[layer])
        eight = jnp.concatenate([one[0:4], two[3:4], two[0:3]])
        table = jnp.concatenate([jnp.transpose(eight), bias_up.reshape(D, FF // D)], 1)
        gradients[layer] = (g_qkv_w, g_proj, g_up, g_down, table)
    back_keep, back_send = step.split(g)
    patch_grad = step.scatter(back_keep, step.swap(back_send))

    def scatter_sum(values):
        return lax.psum_scatter(values, AXES, scatter_dimension=0, tiled=True)

    results = []
    for kind in range(5):
        shares = [
            scatter_sum(gradients[layer][kind].reshape(-1).astype(F32)) for layer in range(LAYERS)
        ]
        results.append(step.adam_flat(kind, jnp.stack(shares)))
    cls_grouped = scatter_sum(dense_cls).astype(BF16)
    return outputs(block_out, cls_grouped, patch_grad, results)


def on_device(crop_devices, dp_devices, *arguments):
    step = Step(crop_devices, dp_devices, arguments)
    owned = step.masters[0].shape[1]
    staged = crop_devices * dp_devices == 2 * CHIPS and owned == ROWS * QKV
    if staged and step.crop_count <= ROWS:
        return staged_step(step)
    return plain_step(step)


def solution(mesh):
    crops = [P(AXES, None, None), P(AXES, None), P(AXES), P(AXES), P(AXES, None, None)]
    flat = P(None, AXES)
    return jax.shard_map(
        functools.partial(on_device, mesh.shape["crop"], mesh.shape["dp"]),
        mesh=mesh,
        in_specs=tuple(crops + [P(AXES, None), P()] + [flat] * 15),
        out_specs=(crops[0], crops[1], crops[0]) + (flat,) * 15,
        check_vma=False,
    )
```

```python
import functools

import jax
import jax.numpy as jnp
from jax import lax
from jax.experimental import pallas as pl
from jax.experimental.pallas import tpu as pltpu
from jax.sharding import PartitionSpec as P

D = 384
HEADS = 6
HEAD_DIM = 64
FF = 1536
LAYERS = 2
SLOTS = 144
FOCAL_SLOTS = 32
LEN_ROW = 143

eps_norm = 1e-06
neg_big = -1e30
adam_eps = 1e-08
rate_matrix = 0.04
decay_matrix = 0.05
rate_small = 0.4

F32 = jnp.float32
BF16 = jnp.bfloat16
VM = pl.BlockSpec(memory_space=pltpu.VMEM)
SM = pl.BlockSpec(memory_space=pltpu.SMEM)
AXES = ("crop", "dp")
VMEM_LIMIT = 12 * 1024 * 1024
NO_COST = pl.CostEstimate(flops=1, bytes_accessed=1, transcendentals=0)


def sds(shape, dtype):
    return jax.ShapeDtypeStruct(shape, dtype)


def call(body, out_shape, scratch=(), smem=1):
    def run(*operands):
        return pl.pallas_call(
            body,
            out_shape=out_shape,
            in_specs=[SM] * smem + [VM] * (len(operands) - smem),
            out_specs=jax.tree.map(lambda _: VM, out_shape),
            scratch_shapes=list(scratch),
            compiler_params=pltpu.CompilerParams(vmem_limit_bytes=VMEM_LIMIT),
            cost_estimate=NO_COST,
        )(*operands)

    return run


def iota(shape, axis):
    return lax.broadcasted_iota(jnp.int32, shape, axis)


def dot(a, b, ca, cb):
    return lax.dot_general(a, b, (((ca,), (cb,)), ((), ())), preferred_element_type=F32)


def slot_onehot(slots, c, patch_count):
    row = slots[pl.ds(c, 1), :]
    return row, (iota((patch_count, SLOTS), 0) == row).astype(F32).astype(BF16)


def tokens_body(half, patch_count, place, patches, slots, keep, send):
    y = place[1]
    row_index = iota((SLOTS, D), 0)
    for i in range(half):
        for out, c in ((keep, half * y + i), (send, half * (1 - y) + i)):
            row, onehot = slot_onehot(slots, c, patch_count)
            count = jnp.sum((row >= 0).astype(F32), axis=1, keepdims=True) - 1.0
            picked = dot(onehot, patches[c], 0, 0)
            out[i] = jnp.where(row_index == LEN_ROW, count, picked).astype(BF16)


class Halves:
    def __init__(self, first, second):
        self.parts, self.count = (first, second), first.shape[0]

    def __getitem__(self, key):
        i = key[0] if isinstance(key, tuple) else key
        rest = key[1:] if isinstance(key, tuple) else ()
        return self.parts[i // self.count][(i % self.count,) + tuple(rest)]


def arrange_body(half, place, keep, recv, x_ref, bias_ref, lens_ref):
    y = place[1]
    base = half * SLOTS
    used = half * FOCAL_SLOTS

    def run(v_src, f_src):
        k = iota((SLOTS, 2 * SLOTS), 0)
        q = iota((SLOTS, 2 * SLOTS), 1) % SLOTS
        row_index = iota((SLOTS, D), 0)
        for i in range(half):
            t = v_src[i].astype(F32)
            n = t[LEN_ROW : LEN_ROW + 1, 0:1]
            x_ref[SLOTS * i : SLOTS * (i + 1), :] = jnp.where(row_index == LEN_ROW, 0.0, t)
            bias_ref[i] = jnp.where(k.astype(F32) <= n, 0.0, neg_big)
            lens_ref[i : i + 1, :] = jnp.broadcast_to(n, (1, 128))
        limit = jnp.full((SLOTS, 2 * SLOTS), 1000.0, F32)
        for i in range(half):
            x_ref[base + FOCAL_SLOTS * i : base + FOCAL_SLOTS * (i + 1), :] = f_src[
                i, 0:FOCAL_SLOTS
            ].astype(F32)
            n = f_src[i, SLOTS - 16 : SLOTS].astype(F32)[15:16, 0:1]
            limit = jnp.where((k // FOCAL_SLOTS) == i, n, limit)
            lens_ref[half + i : half + i + 1, :] = jnp.broadcast_to(n, (1, 128))
        if used < SLOTS:
            x_ref[base + used : base + SLOTS, :] = jnp.zeros((SLOTS - used, D), F32)
        same = (q // FOCAL_SLOTS) == (k // FOCAL_SLOTS)
        inside = (k % FOCAL_SLOTS).astype(F32) <= limit
        bias_ref[half] = jnp.where(same & inside, 0.0, neg_big)

    @pl.when(y == 0)
    def _():
        run(keep, recv)

    @pl.when(y == 1)
    def _():
        run(recv, keep)


def turn_body(half, first_ids, place, x_ref, lens, cot, recv_a, recv_b, order, every_cot, *outs):
    keep, send, g_ref, dense = outs
    recv = Halves(recv_a, recv_b)
    y = place[1]
    base = half * SLOTS
    used = half * FOCAL_SLOTS
    views, focals = first_ids(place)
    index = iota((2 * half, 1), 0)
    ids = jnp.where(index < half, views + index, focals + index - half).astype(F32)
    chosen = (order[...] == ids).astype(F32).astype(BF16)
    top = dot(chosen, every_cot[...], 1, 0)

    def piece(values, n, row, rows):
        at = iota((rows, D), 0)
        masked = jnp.where(at.astype(F32) <= n, values, 0.0)
        return masked + jnp.where(at == 0, row, 0.0)

    def run(v_out, f_out, v_get, f_get):
        cls = []
        for i in range(half):
            n = lens[i : i + 1, 0:1]
            rows = slice(SLOTS * i, SLOTS * (i + 1))
            v = x_ref[rows, :]
            cls.append(v[0:1])
            v_out[i] = jnp.where(iota((SLOTS, D), 0).astype(F32) <= n, v, 0.0).astype(BF16)
            g_ref[rows, :] = piece(v_get(i).astype(F32), n, top[i : i + 1], SLOTS)
        for i in range(half):
            n = lens[half + i : half + i + 1, 0:1]
            rows = slice(base + FOCAL_SLOTS * i, base + FOCAL_SLOTS * (i + 1))
            f = x_ref[rows, :]
            cls.append(f[0:1])
            f = jnp.where(iota((FOCAL_SLOTS, D), 0).astype(F32) <= n, f, 0.0)
            f_out[i, 0:FOCAL_SLOTS] = f.astype(BF16)
            f_out[i, FOCAL_SLOTS:SLOTS] = jnp.zeros((SLOTS - FOCAL_SLOTS, D), BF16)
            g_ref[rows, :] = piece(
                f_get(i)[0:FOCAL_SLOTS].astype(F32), n, top[half + i : half + i + 1], FOCAL_SLOTS
            )
        if used < SLOTS:
            g_ref[base + used : base + SLOTS, :] = jnp.zeros((SLOTS - used, D), F32)
        dense[...] = dot(chosen, jnp.concatenate(cls, 0).astype(BF16), 0, 0)

    @pl.when(y == 0)
    def _():
        run(keep, send, lambda i: cot[i], lambda i: recv[i])

    @pl.when(y == 1)
    def _():
        run(send, keep, lambda i: recv[i], lambda i: cot[half + i])


def split_body(half, place, x_ref, keep, send):
    y = place[1]
    base = half * SLOTS

    def run(v_out, f_out):
        for i in range(half):
            v_out[i] = x_ref[SLOTS * i : SLOTS * (i + 1), :].astype(BF16)
            rows = slice(base + FOCAL_SLOTS * i, base + FOCAL_SLOTS * (i + 1))
            f_out[i, 0:FOCAL_SLOTS] = x_ref[rows, :].astype(BF16)
            f_out[i, FOCAL_SLOTS:SLOTS] = jnp.zeros((SLOTS - FOCAL_SLOTS, D), BF16)

    @pl.when(y == 0)
    def _():
        run(keep, send)

    @pl.when(y == 1)
    def _():
        run(send, keep)


def join_body(half, place, keep, recv, out):
    y = place[1]
    for i in range(half):
        out[half * y + i] = keep[i]
        out[half * (1 - y) + i] = recv[i]


def scatter_body(half, patch_count, place, keep, recv, slots, out, *work):
    y = place[1]
    stride = work[0].shape[0] // (2 * half)
    for i in range(half):
        for src, c in ((keep, half * y + i), (recv, half * (1 - y) + i)):
            _, onehot = slot_onehot(slots, c, patch_count)
            first = pl.multiple_of(c * stride, 8)
            rows = dot(onehot, src[i], 1, 0)
            for t, part in enumerate(work):
                part[pl.ds(first, patch_count), :] = rows[:, 128 * t : 128 * (t + 1)]

    def copy(p):
        for t, part in enumerate(work):
            out[p, :, 128 * t : 128 * (t + 1)] = part[pl.ds(p, 2 * half, stride=stride), :]

    group = 8

    def step(i, _):
        for j in range(group):
            copy(i * group + j)
        return 0

    lax.fori_loop(0, patch_count // group, step, 0)
    for p in range(patch_count // group * group, patch_count):
        copy(p)


def lane_mask(second, value):
    lane = iota((1, 128), 1)
    chosen = (lane >= HEAD_DIM) if second else (lane < HEAD_DIM)
    return jnp.where(chosen, value, 0.0).astype(BF16)


def pair_rows(values, scale):
    return jnp.concatenate([values * lane_mask(0, scale), values * lane_mask(1, scale)], 0)


def pair_lanes(values):
    own = iota((SLOTS, 128), 1) < HEAD_DIM
    return jnp.where(own, values[:SLOTS], values[SLOTS:])


def heads_at(part, pair):
    return slice(part * D + 128 * pair, part * D + 128 * (pair + 1))


PAIRS = HEADS // 2
HEAD_SCALE = HEAD_DIM**-0.5


def block_rows(b):
    return slice(b * SLOTS, (b + 1) * SLOTS)


def attend_scores(qkv, bias, prob, r, b):
    for i in range(PAIRS):
        queries = pair_rows(qkv[r, heads_at(0, i)], HEAD_SCALE)
        s = dot(qkv[r, heads_at(1, i)], queries, 1, 1) + bias
        e = jnp.exp(s - jnp.max(s, 0, keepdims=True))
        prob[b, i] = (e * (1.0 / jnp.sum(e, 0, keepdims=True))).astype(BF16)


def attend_values(qkv, attended, prob, r, b):
    for i in range(PAIRS):
        out = dot(prob[b, i], qkv[r, heads_at(2, i)], 0, 0)
        attended[r, heads_at(0, i)] = pair_lanes(out).astype(BF16)


def attend_backward_block(qkv, prob, grad, out, r, b):
    grads = [pair_rows(grad[r, heads_at(0, i)], 1.0) for i in range(PAIRS)]
    inner = [dot(qkv[r, heads_at(2, i)], grads[i], 1, 1) for i in range(PAIRS)]
    for i in range(PAIRS):
        out[r, heads_at(2, i)] = dot(prob[b, i], grads[i], 1, 0).astype(BF16)
    scores = []
    for i in range(PAIRS):
        p = prob[b, i].astype(F32)
        t = p * inner[i]
        scores.append((t - p * jnp.sum(t, 0, keepdims=True)).astype(BF16))
    for i in range(PAIRS):
        queries = pair_rows(qkv[r, heads_at(0, i)], HEAD_SCALE)
        out[r, heads_at(1, i)] = dot(scores[i], queries, 1, 0).astype(BF16)
    for i in range(PAIRS):
        back = pair_lanes(dot(scores[i], qkv[r, heads_at(1, i)], 0, 0))
        out[r, heads_at(0, i)] = (back * HEAD_SCALE).astype(BF16)


def total(values):
    return jnp.sum(values, 0, keepdims=True)


def normalized(values):
    centered = values - jnp.mean(values, -1, keepdims=True)
    scale = lax.rsqrt(jnp.mean(centered * centered, -1, keepdims=True) + eps_norm)
    return centered * scale, scale


def gelu_parts(v):
    c = 0.7978845608028654
    a = 0.044715
    square = v * v
    t = jnp.tanh(v * (c + (c * a) * square))
    h = 0.5 * v
    ht = h * t
    return h + ht, 0.5 * (1.0 + t) + (h - ht * t) * (c + (3.0 * a * c) * square)


def attention_body(x, bias, qkv_w, proj_w, small, *outs):
    unit_one, scale_one, unit_two, scale_two, normed_one, qkv, attended, prob, mid, normed_two = outs
    count = x.shape[0] // SLOTS

    def norm(values, unit_ref, scale_ref, normed_ref, first):
        unit, scale = normalized(values)
        unit_ref[...] = unit.astype(BF16)
        scale_ref[...] = scale
        normed_ref[...] = (unit * small[first : first + 1] + small[first + 1 : first + 2]).astype(
            BF16
        )

    norm(x[...], unit_one, scale_one, normed_one, 0)
    for c in range(3):
        w = slice(c * D, (c + 1) * D)
        part = dot(normed_one[...], qkv_w[:, w], 1, 0)
        if c != 1:
            part = part + small[2 + c // 2 : 3 + c // 2]
        qkv[:, w] = part.astype(BF16)
    for b in range(count + 1):
        if b < count:
            attend_scores(qkv, bias[b], prob, block_rows(b), b)
        if b > 0:
            attend_values(qkv, attended, prob, block_rows(b - 1), b - 1)
    whole = x[...] + dot(attended[...], proj_w[...], 1, 0) + small[4:5]
    mid[...] = whole
    norm(whole, unit_two, scale_two, normed_two, 5)


def layer_forward_one(x, bias, qkv_w, proj_w, small):
    rows = x.shape[0]
    row = sds((rows, D), BF16)
    scale = sds((rows, 1), F32)
    out = call(
        attention_body,
        [
            row, scale, row, scale, row, sds((rows, 3 * D), BF16), row,
            sds((rows // SLOTS, PAIRS, SLOTS, 2 * SLOTS), BF16), sds((rows, D), F32), row,
        ],
        smem=0,
    )(x, bias, qkv_w, proj_w, small)
    return (tuple(out[:4]),) + tuple(out[4:])


def feed_forward_body(mid, normed, up_w, down_w, small, up_bias, out, active, slope):
    for c in range(FF // 256):
        w = slice(c * 256, (c + 1) * 256)
        value, derivative = gelu_parts(dot(normed[...], up_w[:, w], 1, 0) + up_bias[:, w])
        active[:, w] = value.astype(BF16)
        slope[:, w] = derivative.astype(BF16)
    out[...] = dot(active[...], down_w[...], 1, 0) + mid[...] + small[7:8]


def layer_forward_two(mid, normed_two, up_w, down_w, small, up_bias):
    rows = mid.shape[0]
    return call(
        feed_forward_body,
        [sds((rows, D), F32), sds((rows, FF), BF16), sds((rows, FF), BF16)],
        smem=0,
    )(mid, normed_two, up_w, down_w, small, up_bias)


def norm_back(grad, unit, scale, gain):
    inner = grad * gain
    mean, along = jnp.mean(inner, -1, keepdims=True), jnp.mean(inner * unit, -1, keepdims=True)
    return scale * (inner - mean - unit * along)


def mlp_weights_body(finish, place, g, normed, active, slope, down_w, *refs):
    outs, (branch, up, down) = refs[:-3], refs[-3:]
    g_hidden, bias_up = outs[-2:]
    branch[...] = g[...].astype(BF16)
    for c in range(FF // D):
        w = slice(c * D, (c + 1) * D)
        t = (dot(branch[...], down_w[w, :], 1, 1) * slope[:, w].astype(F32)).astype(BF16)
        g_hidden[:, w] = t
        bias_up[:, w] = total(t.astype(F32))
    for c in range(FF // D):
        w = slice(c * D, (c + 1) * D)
        down[w, :] = dot(active[:, w], branch[...], 0, 0)
    up[...] = dot(normed[...], g_hidden[...], 0, 0)
    finish(place, (up, down), outs[:-2])


def mlp_rows_body(g, g_hidden, unit, scale, attended, up_w, proj_w, small, g_mid, g_proj, g_att, rows, work):
    grad = dot(g_hidden[...], up_w[...], 1, 1)
    along = unit[...].astype(F32)
    rows[...] = jnp.zeros(rows.shape, F32)
    rows[0:1] = total(grad * along)
    rows[1:2] = total(grad)
    rows[2:3] = total(g[...].astype(BF16).astype(F32))
    whole = norm_back(grad, along, scale[...], small[5:6]) + g[...]
    g_mid[...] = whole
    work[...] = whole.astype(BF16)
    rows[3:4] = total(work[...].astype(F32))
    g_att[...] = dot(work[...], proj_w[...], 1, 1).astype(BF16)
    g_proj[...] = dot(attended[...], work[...], 0, 0)


def qkv_weights_body(finish, extra_count, place, g_att, normed, qkv, prob, unit, qkv_w, *refs):
    extra, outs, (g_qkv, weight) = refs[:extra_count], refs[extra_count:-2], refs[-2:]
    g_normed, rows = outs[-2:]
    for b in range(unit.shape[0] // SLOTS):
        attend_backward_block(qkv, prob, g_att, g_qkv, block_rows(b), b)
    grad = dot(g_qkv[...], qkv_w[...], 1, 1)
    g_normed[...] = grad
    rows[...] = jnp.zeros(rows.shape, F32)
    rows[0:1] = total(grad * unit[...].astype(F32))
    rows[1:2] = total(grad)
    rows[2:3] = total(g_qkv[:, 0:D].astype(F32))
    rows[3:4] = total(g_qkv[:, 2 * D : 3 * D].astype(F32))
    weight[...] = dot(normed[...], g_qkv[...], 0, 0)
    finish(place, (weight,) + extra, outs[:-2], rows)


def norm_one_body(g_normed, unit, scale, g_mid, small, out):
    back = norm_back(g_normed[...], unit[...].astype(F32), scale[...], small[0:1])
    out[...] = back + g_mid[...]


def mlp_weights(place, finish, shapes, g, normed, active, slope, down_w):
    rows = g.shape[0]
    return call(
        functools.partial(mlp_weights_body, finish),
        list(shapes) + [sds((rows, FF), BF16), sds((1, FF), F32)],
        scratch=[
            pltpu.VMEM((rows, D), BF16),
            pltpu.VMEM((D, FF), F32),
            pltpu.VMEM((FF, D), F32),
        ],
    )(place, g, normed, active, slope, down_w)


def mlp_rows(g, g_hidden, unit, scale, attended, up_w, proj_w, small):
    rows = g.shape[0]
    return call(
        mlp_rows_body,
        [sds((rows, D), F32), sds((D, D), F32), sds((rows, D), BF16), sds((8, D), F32)],
        scratch=[pltpu.VMEM((rows, D), BF16)],
        smem=0,
    )(g, g_hidden, unit, scale, attended, up_w, proj_w, small)


def qkv_weights(place, finish, shapes, extra, g_att, normed, qkv, prob, unit, qkv_w):
    rows = unit.shape[0]
    return call(
        functools.partial(qkv_weights_body, finish, len(extra)),
        list(shapes) + [sds((rows, D), F32), sds((8, D), F32)],
        scratch=[pltpu.VMEM((rows, 3 * D), BF16), pltpu.VMEM((D, 3 * D), F32)],
    )(place, g_att, normed, qkv, prob, unit, qkv_w, *extra)


def norm_one(g_normed, unit, scale, g_mid, small):
    return call(norm_one_body, sds(g_mid.shape, F32), smem=0)(g_normed, unit, scale, g_mid, small)


def small_table(groups):
    flat, wide = [], []
    lane = iota((1, FF), 1) % 4
    for rows_one, rows_two, bias_up in groups:
        flat += [rows_one[0:4, :], rows_two[3:4, :], rows_two[0:3, :], jnp.zeros((4, D), F32)]
        wide += [jnp.zeros((8, FF), F32)]
        wide += [jnp.where(lane == k, bias_up[...], 0.0) for k in range(4)]
    flat = jnp.concatenate(flat + [jnp.zeros((8, D), F32)], 0).astype(BF16)
    wide = jnp.concatenate(wide + [jnp.zeros((8, FF), F32)], 0).astype(BF16)
    same = (iota((D, D), 0) == iota((D, D), 1)).astype(F32).astype(BF16)
    spread = (iota((D, FF), 1) // 4 == iota((D, FF), 0)).astype(F32).astype(BF16)
    return dot(same, flat, 1, 1) + dot(spread, wide, 1, 1)


ROWS = 12
PAIR = 24
CHIPS = 16
QKV, PROJ, UP, SMALL, CLS, ORDER, PAD = 3 * D, D, FF, 128, D, 128, 128
CORE = (1, 1)
TABLES = ("small", "order")
GATHER_STAGES = ((4, 8), (8, 4), (2, 16), (16, 2))
BESIDE_STAGES = ((2, 16), (4, 8), (8, 4), (16, 2))


class Chunk:
    def __init__(self, names, widths, down):
        self.names, self.widths, self.down = names, widths, down
        self.half = sum(widths) // 2
        self.width = self.half + (2 * D if down is not None else 0)
        self.arrays = [n for n in names if n != "pad"] + (["down"] if down is not None else [])

    def pieces(self, which):
        low, high, start, found = which * self.half, (which + 1) * self.half, 0, []
        for name, width in zip(self.names, self.widths):
            a, b = max(start, low), min(start + width, high)
            if a < b:
                found.append((name, a - start, a - low, b - a))
            start += width
        return found


GATHERED = (
    Chunk(("qkv0", "proj0", "up0", "small", "pad"), (QKV, PROJ, UP, SMALL, PAD), 0),
    Chunk(("qkv1", "proj1", "cls", "order"), (QKV, PROJ, CLS, ORDER), None),
    Chunk(("up1",), (UP,), 1),
)
MLP_SUMS = (Chunk(("up0",), (UP,), 0), Chunk(("up1",), (UP,), 1))
QKV_SUMS = (
    Chunk(("qkv0", "proj0", "small", "pad"), (QKV, PROJ, SMALL, PAD), None),
    Chunk(("qkv1", "proj1", "cls", "pad"), (QKV, PROJ, CLS, PAD), None),
)
FLAT = {"qkv": QKV, "proj": PROJ, "up": UP}


def by_core(place, run):
    for b in range(2):

        @pl.when((place[0] & 1) == b)
        def _(b=b):
            run(b)


def chip_of(place, core, bits, stages=GATHER_STAGES):
    mask = 0
    for bit, stage in zip(bits, stages):
        mask ^= stage[core] * bit
    return (place[0] ^ mask) >> 1


def bits_of(index, count=4):
    return [(index >> k) & 1 for k in range(count)]


def tie(*values):
    return lax.optimization_barrier(values)


def small_block(flat, layer):
    row = flat[layer : layer + 1, :].astype(BF16).astype(F32)
    width = ROWS * ROWS
    spread = jnp.where(iota((16, width), 1) // ROWS == iota((16, width), 0), row, 0.0).astype(BF16)
    at = iota((width, 128), 0) % ROWS + ROWS * layer
    chosen = (at == iota((width, 128), 1)).astype(F32).astype(BF16)
    return dot(spread, chosen, 1, 0)[0:ROWS]


def order_block(ref):
    count = ref.shape[1]
    row = ref[...].astype(F32)
    mine = iota((16, count), 0) == iota((16, count), 1)
    number = jnp.sum(jnp.where(mine, row, 0.0), 1, keepdims=True)
    number = jnp.where(iota((16, 1), 0) < count, number, -129.0)
    high = jnp.floor(number * (1.0 / 128.0))
    lane = iota((16, 128), 1)
    return jnp.where(lane == 0, high, number - 128.0 * high)[0:ROWS]


def pack_body(place, *refs):
    held, (keep, send, down_out), local, sem = refs[0:7], refs[7:10], refs[10:17], refs[17]
    copies = [
        pltpu.make_async_copy(src, dst, sem.at[i]) for i, (src, dst) in enumerate(zip(held, local))
    ]
    for copy in copies:
        copy.start()
    for copy in copies:
        copy.wait()
    source = dict(zip(("qkv", "proj", "up", "small", "cls", "order"), local))
    down = local[6]

    def run(b):
        base = 0
        for chunk in GATHERED:
            for out, which in ((keep, b), (send, 1 - b)):
                for name, column, at, width in chunk.pieces(which):
                    span = slice(base + at, base + at + width)
                    if name == "pad":
                        out[:, span] = jnp.zeros((ROWS, width), F32)
                    elif name == "small":
                        out[:, span] = small_block(source["small"], 0) + small_block(
                            source["small"], 1
                        )
                    elif name == "order":
                        out[:, span] = order_block(source["order"])
                    elif name == "cls":
                        count = source["cls"].shape[0]
                        out[:, span] = jnp.zeros((ROWS, width), F32)
                        out[0:count, span] = source["cls"][:, column : column + width].astype(F32)
                    else:
                        flat, full = source[name[:-1]], FLAT[name[:-1]]
                        for r in range(ROWS):
                            first = r * full + column
                            layer = int(name[-1])
                            out[r : r + 1, span] = flat[layer : layer + 1, first : first + width]
            base += chunk.half

    by_core(place, run)
    for layer in range(LAYERS):
        for r in range(2 * PAIR):
            first = (2 * layer + r // PAIR) * D
            down_out[r % PAIR : r % PAIR + 1, first : first + D] = down[
                layer : layer + 1, r * D : (r + 1) * D
            ]


def merge_body(place, keep, recv, down, *rest):
    outs, work = rest[:2], rest[2]

    def run(b):
        work[ROWS * b : ROWS * (b + 1), :] = keep[...]
        work[ROWS * (1 - b) : ROWS * (2 - b), :] = recv[...]

    by_core(place, run)
    source = target = 0
    for number, chunk in enumerate(GATHERED):
        out = outs[min(number, 1)]
        if number <= 1:
            target = 0
        out[0, :, target : target + chunk.half] = work[:, source : source + chunk.half].astype(BF16)
        if chunk.down is not None:
            at, first = target + chunk.half, 2 * D * chunk.down
            out[0, :, at : at + 2 * D] = down[:, first : first + 2 * D].astype(BF16)
        source, target = source + chunk.half, target + chunk.width


def unpack_body(chunk, base, stages, place, *refs):
    own, sib, outs = refs[0:2], refs[2:4], refs[4:]
    target = dict(zip([n for n in chunk.arrays if n not in TABLES], outs))
    if "small" in chunk.names:
        rows_out, up_out, target["small"] = outs[-3:]
    if "order" in chunk.names:
        order_out, target["order"] = outs[-2:]

    def run(b):
        for which in range(2):
            source = own if which == b else sib
            for received in range(2):
                block = source[received]

                def step(index, _, which=which, received=received, block=block):
                    chip = chip_of(place, which, bits_of(index, 3) + [received], stages)
                    for name, column, at, width in chunk.pieces(which):
                        if name == "pad":
                            continue
                        values = block[index, :, base + at : base + at + width]
                        if name in TABLES:
                            values = values.astype(F32)
                        target[name][chip, :, column : column + width] = values
                    for part in range(0 if chunk.down is None else 2):
                        first = base + chunk.half + part * D
                        target["down"][chip * 4 + 2 * which + part] = block[
                            index, :, first : first + D
                        ]
                    return 0

                lax.fori_loop(0, CHIPS // 2, step, 0)

    by_core(place, run)
    if "order" in chunk.names:
        across = jnp.transpose(target["order"][...].reshape(D, ORDER))
        order_out[...] = across[0:1] * 128.0 + across[1:2]
    if "small" in chunk.names:
        across = jnp.transpose(target["small"][...].reshape(D, SMALL))
        rows_out[...] = across[0:24]
        ups = jnp.concatenate([across[8:12], across[20:24]], 0).astype(BF16)
        spread = (iota((D, FF), 1) // 4 == iota((D, FF), 0)).astype(F32).astype(BF16)
        wide = dot(ups, spread, 1, 0)
        lane = iota((1, FF), 1) % 4
        for layer in range(LAYERS):
            row = jnp.zeros((1, FF), F32)
            for k in range(4):
                row = jnp.where(lane == k, wide[4 * layer + k : 4 * layer + k + 1], row)
            up_out[layer : layer + 1, :] = row


def permute(x, masks):
    return lax.ppermute(x, AXES, [(i, i ^ masks[i & 1]) for i in range(2 * CHIPS)])


def unpack(chunk, base, stages, pieces, sib, place):
    shapes = [
        sds((CHIPS, PAIR, width), BF16)
        for name, width in zip(chunk.names, chunk.widths)
        if name != "pad" and name not in TABLES
    ]
    if chunk.down is not None:
        shapes.append(sds((4 * CHIPS, PAIR, D), BF16))
    count, scratch = len(shapes), []
    if "small" in chunk.names:
        shapes += [sds((24, D), F32), sds((LAYERS, FF), F32)]
        scratch = [pltpu.VMEM((CHIPS, PAIR, SMALL), F32)]
    if "order" in chunk.names:
        shapes += [sds((1, D), F32)]
        scratch = [pltpu.VMEM((CHIPS, PAIR, ORDER), F32)]
    out = call(functools.partial(unpack_body, chunk, base, stages), shapes, scratch=scratch)(
        place, *pieces, *sib
    )
    return [b.reshape(-1, b.shape[2]) for b in out[:count]] + list(out[count:])


def arrange_sums(chunk, place, matrices, keep, send):
    source = dict(zip(chunk.arrays, matrices))

    def run(b):
        for out, which in ((keep, b), (send, 1 - b)):

            def step(index, _, out=out, which=which):
                chip = chip_of(place, which, bits_of(index))
                rows = pl.ds(pl.multiple_of(chip * PAIR, 8), PAIR)
                for name, column, at, width in chunk.pieces(which):
                    if name == "pad":
                        out[index, :, at : at + width] = jnp.zeros((PAIR, width), BF16)
                    else:
                        out[index, :, at : at + width] = source[name][
                            rows, column : column + width
                        ].astype(BF16)
                for part in range(0 if chunk.down is None else 2):
                    at = chunk.half + part * D
                    first = pl.multiple_of((chip * 4 + 2 * which + part) * PAIR, 8)
                    out[index, :, at : at + D] = source["down"][pl.ds(first, PAIR), :].astype(BF16)
                return 0

            lax.fori_loop(0, CHIPS, step, 0)

    by_core(place, run)


def sum_shapes(chunk):
    return [sds((CHIPS, PAIR, chunk.width), BF16)] * 2


def split_rows_body(chunk, place, own, recv, keep, send, *down_out):
    def run(b):
        whole = own[...] + recv[...].astype(F32)
        for out, core in ((keep, b), (send, 1 - b)):
            out[...] = whole[ROWS * core : ROWS * (core + 1), : chunk.half]
        if chunk.down is not None:
            down_out[0][...] = whole[:, chunk.half :]

    by_core(place, run)


class Reduction:
    def __init__(self, chunk, keep, send, place, direct=False):
        self.chunk, self.place, self.stage = chunk, place, 0
        self.keep, self.send = keep, [send]
        z_one, z_two, near, far = GATHER_STAGES
        across = [[near, far, (near[0] ^ far[0],) * 2]] if direct else [[far], [near]]
        self.routes = [[CORE]] + across + [[z_two], [z_one], [CORE]]

    def move(self):
        self.stage += 1
        return [permute(s, mask) for s, mask in zip(self.send, self.routes[self.stage - 1])]

    def absorb(self, received):
        if self.stage == len(self.routes):
            self.result = (self.keep, received[0]) + tuple(self.rest)
            return
        if self.stage == len(self.routes) - 1:
            chunk = self.chunk
            shapes = [sds((ROWS, chunk.half), F32)] * 2
            if chunk.down is not None:
                shapes.append(sds((PAIR, 2 * D), F32))
            self.keep, send, *self.rest = call(functools.partial(split_rows_body, chunk), shapes)(
                self.place, self.keep[0], received[0][0]
            )
            self.send = [send]
            return
        parts = len(self.routes[self.stage]) + 1
        count = self.keep.shape[0] // parts

        def part(i):
            span = slice(i * count, (i + 1) * count)
            return sum([r[span].astype(F32) for r in received], self.keep[span].astype(F32))

        self.send = [part(i).astype(BF16) for i in range(1, parts)]
        self.keep = part(0)


class Transfer:
    def __init__(self, swap, send):
        self.swap, self.send = swap, [send]

    def move(self):
        return [self.swap(self.send[0])]

    def absorb(self, received):
        self.recv = received[0]


def beside(moving, run, *inputs):
    sends, inputs = lax.optimization_barrier(([m.send for m in moving], inputs))
    for m, send in zip(moving, sends):
        m.send = send
    received = [m.move() for m in moving]
    received, out = lax.optimization_barrier((received, run(*inputs)))
    for m, got in zip(moving, received):
        m.absorb(got)
    return out


def adam_math(fix, master, first, second, grad, rate, decay):
    moment = 0.5 * first + 0.5 * grad
    square = 0.5 * second + 0.5 * grad * grad
    update = moment / fix / (jnp.sqrt(square / fix) + adam_eps) + decay * master
    return master - rate * update, moment, square


def small_flat(table):
    width = ROWS * ROWS
    row, column = iota((ROWS, width), 1) // ROWS, iota((ROWS, width), 1) % ROWS
    at = iota((ROWS, width), 0)
    rows = []
    for layer in range(LAYERS):
        mine = table[:, ROWS * layer : ROWS * (layer + 1)]
        spread = jnp.zeros((ROWS, width), F32)
        for j in range(ROWS):
            spread = jnp.where(column == j, mine[:, j : j + 1], spread)
        rows.append(jnp.sum(jnp.where(row == at, spread, 0.0), 0, keepdims=True))
    return jnp.concatenate(rows, 0)


def adam_body(plan, place, fix_ref, *refs):
    chunks, names, extras = plan
    grads, at = [], 0
    for chunk in chunks:
        size = 2 if chunk.down is None else 3
        grads.append(refs[at : at + size])
        at += size
    flats = refs[at : at + 3 * len(names)]
    outs = refs[at + 3 * len(names) : at + 6 * len(names)]
    rest = refs[at + 6 * len(names) :]
    extra = dict(zip(extras, rest))
    work = dict(zip(names, rest[len(extras) :]))

    def run(b):
        for chunk, parts in zip(chunks, grads):
            sides = (parts[0], parts[1]) if b == 0 else (parts[1], parts[0])
            for which in range(2):
                for name, column, first, width in chunk.pieces(which):
                    span = slice(first, first + width)
                    if name in extra:
                        out = extra[name]
                        out[:, column : column + width] = sides[which][
                            0 : out.shape[0], span
                        ].astype(out.dtype)
                    elif name == "small" and name in work:
                        work[name][:, column : column + width] = sides[which][:, span]
                    elif name[:-1] in work:
                        full, layer = FLAT[name[:-1]], int(name[-1])
                        for r in range(ROWS):
                            to = r * full + column
                            work[name[:-1]][layer : layer + 1, to : to + width] = sides[which][
                                r : r + 1, span
                            ]
            if chunk.down is not None and "down" in work:
                layer = chunk.down
                for r in range(2 * PAIR):
                    first = (r // PAIR) * D
                    work["down"][layer : layer + 1, r * D : (r + 1) * D] = parts[2][
                        r % PAIR : r % PAIR + 1, first : first + D
                    ]

    by_core(place, run)
    for i, name in enumerate(names):
        new = adam_math(
            fix_ref[0],
            flats[3 * i][...],
            flats[3 * i + 1][...],
            flats[3 * i + 2][...],
            small_flat(work[name][...]) if name == "small" else work[name][...],
            rate_small if name == "small" else rate_matrix,
            0.0 if name == "small" else decay_matrix,
        )
        for k in range(3):
            outs[3 * i + k][...] = new[k]


class Step:
    def __init__(self, crop_devices, dp_devices, arguments):
        (
            self.patches,
            self.kept_index,
            self.lengths,
            self.source_order,
            self.cot_tokens,
            self.cot_cls,
            step_count,
        ) = arguments[:7]
        self.masters, self.firsts, self.seconds = arguments[7:12], arguments[12:17], arguments[17:22]
        self.crop_count, self.patch_count = self.patches.shape[:2]
        self.half = self.crop_count // 2
        self.dp_devices = dp_devices
        me = lax.axis_index(AXES)
        self.place = jnp.stack([me, me // dp_devices]).astype(jnp.int32)
        self.swap = functools.partial(lax.ppermute, axis_name="crop", perm=[(0, 1), (1, 0)])
        self.crops_half = sds((self.half, SLOTS, D), BF16)
        self.rows = (self.half + 1) * SLOTS
        self.fix = (1.0 - jnp.power(0.5, step_count[0].astype(F32))).reshape(1)

    def tokens(self):
        positions = jnp.arange(SLOTS, dtype=jnp.int32)[None, :]
        rest = SLOTS - self.kept_index.shape[1] - 1
        slots = jnp.pad(self.kept_index, ((0, 0), (1, rest)), constant_values=-1)
        self.slots = jnp.where(positions <= self.lengths[:, None], slots + 1, -1)
        return call(
            functools.partial(tokens_body, self.half, self.patch_count),
            [self.crops_half] * 2,
        )(self.place, self.patches, self.slots)

    def arrange(self, keep, recv):
        return call(
            functools.partial(arrange_body, self.half),
            [
                sds((self.rows, D), F32),
                sds((self.half + 1, SLOTS, 2 * SLOTS), F32),
                sds((2 * self.half, 128), F32),
            ],
        )(self.place, keep, recv)

    def first_ids(self, place):
        views = self.crop_count * (place[0] - place[1] * self.dp_devices) + self.half * place[1]
        return views, views + self.crop_count * self.dp_devices

    def cot_send(self):
        start, count = self.half * (1 - self.place[1]), self.half // 2
        return [
            lax.dynamic_slice_in_dim(self.cot_tokens, start + i * count, count, 0) for i in range(2)
        ]

    def turn(self, x, lens, cot_a, cot_b, order, every_cot):
        shapes = [self.crops_half] * 2 + [sds((self.rows, D), F32), sds(every_cot.shape, F32)]
        return call(functools.partial(turn_body, self.half, self.first_ids), shapes)(
            self.place, x, lens, self.cot_tokens, cot_a, cot_b, order, every_cot
        )

    def split(self, x):
        return call(functools.partial(split_body, self.half), [self.crops_half] * 2)(self.place, x)

    def join(self, keep, recv):
        return call(
            functools.partial(join_body, self.half), sds((self.crop_count, SLOTS, D), BF16)
        )(self.place, keep, recv)

    def scatter(self, keep, recv):
        stride = -(-self.patch_count // 8) * 8
        out = call(
            functools.partial(scatter_body, self.half, self.patch_count),
            sds((self.patch_count, self.crop_count, D), F32),
            scratch=[pltpu.VMEM((self.crop_count * stride, 128), F32)] * (D // 128),
        )(self.place, keep, recv, self.slots)
        return jnp.transpose(out, (1, 0, 2))

    def adam_flat(self, kind, grad):
        return adam_math(
            self.fix[0],
            self.masters[kind],
            self.firsts[kind],
            self.seconds[kind],
            grad,
            rate_small if kind == 4 else rate_matrix,
            0.0 if kind == 4 else decay_matrix,
        )

    def adam_rows(self, fix, chunks, names, kinds, parts, extras, small=False):
        names, kinds = names + ["small"] * small, kinds + [4] * small
        flats = [f[kind] for kind in kinds for f in (self.masters, self.firsts, self.seconds)]
        shapes = [sds(f.shape, F32) for f in flats] + [shape for _, shape in extras]
        plan = (chunks, names, [name for name, _ in extras])
        out = call(
            functools.partial(adam_body, plan),
            shapes,
            scratch=[
                pltpu.VMEM((ROWS, SMALL) if name == "small" else flats[3 * i].shape, F32)
                for i, name in enumerate(names)
            ],
            smem=2,
        )(self.place, fix, *[a for part in parts for a in part], *flats)
        return [list(out[3 * i : 3 * i + 3]) for i in range(len(kinds))], out[3 * len(kinds) :]


def outputs(block_out, cls_grouped, patch_grad, results):
    return (block_out, cls_grouped, patch_grad) + tuple(
        results[kind][part] for part in range(3) for kind in range(5)
    )


def pack_call(place, operands, shapes):
    return pl.pallas_call(
        pack_body,
        in_specs=[SM] + [pl.BlockSpec(memory_space=pltpu.HBM)] * len(operands),
        out_specs=[VM] * len(shapes),
        out_shape=shapes,
        scratch_shapes=[pltpu.VMEM(a.shape, a.dtype) for a in operands]
        + [pltpu.SemaphoreType.DMA((len(operands),))],
        compiler_params=pltpu.CompilerParams(vmem_limit_bytes=VMEM_LIMIT),
        cost_estimate=NO_COST,
    )(place, *[pltpu.with_memory_space_constraint(a, pltpu.HBM) for a in operands])


def staged_step(step):
    place = step.place
    total_half = sum(c.half for c in GATHERED)
    rows_shape = sds((ROWS, total_half), F32)
    keep, send, downs = pack_call(
        place,
        step.masters[:3]
        + (step.masters[4], step.cot_cls, step.source_order[None, :], step.masters[3]),
        [rows_shape, rows_shape, sds((PAIR, 4 * D), F32)],
    )
    recv = permute(send, CORE)
    width = GATHERED[1].width
    a, b = call(
        merge_body,
        [
            sds((1, PAIR, GATHERED[0].width), BF16),
            sds((1, PAIR, width + GATHERED[2].width), BF16),
        ],
        scratch=[pltpu.VMEM((PAIR, total_half), F32)],
    )(place, keep, recv, downs)

    step.kept_index, step.patches, a = tie(step.kept_index, step.patches, a)
    a_recv = permute(a, GATHER_STAGES[0])
    tok_keep, tok_send = step.tokens()
    tok_recv = step.swap(tok_send)
    a_recv, b = tie(a_recv, b)
    a = jnp.concatenate([a, a_recv])
    a_recv = permute(a, GATHER_STAGES[1])
    b_recv = permute(b, BESIDE_STAGES[0])
    a_recv, tok_recv, b_recv = tie(a_recv, tok_recv, b_recv)
    a = jnp.concatenate([a, a_recv])
    b = jnp.concatenate([b, b_recv])
    a_recv = permute(a, GATHER_STAGES[2])
    b_recv = permute(b, BESIDE_STAGES[1])
    x, bias, lens = step.arrange(tok_keep, tok_recv)
    a_recv, b_recv, x = tie(a_recv, b_recv, x)
    a = jnp.concatenate([a, a_recv])
    b = jnp.concatenate([b, b_recv])
    a_recv = permute(a, GATHER_STAGES[3])
    b_recv = permute(b, BESIDE_STAGES[2])
    a_sib = permute(a, CORE)
    cot_a, cot_b = step.cot_send()
    a, a_recv, a_sib, b_recv, cot_a, cot_b = tie(a, a_recv, a_sib, b_recv, cot_a, cot_b)
    a_sib = (a_sib, permute(a_recv, CORE))
    b = jnp.concatenate([b, b_recv])
    b_recv = permute(b, BESIDE_STAGES[3])
    b_sib = permute(b, CORE)
    qkv0, proj0, up0, down0, small, up_bias = unpack(
        GATHERED[0], 0, GATHER_STAGES, (a, a_recv), a_sib, place
    )

    small0, small1 = small[0:12], small[12:24]
    norms_0, n1_0, qkv_0, att_0, prob_0, mid_0, n2_0 = layer_forward_one(
        x, bias, qkv0, proj0, small0
    )
    x_1, act_0, slope_0 = layer_forward_two(mid_0, n2_0, up0, down0, small0, up_bias[0:1])
    x_1, b_recv, b_sib = tie(x_1, b_recv, b_sib)
    b_sib = (b_sib, permute(b_recv, CORE))
    cot_a = step.swap(cot_a)
    qkv1, proj1, every_cot, order = unpack(
        GATHERED[1], 0, BESIDE_STAGES, (b, b_recv), b_sib, place
    )
    norms_1, n1_1, qkv_1, att_1, prob_1, mid_1, n2_1 = layer_forward_one(
        x_1, bias, qkv1, proj1, small1
    )
    mid_1, n2_1, cot_a, cot_b = tie(mid_1, n2_1, cot_a, cot_b)
    cot_b = step.swap(cot_b)
    up1, down1 = unpack(GATHERED[2], width, BESIDE_STAGES, (b, b_recv), b_sib, place)
    final, act_1, slope_1 = layer_forward_two(mid_1, n2_1, up1, down1, small1, up_bias[1:2])
    out_keep, out_send, g, dense_cls = step.turn(final, lens, cot_a, cot_b, order, every_cot)

    def mlp_finish(layer):
        def finish(place, matrices, outs):
            arrange_sums(MLP_SUMS[layer], place, matrices, outs[0], outs[1])

        return finish

    def qkv_finish(layer):
        def finish(place, matrices, outs, rows):
            matrices = list(matrices)
            if layer == 0:
                weight, proj, rows_one1, rows_two1, up1, rows_two0, up0 = matrices
                table = outs[2]
                table[...] = jnp.zeros(table.shape, F32)
                table[:, 0:32] = small_table(((rows, rows_two0, up0), (rows_one1, rows_two1, up1)))
                matrices = [weight, proj, table]
            arrange_sums(QKV_SUMS[layer], place, matrices, outs[0], outs[1])

        return finish

    out_swap = Transfer(step.swap, out_send)
    keep, send, g_hid, bias_up1 = beside(
        [out_swap],
        lambda g: mlp_weights(
            place, mlp_finish(1), sum_shapes(MLP_SUMS[1]), g, n2_1, act_1, slope_1, down1
        ),
        g,
    )
    m1 = Reduction(MLP_SUMS[1], keep, send, place)
    g_mid, g_proj, g_att, rows_two1 = beside(
        [m1],
        lambda g_hid: mlp_rows(g, g_hid, norms_1[2], norms_1[3], att_1, up1, proj1, small1),
        g_hid,
    )

    def last_qkv(g_att):
        keep, send, g_nrm, rows = qkv_weights(
            place, qkv_finish(1), sum_shapes(QKV_SUMS[1]), (g_proj, dense_cls),
            g_att, n1_1, qkv_1, prob_1, norms_1[0], qkv1,
        )
        return keep, send, norm_one(g_nrm, norms_1[0], norms_1[1], g_mid, small1), rows

    keep, send, g, rows_one1 = beside([m1], last_qkv, g_att)
    q1 = Reduction(QKV_SUMS[1], keep, send, place)

    keep, send, g_hid, bias_up0 = beside(
        [q1, m1],
        lambda g: mlp_weights(
            place, mlp_finish(0), sum_shapes(MLP_SUMS[0]), g, n2_0, act_0, slope_0, down0
        ),
        g,
    )
    m0 = Reduction(MLP_SUMS[0], keep, send, place)
    g_mid, g_proj, g_att, rows_two0 = beside(
        [m0, q1, m1],
        lambda g_hid: mlp_rows(g, g_hid, norms_0[2], norms_0[3], att_0, up0, proj0, small0),
        g_hid,
    )
    keep, send, _, g_nrm, _ = beside(
        [m0, q1, m1],
        lambda g_att: qkv_weights(
            place, qkv_finish(0), sum_shapes(QKV_SUMS[0]) + [sds((D, SMALL), F32)],
            (g_proj, rows_one1, rows_two1, bias_up1, rows_two0, bias_up0),
            g_att, n1_0, qkv_0, prob_0, norms_0[0], qkv0,
        ),
        g_att,
    )
    q0 = Reduction(QKV_SUMS[0], keep, send, place, direct=True)
    back_keep, back_send = beside(
        [q0, m0, q1],
        lambda g_nrm: step.split(norm_one(g_nrm, norms_0[0], norms_0[1], g_mid, small0)),
        g_nrm,
    )
    block_out = beside(
        [q0, m0, q1], lambda keep, recv: step.join(keep, recv), out_keep, out_swap.recv
    )
    back_send, q0.send = tie(back_send, q0.send)
    back_recv = step.swap(back_send)
    back_keep = beside([q0, m0, q1, m1], lambda v: v, back_keep)
    patch_grad = beside([q0, m0], lambda keep: step.scatter(keep, back_recv), back_keep)

    def adam_mlp(fix):
        new, _ = step.adam_rows(
            fix, [MLP_SUMS[1], MLP_SUMS[0]], ["up", "down"], [2, 3], [m1.result, m0.result], []
        )
        return new[0] + new[1]

    new = beside([q0], adam_mlp, step.fix)
    new_up, new_down = new[:3], new[3:]
    (new_qkv, new_proj, new_small), (cls_grouped,) = step.adam_rows(
        step.fix,
        [QKV_SUMS[1], QKV_SUMS[0]],
        ["qkv", "proj"],
        [0, 1],
        [q1.result, q0.result],
        [("cls", sds((step.crop_count, CLS), BF16))],
        small=True,
    )
    return outputs(block_out, cls_grouped, patch_grad, (new_qkv, new_proj, new_up, new_down, new_small))


def plain_step(step):
    def gather(values):
        return lax.all_gather(values, AXES, axis=0, tiled=True)

    weights, smalls, up_biases = [], [], []
    for layer in range(LAYERS):
        flat = [gather(m[layer].astype(BF16)) for m in step.masters]
        small = flat[4].reshape(D, 8 + FF // D).astype(F32)
        weights.append(
            (
                flat[0].reshape(D, QKV),
                flat[1].reshape(D, D),
                flat[2].reshape(D, FF),
                flat[3].reshape(FF, D),
            )
        )
        smalls.append(jnp.transpose(small[:, :8]))
        up_biases.append(small[:, 8:].reshape(1, FF))
    keep, send = step.tokens()
    x, bias, lens = step.arrange(keep, step.swap(send))
    saved = []
    for layer in range(LAYERS):
        qkv_w, proj_w, up_w, down_w = weights[layer]
        one = layer_forward_one(x, bias, qkv_w, proj_w, smalls[layer])
        x, active, slope = layer_forward_two(
            one[5], one[6], up_w, down_w, smalls[layer], up_biases[layer]
        )
        saved.append(one + (active, slope))
    order = gather(step.source_order).astype(F32)[None, :]
    out_keep, out_send, g, dense_cls = step.turn(
        x, lens, *[step.swap(item) for item in step.cot_send()], order, gather(step.cot_cls)
    )
    block_out = step.join(out_keep, step.swap(out_send))
    gradients = [None] * LAYERS

    def two_out(place, matrices, outs, *_):
        for value, out in zip(matrices, outs):
            out[...] = value[...]

    for layer in reversed(range(LAYERS)):
        norms, normed_one, qkv, attended, prob, _, normed_two, active, slope = saved[layer]
        qkv_w, proj_w, up_w, down_w = weights[layer]
        g_up, g_down, g_hid, bias_up = mlp_weights(
            step.place, two_out, [sds((D, FF), F32), sds((FF, D), F32)],
            g, normed_two, active, slope, down_w,
        )
        g_mid, g_proj, g_att, two = mlp_rows(
            g, g_hid, norms[2], norms[3], attended, up_w, proj_w, smalls[layer]
        )
        g_qkv_w, g_nrm, one = qkv_weights(
            step.place, two_out, [sds((D, QKV), F32)], (),
            g_att, normed_one, qkv, prob, norms[0], qkv_w,
        )
        g = norm_one(g_nrm, norms[0], norms[1], g_mid, smalls[layer])
        eight = jnp.concatenate([one[0:4], two[3:4], two[0:3]])
        table = jnp.concatenate([jnp.transpose(eight), bias_up.reshape(D, FF // D)], 1)
        gradients[layer] = (g_qkv_w, g_proj, g_up, g_down, table)
    back_keep, back_send = step.split(g)
    patch_grad = step.scatter(back_keep, step.swap(back_send))

    def scatter_sum(values):
        return lax.psum_scatter(values, AXES, scatter_dimension=0, tiled=True)

    results = []
    for kind in range(5):
        shares = [
            scatter_sum(gradients[layer][kind].reshape(-1).astype(F32)) for layer in range(LAYERS)
        ]
        results.append(step.adam_flat(kind, jnp.stack(shares)))
    cls_grouped = scatter_sum(dense_cls).astype(BF16)
    return outputs(block_out, cls_grouped, patch_grad, results)


def on_device(crop_devices, dp_devices, *arguments):
    step = Step(crop_devices, dp_devices, arguments)
    owned = step.masters[0].shape[1]
    staged = crop_devices * dp_devices == 2 * CHIPS and owned == ROWS * QKV
    if staged and step.crop_count <= ROWS:
        return staged_step(step)
    return plain_step(step)


def solution(mesh):
    crops = [P(AXES, None, None), P(AXES, None), P(AXES), P(AXES), P(AXES, None, None)]
    flat = P(None, AXES)
    return jax.shard_map(
        functools.partial(on_device, mesh.shape["crop"], mesh.shape["dp"]),
        mesh=mesh,
        in_specs=tuple(crops + [P(AXES, None), P()] + [flat] * 15),
        out_specs=(crops[0], crops[1], crops[0]) + (flat,) * 15,
        check_vma=False,
    )
```

```python
import functools

import jax
import jax.numpy as jnp
from jax import lax
from jax.experimental import pallas as pl
from jax.experimental.pallas import tpu as pltpu
from jax.sharding import PartitionSpec as P

D = 384
HEADS = 6
HEAD_DIM = 64
FF = 1536
LAYERS = 2
SLOTS = 144
FOCAL_SLOTS = 32
LEN_ROW = 143

eps_norm = 1e-06
neg_big = -1e30
adam_eps = 1e-08
rate_matrix = 0.04
decay_matrix = 0.05
rate_small = 0.4

F32 = jnp.float32
BF16 = jnp.bfloat16
VM = pl.BlockSpec(memory_space=pltpu.VMEM)
SM = pl.BlockSpec(memory_space=pltpu.SMEM)
AXES = ("crop", "dp")
VMEM_LIMIT = 12 * 1024 * 1024
NO_COST = pl.CostEstimate(flops=1, bytes_accessed=1, transcendentals=0)


def sds(shape, dtype):
    return jax.ShapeDtypeStruct(shape, dtype)


def call(body, out_shape, scratch=(), smem=1):
    def run(*operands):
        return pl.pallas_call(
            body,
            out_shape=out_shape,
            in_specs=[SM] * smem + [VM] * (len(operands) - smem),
            out_specs=jax.tree.map(lambda _: VM, out_shape),
            scratch_shapes=list(scratch),
            compiler_params=pltpu.CompilerParams(vmem_limit_bytes=VMEM_LIMIT),
            cost_estimate=NO_COST,
        )(*operands)

    return run


def iota(shape, axis):
    return lax.broadcasted_iota(jnp.int32, shape, axis)


def dot(a, b, ca, cb):
    return lax.dot_general(a, b, (((ca,), (cb,)), ((), ())), preferred_element_type=F32)


def slot_onehot(slots, c, patch_count):
    row = slots[pl.ds(c, 1), :]
    return row, (iota((patch_count, SLOTS), 0) == row).astype(F32).astype(BF16)


def tokens_body(half, patch_count, place, patches, slots, keep, send):
    y = place[1]
    row_index = iota((SLOTS, D), 0)
    for i in range(half):
        for out, c in ((keep, half * y + i), (send, half * (1 - y) + i)):
            row, onehot = slot_onehot(slots, c, patch_count)
            count = jnp.sum((row >= 0).astype(F32), axis=1, keepdims=True) - 1.0
            picked = dot(onehot, patches[c], 0, 0)
            out[i] = jnp.where(row_index == LEN_ROW, count, picked).astype(BF16)


class Halves:
    def __init__(self, first, second):
        self.parts, self.count = (first, second), first.shape[0]

    def __getitem__(self, key):
        i = key[0] if isinstance(key, tuple) else key
        rest = key[1:] if isinstance(key, tuple) else ()
        return self.parts[i // self.count][(i % self.count,) + tuple(rest)]


def arrange_body(half, place, keep, recv, x_ref, bias_ref, lens_ref):
    y = place[1]
    base = half * SLOTS
    used = half * FOCAL_SLOTS

    def run(v_src, f_src):
        k = iota((SLOTS, 2 * SLOTS), 0)
        q = iota((SLOTS, 2 * SLOTS), 1) % SLOTS
        row_index = iota((SLOTS, D), 0)
        for i in range(half):
            t = v_src[i].astype(F32)
            n = t[LEN_ROW : LEN_ROW + 1, 0:1]
            x_ref[SLOTS * i : SLOTS * (i + 1), :] = jnp.where(row_index == LEN_ROW, 0.0, t)
            bias_ref[i] = jnp.where(k.astype(F32) <= n, 0.0, neg_big)
            lens_ref[i : i + 1, :] = jnp.broadcast_to(n, (1, 128))
        limit = jnp.full((SLOTS, 2 * SLOTS), 1000.0, F32)
        for i in range(half):
            x_ref[base + FOCAL_SLOTS * i : base + FOCAL_SLOTS * (i + 1), :] = f_src[
                i, 0:FOCAL_SLOTS
            ].astype(F32)
            n = f_src[i, SLOTS - 16 : SLOTS].astype(F32)[15:16, 0:1]
            limit = jnp.where((k // FOCAL_SLOTS) == i, n, limit)
            lens_ref[half + i : half + i + 1, :] = jnp.broadcast_to(n, (1, 128))
        if used < SLOTS:
            x_ref[base + used : base + SLOTS, :] = jnp.zeros((SLOTS - used, D), F32)
        same = (q // FOCAL_SLOTS) == (k // FOCAL_SLOTS)
        inside = (k % FOCAL_SLOTS).astype(F32) <= limit
        bias_ref[half] = jnp.where(same & inside, 0.0, neg_big)

    @pl.when(y == 0)
    def _():
        run(keep, recv)

    @pl.when(y == 1)
    def _():
        run(recv, keep)


def turn_body(half, first_ids, place, x_ref, lens, cot, recv_a, recv_b, order, every_cot, *outs):
    keep, send, g_ref, dense = outs
    recv = Halves(recv_a, recv_b)
    y = place[1]
    base = half * SLOTS
    used = half * FOCAL_SLOTS
    views, focals = first_ids(place)
    index = iota((2 * half, 1), 0)
    ids = jnp.where(index < half, views + index, focals + index - half).astype(F32)
    chosen = (order[...] == ids).astype(F32).astype(BF16)
    top = dot(chosen, every_cot[...], 1, 0)

    def piece(values, n, row, rows):
        at = iota((rows, D), 0)
        masked = jnp.where(at.astype(F32) <= n, values, 0.0)
        return masked + jnp.where(at == 0, row, 0.0)

    def run(v_out, f_out, v_get, f_get):
        cls = []
        for i in range(half):
            n = lens[i : i + 1, 0:1]
            rows = slice(SLOTS * i, SLOTS * (i + 1))
            v = x_ref[rows, :]
            cls.append(v[0:1])
            v_out[i] = jnp.where(iota((SLOTS, D), 0).astype(F32) <= n, v, 0.0).astype(BF16)
            g_ref[rows, :] = piece(v_get(i).astype(F32), n, top[i : i + 1], SLOTS)
        for i in range(half):
            n = lens[half + i : half + i + 1, 0:1]
            rows = slice(base + FOCAL_SLOTS * i, base + FOCAL_SLOTS * (i + 1))
            f = x_ref[rows, :]
            cls.append(f[0:1])
            f = jnp.where(iota((FOCAL_SLOTS, D), 0).astype(F32) <= n, f, 0.0)
            f_out[i, 0:FOCAL_SLOTS] = f.astype(BF16)
            f_out[i, FOCAL_SLOTS:SLOTS] = jnp.zeros((SLOTS - FOCAL_SLOTS, D), BF16)
            g_ref[rows, :] = piece(
                f_get(i)[0:FOCAL_SLOTS].astype(F32), n, top[half + i : half + i + 1], FOCAL_SLOTS
            )
        if used < SLOTS:
            g_ref[base + used : base + SLOTS, :] = jnp.zeros((SLOTS - used, D), F32)
        dense[...] = dot(chosen, jnp.concatenate(cls, 0).astype(BF16), 0, 0)

    @pl.when(y == 0)
    def _():
        run(keep, send, lambda i: cot[i], lambda i: recv[i])

    @pl.when(y == 1)
    def _():
        run(send, keep, lambda i: recv[i], lambda i: cot[half + i])


def split_body(half, place, x_ref, keep, send):
    y = place[1]
    base = half * SLOTS

    def run(v_out, f_out):
        for i in range(half):
            v_out[i] = x_ref[SLOTS * i : SLOTS * (i + 1), :].astype(BF16)
            rows = slice(base + FOCAL_SLOTS * i, base + FOCAL_SLOTS * (i + 1))
            f_out[i, 0:FOCAL_SLOTS] = x_ref[rows, :].astype(BF16)
            f_out[i, FOCAL_SLOTS:SLOTS] = jnp.zeros((SLOTS - FOCAL_SLOTS, D), BF16)

    @pl.when(y == 0)
    def _():
        run(keep, send)

    @pl.when(y == 1)
    def _():
        run(send, keep)


def join_body(half, place, keep, recv, out):
    y = place[1]
    for i in range(half):
        out[half * y + i] = keep[i]
        out[half * (1 - y) + i] = recv[i]


def scatter_body(half, patch_count, place, keep, recv, slots, out, *work):
    y = place[1]
    stride = work[0].shape[0] // (2 * half)
    for i in range(half):
        for src, c in ((keep, half * y + i), (recv, half * (1 - y) + i)):
            _, onehot = slot_onehot(slots, c, patch_count)
            first = pl.multiple_of(c * stride, 8)
            rows = dot(onehot, src[i], 1, 0)
            for t, part in enumerate(work):
                part[pl.ds(first, patch_count), :] = rows[:, 128 * t : 128 * (t + 1)]

    def copy(p):
        for t, part in enumerate(work):
            out[p, :, 128 * t : 128 * (t + 1)] = part[pl.ds(p, 2 * half, stride=stride), :]

    group = 8

    def step(i, _):
        for j in range(group):
            copy(i * group + j)
        return 0

    lax.fori_loop(0, patch_count // group, step, 0)
    for p in range(patch_count // group * group, patch_count):
        copy(p)


def lane_mask(second, value):
    lane = iota((1, 128), 1)
    chosen = (lane >= HEAD_DIM) if second else (lane < HEAD_DIM)
    return jnp.where(chosen, value, 0.0).astype(BF16)


def pair_rows(values, scale):
    return jnp.concatenate([values * lane_mask(0, scale), values * lane_mask(1, scale)], 0)


def pair_lanes(values):
    own = iota((SLOTS, 128), 1) < HEAD_DIM
    return jnp.where(own, values[:SLOTS], values[SLOTS:])


def heads_at(part, pair):
    return slice(part * D + 128 * pair, part * D + 128 * (pair + 1))


PAIRS = HEADS // 2
HEAD_SCALE = HEAD_DIM**-0.5


def block_rows(b):
    return slice(b * SLOTS, (b + 1) * SLOTS)


def attend_scores(qkv, bias, prob, r, b):
    for i in range(PAIRS):
        queries = pair_rows(qkv[r, heads_at(0, i)], HEAD_SCALE)
        s = jnp.where(bias < 0.0, neg_big, dot(qkv[r, heads_at(1, i)], queries, 1, 1))
        e = jnp.exp(s - jnp.max(s, 0, keepdims=True))
        prob[b, i] = (e * (1.0 / jnp.sum(e, 0, keepdims=True))).astype(BF16)


def attend_values(qkv, attended, prob, r, b):
    for i in range(PAIRS):
        out = dot(prob[b, i], qkv[r, heads_at(2, i)], 0, 0)
        attended[r, heads_at(0, i)] = pair_lanes(out).astype(BF16)


def attend_backward_block(qkv, prob, grad, out, r, b):
    grads = [pair_rows(grad[r, heads_at(0, i)], 1.0) for i in range(PAIRS)]
    inner = [dot(qkv[r, heads_at(2, i)], grads[i], 1, 1) for i in range(PAIRS)]
    for i in range(PAIRS):
        out[r, heads_at(2, i)] = dot(prob[b, i], grads[i], 1, 0).astype(BF16)
    scores = []
    for i in range(PAIRS):
        p = prob[b, i].astype(F32)
        t = p * inner[i]
        scores.append((t - p * jnp.sum(t, 0, keepdims=True)).astype(BF16))
    for i in range(PAIRS):
        queries = pair_rows(qkv[r, heads_at(0, i)], HEAD_SCALE)
        out[r, heads_at(1, i)] = dot(scores[i], queries, 1, 0).astype(BF16)
    for i in range(PAIRS):
        back = pair_lanes(dot(scores[i], qkv[r, heads_at(1, i)], 0, 0))
        out[r, heads_at(0, i)] = (back * HEAD_SCALE).astype(BF16)


def total(values):
    return jnp.sum(values, 0, keepdims=True)


def normalized(values):
    centered = values - jnp.mean(values, -1, keepdims=True)
    scale = lax.rsqrt(jnp.mean(centered * centered, -1, keepdims=True) + eps_norm)
    return centered * scale, scale


def gelu_parts(v):
    c = 0.7978845608028654
    a = 0.044715
    square = v * v
    t = jnp.tanh(v * (c + (c * a) * square))
    h = 0.5 * v
    ht = h * t
    return h + ht, 0.5 * (1.0 + t) + (h - ht * t) * (c + (3.0 * a * c) * square)


def attention_body(x, bias, qkv_w, proj_w, small, *outs):
    unit_one, scale_one, unit_two, scale_two, normed_one, qkv, attended, prob, mid, normed_two = outs
    count = x.shape[0] // SLOTS

    def norm(values, unit_ref, scale_ref, normed_ref, first):
        unit, scale = normalized(values)
        unit_ref[...] = unit.astype(BF16)
        scale_ref[...] = scale
        normed_ref[...] = (unit * small[first : first + 1] + small[first + 1 : first + 2]).astype(
            BF16
        )

    norm(x[...], unit_one, scale_one, normed_one, 0)
    for c in range(3):
        w = slice(c * D, (c + 1) * D)
        part = dot(normed_one[...], qkv_w[:, w], 1, 0)
        if c != 1:
            part = part + small[2 + c // 2 : 3 + c // 2]
        qkv[:, w] = part.astype(BF16)
    for b in range(count + 1):
        if b < count:
            attend_scores(qkv, bias[b], prob, block_rows(b), b)
        if b > 0:
            attend_values(qkv, attended, prob, block_rows(b - 1), b - 1)
    whole = x[...] + dot(attended[...], proj_w[...], 1, 0) + small[4:5]
    mid[...] = whole
    norm(whole, unit_two, scale_two, normed_two, 5)


def layer_forward_one(x, bias, qkv_w, proj_w, small):
    rows = x.shape[0]
    row = sds((rows, D), BF16)
    scale = sds((rows, 1), F32)
    out = call(
        attention_body,
        [
            row, scale, row, scale, row, sds((rows, 3 * D), BF16), row,
            sds((rows // SLOTS, PAIRS, SLOTS, 2 * SLOTS), BF16), sds((rows, D), F32), row,
        ],
        smem=0,
    )(x, bias, qkv_w, proj_w, small)
    return (tuple(out[:4]),) + tuple(out[4:])


def feed_forward_body(mid, normed, up_w, down_w, small, up_bias, out, active, slope):
    for c in range(FF // 256):
        w = slice(c * 256, (c + 1) * 256)
        value, derivative = gelu_parts(dot(normed[...], up_w[:, w], 1, 0) + up_bias[:, w])
        active[:, w] = value.astype(BF16)
        slope[:, w] = derivative.astype(BF16)
    out[...] = dot(active[...], down_w[...], 1, 0) + mid[...] + small[7:8]


def layer_forward_two(mid, normed_two, up_w, down_w, small, up_bias):
    rows = mid.shape[0]
    return call(
        feed_forward_body,
        [sds((rows, D), F32), sds((rows, FF), BF16), sds((rows, FF), BF16)],
        smem=0,
    )(mid, normed_two, up_w, down_w, small, up_bias)


def norm_back(grad, unit, scale, gain):
    inner = grad * gain
    mean, along = jnp.mean(inner, -1, keepdims=True), jnp.mean(inner * unit, -1, keepdims=True)
    return scale * (inner - mean - unit * along)


def mlp_weights_body(finish, place, g, normed, active, slope, down_w, *refs):
    outs, (branch, up, down) = refs[:-3], refs[-3:]
    g_hidden, bias_up = outs[-2:]
    branch[...] = g[...].astype(BF16)
    for c in range(FF // D):
        w = slice(c * D, (c + 1) * D)
        t = (dot(branch[...], down_w[w, :], 1, 1) * slope[:, w].astype(F32)).astype(BF16)
        g_hidden[:, w] = t
        bias_up[:, w] = total(t.astype(F32))
    for c in range(FF // D):
        w = slice(c * D, (c + 1) * D)
        down[w, :] = dot(active[:, w], branch[...], 0, 0)
    up[...] = dot(normed[...], g_hidden[...], 0, 0)
    finish(place, (up, down), outs[:-2])


def mlp_rows_body(g, g_hidden, unit, scale, attended, up_w, proj_w, small, g_mid, g_proj, g_att, rows, work):
    grad = dot(g_hidden[...], up_w[...], 1, 1)
    along = unit[...].astype(F32)
    rows[...] = jnp.zeros(rows.shape, F32)
    rows[0:1] = total(grad * along)
    rows[1:2] = total(grad)
    rows[2:3] = total(g[...].astype(BF16).astype(F32))
    whole = norm_back(grad, along, scale[...], small[5:6]) + g[...]
    g_mid[...] = whole
    work[...] = whole.astype(BF16)
    rows[3:4] = total(work[...].astype(F32))
    g_att[...] = dot(work[...], proj_w[...], 1, 1).astype(BF16)
    g_proj[...] = dot(attended[...], work[...], 0, 0)


def qkv_weights_body(finish, extra_count, place, g_att, normed, qkv, prob, unit, qkv_w, *refs):
    extra, outs, (g_qkv, weight) = refs[:extra_count], refs[extra_count:-2], refs[-2:]
    g_normed, rows = outs[-2:]
    for b in range(unit.shape[0] // SLOTS):
        attend_backward_block(qkv, prob, g_att, g_qkv, block_rows(b), b)
    grad = dot(g_qkv[...], qkv_w[...], 1, 1)
    g_normed[...] = grad
    rows[...] = jnp.zeros(rows.shape, F32)
    rows[0:1] = total(grad * unit[...].astype(F32))
    rows[1:2] = total(grad)
    rows[2:3] = total(g_qkv[:, 0:D].astype(F32))
    rows[3:4] = total(g_qkv[:, 2 * D : 3 * D].astype(F32))
    weight[...] = dot(normed[...], g_qkv[...], 0, 0)
    finish(place, (weight,) + extra, outs[:-2], rows)


def norm_one_body(g_normed, unit, scale, g_mid, small, out):
    back = norm_back(g_normed[...], unit[...].astype(F32), scale[...], small[0:1])
    out[...] = back + g_mid[...]


def mlp_weights(place, finish, shapes, g, normed, active, slope, down_w):
    rows = g.shape[0]
    return call(
        functools.partial(mlp_weights_body, finish),
        list(shapes) + [sds((rows, FF), BF16), sds((1, FF), F32)],
        scratch=[
            pltpu.VMEM((rows, D), BF16),
            pltpu.VMEM((D, FF), F32),
            pltpu.VMEM((FF, D), F32),
        ],
    )(place, g, normed, active, slope, down_w)


def mlp_rows(g, g_hidden, unit, scale, attended, up_w, proj_w, small):
    rows = g.shape[0]
    return call(
        mlp_rows_body,
        [sds((rows, D), F32), sds((D, D), F32), sds((rows, D), BF16), sds((8, D), F32)],
        scratch=[pltpu.VMEM((rows, D), BF16)],
        smem=0,
    )(g, g_hidden, unit, scale, attended, up_w, proj_w, small)


def qkv_weights(place, finish, shapes, extra, g_att, normed, qkv, prob, unit, qkv_w):
    rows = unit.shape[0]
    return call(
        functools.partial(qkv_weights_body, finish, len(extra)),
        list(shapes) + [sds((rows, D), F32), sds((8, D), F32)],
        scratch=[pltpu.VMEM((rows, 3 * D), BF16), pltpu.VMEM((D, 3 * D), F32)],
    )(place, g_att, normed, qkv, prob, unit, qkv_w, *extra)


def norm_one(g_normed, unit, scale, g_mid, small):
    return call(norm_one_body, sds(g_mid.shape, F32), smem=0)(g_normed, unit, scale, g_mid, small)


def small_table(groups):
    flat, wide = [], []
    lane = iota((1, FF), 1) % 4
    for rows_one, rows_two, bias_up in groups:
        flat += [rows_one[0:4, :], rows_two[3:4, :], rows_two[0:3, :], jnp.zeros((4, D), F32)]
        wide += [jnp.zeros((8, FF), F32)]
        wide += [jnp.where(lane == k, bias_up[...], 0.0) for k in range(4)]
    flat = jnp.concatenate(flat + [jnp.zeros((8, D), F32)], 0).astype(BF16)
    wide = jnp.concatenate(wide + [jnp.zeros((8, FF), F32)], 0).astype(BF16)
    same = (iota((D, D), 0) == iota((D, D), 1)).astype(F32).astype(BF16)
    spread = (iota((D, FF), 1) // 4 == iota((D, FF), 0)).astype(F32).astype(BF16)
    return dot(same, flat, 1, 1) + dot(spread, wide, 1, 1)


ROWS = 12
PAIR = 24
CHIPS = 16
QKV, PROJ, UP, SMALL, CLS, ORDER, PAD = 3 * D, D, FF, 128, D, 128, 128
CORE = (1, 1)
TABLES = ("small", "order")
GATHER_STAGES = ((4, 8), (8, 4), (2, 16), (16, 2))
BESIDE_STAGES = ((2, 16), (4, 8), (8, 4), (16, 2))


class Chunk:
    def __init__(self, names, widths, down):
        self.names, self.widths, self.down = names, widths, down
        self.half = sum(widths) // 2
        self.width = self.half + (2 * D if down is not None else 0)
        self.arrays = [n for n in names if n != "pad"] + (["down"] if down is not None else [])

    def pieces(self, which):
        low, high, start, found = which * self.half, (which + 1) * self.half, 0, []
        for name, width in zip(self.names, self.widths):
            a, b = max(start, low), min(start + width, high)
            if a < b:
                found.append((name, a - start, a - low, b - a))
            start += width
        return found


GATHERED = (
    Chunk(("qkv0", "proj0", "up0", "small", "pad"), (QKV, PROJ, UP, SMALL, PAD), 0),
    Chunk(("qkv1", "proj1", "cls", "order"), (QKV, PROJ, CLS, ORDER), None),
    Chunk(("up1",), (UP,), 1),
)
MLP_SUMS = (Chunk(("up0",), (UP,), 0), Chunk(("up1",), (UP,), 1))
QKV_SUMS = (
    Chunk(("qkv0", "proj0", "small", "pad"), (QKV, PROJ, SMALL, PAD), None),
    Chunk(("qkv1", "proj1", "cls", "pad"), (QKV, PROJ, CLS, PAD), None),
)
FLAT = {"qkv": QKV, "proj": PROJ, "up": UP}


def by_core(place, run):
    for b in range(2):

        @pl.when((place[0] & 1) == b)
        def _(b=b):
            run(b)


def chip_of(place, core, bits, stages=GATHER_STAGES):
    mask = 0
    for bit, stage in zip(bits, stages):
        mask ^= stage[core] * bit
    return (place[0] ^ mask) >> 1


def bits_of(index, count=4):
    return [(index >> k) & 1 for k in range(count)]


def tie(*values):
    return lax.optimization_barrier(values)


def small_block(flat, layer):
    row = flat[layer : layer + 1, :].astype(BF16).astype(F32)
    width = ROWS * ROWS
    spread = jnp.where(iota((16, width), 1) // ROWS == iota((16, width), 0), row, 0.0).astype(BF16)
    at = iota((width, 128), 0) % ROWS + ROWS * layer
    chosen = (at == iota((width, 128), 1)).astype(F32).astype(BF16)
    return dot(spread, chosen, 1, 0)[0:ROWS]


def order_block(ref):
    count = ref.shape[1]
    row = ref[...].astype(F32)
    mine = iota((16, count), 0) == iota((16, count), 1)
    number = jnp.sum(jnp.where(mine, row, 0.0), 1, keepdims=True)
    number = jnp.where(iota((16, 1), 0) < count, number, -129.0)
    high = jnp.floor(number * (1.0 / 128.0))
    lane = iota((16, 128), 1)
    return jnp.where(lane == 0, high, number - 128.0 * high)[0:ROWS]


def pack_body(place, *refs):
    held, (keep, send, down_out), local, sem = refs[0:7], refs[7:10], refs[10:17], refs[17]
    copies = [
        pltpu.make_async_copy(src, dst, sem.at[i]) for i, (src, dst) in enumerate(zip(held, local))
    ]
    for copy in copies:
        copy.start()
    for copy in copies:
        copy.wait()
    source = dict(zip(("qkv", "proj", "up", "small", "cls", "order"), local))
    down = local[6]

    def run(b):
        base = 0
        for chunk in GATHERED:
            for out, which in ((keep, b), (send, 1 - b)):
                for name, column, at, width in chunk.pieces(which):
                    span = slice(base + at, base + at + width)
                    if name == "pad":
                        out[:, span] = jnp.zeros((ROWS, width), F32)
                    elif name == "small":
                        out[:, span] = small_block(source["small"], 0) + small_block(
                            source["small"], 1
                        )
                    elif name == "order":
                        out[:, span] = order_block(source["order"])
                    elif name == "cls":
                        count = source["cls"].shape[0]
                        out[:, span] = jnp.zeros((ROWS, width), F32)
                        out[0:count, span] = source["cls"][:, column : column + width].astype(F32)
                    else:
                        flat, full = source[name[:-1]], FLAT[name[:-1]]
                        for r in range(ROWS):
                            first = r * full + column
                            layer = int(name[-1])
                            out[r : r + 1, span] = flat[layer : layer + 1, first : first + width]
            base += chunk.half

    by_core(place, run)
    for layer in range(LAYERS):
        for r in range(2 * PAIR):
            first = (2 * layer + r // PAIR) * D
            down_out[r % PAIR : r % PAIR + 1, first : first + D] = down[
                layer : layer + 1, r * D : (r + 1) * D
            ]


def merge_body(place, keep, recv, down, *rest):
    outs, work = rest[:2], rest[2]

    def run(b):
        work[ROWS * b : ROWS * (b + 1), :] = keep[...]
        work[ROWS * (1 - b) : ROWS * (2 - b), :] = recv[...]

    by_core(place, run)
    source = target = 0
    for number, chunk in enumerate(GATHERED):
        out = outs[min(number, 1)]
        if number <= 1:
            target = 0
        out[0, :, target : target + chunk.half] = work[:, source : source + chunk.half].astype(BF16)
        if chunk.down is not None:
            at, first = target + chunk.half, 2 * D * chunk.down
            out[0, :, at : at + 2 * D] = down[:, first : first + 2 * D].astype(BF16)
        source, target = source + chunk.half, target + chunk.width


def unpack_body(chunk, base, stages, place, *refs):
    own, sib, outs = refs[0:2], refs[2:4], refs[4:]
    target = dict(zip([n for n in chunk.arrays if n not in TABLES], outs))
    if "small" in chunk.names:
        rows_out, up_out, target["small"] = outs[-3:]
    if "order" in chunk.names:
        order_out, target["order"] = outs[-2:]

    def run(b):
        for which in range(2):
            source = own if which == b else sib
            for received in range(2):
                block = source[received]

                def step(index, _, which=which, received=received, block=block):
                    chip = chip_of(place, which, bits_of(index, 3) + [received], stages)
                    for name, column, at, width in chunk.pieces(which):
                        if name == "pad":
                            continue
                        values = block[index, :, base + at : base + at + width]
                        if name in TABLES:
                            values = values.astype(F32)
                        target[name][chip, :, column : column + width] = values
                    for part in range(0 if chunk.down is None else 2):
                        first = base + chunk.half + part * D
                        target["down"][chip * 4 + 2 * which + part] = block[
                            index, :, first : first + D
                        ]
                    return 0

                lax.fori_loop(0, CHIPS // 2, step, 0)

    by_core(place, run)
    if "order" in chunk.names:
        across = jnp.transpose(target["order"][...].reshape(D, ORDER))
        order_out[...] = across[0:1] * 128.0 + across[1:2]
    if "small" in chunk.names:
        across = jnp.transpose(target["small"][...].reshape(D, SMALL))
        rows_out[...] = across[0:24]
        ups = jnp.concatenate([across[8:12], across[20:24]], 0).astype(BF16)
        spread = (iota((D, FF), 1) // 4 == iota((D, FF), 0)).astype(F32).astype(BF16)
        wide = dot(ups, spread, 1, 0)
        lane = iota((1, FF), 1) % 4
        for layer in range(LAYERS):
            row = jnp.zeros((1, FF), F32)
            for k in range(4):
                row = jnp.where(lane == k, wide[4 * layer + k : 4 * layer + k + 1], row)
            up_out[layer : layer + 1, :] = row


def permute(x, masks):
    return lax.ppermute(x, AXES, [(i, i ^ masks[i & 1]) for i in range(2 * CHIPS)])


def unpack(chunk, base, stages, pieces, sib, place):
    shapes = [
        sds((CHIPS, PAIR, width), BF16)
        for name, width in zip(chunk.names, chunk.widths)
        if name != "pad" and name not in TABLES
    ]
    if chunk.down is not None:
        shapes.append(sds((4 * CHIPS, PAIR, D), BF16))
    count, scratch = len(shapes), []
    if "small" in chunk.names:
        shapes += [sds((24, D), F32), sds((LAYERS, FF), F32)]
        scratch = [pltpu.VMEM((CHIPS, PAIR, SMALL), F32)]
    if "order" in chunk.names:
        shapes += [sds((1, D), F32)]
        scratch = [pltpu.VMEM((CHIPS, PAIR, ORDER), F32)]
    out = call(functools.partial(unpack_body, chunk, base, stages), shapes, scratch=scratch)(
        place, *pieces, *sib
    )
    return [b.reshape(-1, b.shape[2]) for b in out[:count]] + list(out[count:])


def arrange_sums(chunk, place, matrices, keep, send, stages=GATHER_STAGES):
    source = dict(zip(chunk.arrays, matrices))

    def run(b):
        for out, which in ((keep, b), (send, 1 - b)):

            def step(index, _, out=out, which=which):
                chip = chip_of(place, which, bits_of(index), stages)
                rows = pl.ds(pl.multiple_of(chip * PAIR, 8), PAIR)
                for name, column, at, width in chunk.pieces(which):
                    if name == "pad":
                        out[index, :, at : at + width] = jnp.zeros((PAIR, width), BF16)
                    else:
                        out[index, :, at : at + width] = source[name][
                            rows, column : column + width
                        ].astype(BF16)
                for part in range(0 if chunk.down is None else 2):
                    at = chunk.half + part * D
                    first = pl.multiple_of((chip * 4 + 2 * which + part) * PAIR, 8)
                    out[index, :, at : at + D] = source["down"][pl.ds(first, PAIR), :].astype(BF16)
                return 0

            lax.fori_loop(0, CHIPS, step, 0)

    by_core(place, run)


def sum_shapes(chunk):
    return [sds((CHIPS, PAIR, chunk.width), BF16)] * 2


def split_rows_body(chunk, place, own, recv, keep, send, *down_out):
    def run(b):
        whole = own[...] + recv[...].astype(F32)
        for out, core in ((keep, b), (send, 1 - b)):
            out[...] = whole[ROWS * core : ROWS * (core + 1), : chunk.half]
        if chunk.down is not None:
            down_out[0][...] = whole[:, chunk.half :]

    by_core(place, run)


class Reduction:
    def __init__(self, chunk, keep, send, place, stages=GATHER_STAGES, direct=False):
        self.chunk, self.place, self.stage = chunk, place, 0
        self.keep, self.send = keep, [send]
        one, two, near, far = stages
        across = [[near, far, (near[0] ^ far[0],) * 2]] if direct else [[far], [near]]
        self.routes = [[CORE]] + across + [[two], [one], [CORE]]

    def move(self):
        self.stage += 1
        return [permute(s, mask) for s, mask in zip(self.send, self.routes[self.stage - 1])]

    def absorb(self, received):
        if self.stage == len(self.routes):
            self.result = (self.keep, received[0]) + tuple(self.rest)
            return
        if self.stage == len(self.routes) - 1:
            chunk = self.chunk
            shapes = [sds((ROWS, chunk.half), F32)] * 2
            if chunk.down is not None:
                shapes.append(sds((PAIR, 2 * D), F32))
            self.keep, send, *self.rest = call(functools.partial(split_rows_body, chunk), shapes)(
                self.place, self.keep[0], received[0][0]
            )
            self.send = [send]
            return
        parts = len(self.routes[self.stage]) + 1
        count = self.keep.shape[0] // parts

        def part(i):
            span = slice(i * count, (i + 1) * count)
            return sum([r[span].astype(F32) for r in received], self.keep[span].astype(F32))

        self.send = [part(i).astype(BF16) for i in range(1, parts)]
        self.keep = part(0)


class Transfer:
    def __init__(self, swap, send):
        self.swap, self.send = swap, [send]

    def move(self):
        return [self.swap(self.send[0])]

    def absorb(self, received):
        self.recv = received[0]


def beside(moving, run, *inputs):
    sends, inputs = lax.optimization_barrier(([m.send for m in moving], inputs))
    for m, send in zip(moving, sends):
        m.send = send
    received = [m.move() for m in moving]
    received, out = lax.optimization_barrier((received, run(*inputs)))
    for m, got in zip(moving, received):
        m.absorb(got)
    return out


def adam_math(fix, master, first, second, grad, rate, decay):
    moment = 0.5 * first + 0.5 * grad
    square = 0.5 * second + 0.5 * grad * grad
    update = moment / fix / (jnp.sqrt(square / fix) + adam_eps) + decay * master
    return master - rate * update, moment, square


def small_flat(table):
    width = ROWS * ROWS
    row, column = iota((ROWS, width), 1) // ROWS, iota((ROWS, width), 1) % ROWS
    at = iota((ROWS, width), 0)
    rows = []
    for layer in range(LAYERS):
        mine = table[:, ROWS * layer : ROWS * (layer + 1)]
        spread = jnp.zeros((ROWS, width), F32)
        for j in range(ROWS):
            spread = jnp.where(column == j, mine[:, j : j + 1], spread)
        rows.append(jnp.sum(jnp.where(row == at, spread, 0.0), 0, keepdims=True))
    return jnp.concatenate(rows, 0)


def adam_body(plan, place, fix_ref, *refs):
    chunks, names, extras = plan
    grads, at = [], 0
    for chunk in chunks:
        size = 2 if chunk.down is None else 3
        grads.append(refs[at : at + size])
        at += size
    flats = refs[at : at + 3 * len(names)]
    outs = refs[at + 3 * len(names) : at + 6 * len(names)]
    rest = refs[at + 6 * len(names) :]
    extra = dict(zip(extras, rest))
    work = dict(zip(names, rest[len(extras) :]))

    def run(b):
        for chunk, parts in zip(chunks, grads):
            sides = (parts[0], parts[1]) if b == 0 else (parts[1], parts[0])
            for which in range(2):
                for name, column, first, width in chunk.pieces(which):
                    span = slice(first, first + width)
                    if name in extra:
                        out = extra[name]
                        out[:, column : column + width] = sides[which][
                            0 : out.shape[0], span
                        ].astype(out.dtype)
                    elif name == "small" and name in work:
                        work[name][:, column : column + width] = sides[which][:, span]
                    elif name[:-1] in work:
                        full, layer = FLAT[name[:-1]], int(name[-1])
                        for r in range(ROWS):
                            to = r * full + column
                            work[name[:-1]][layer : layer + 1, to : to + width] = sides[which][
                                r : r + 1, span
                            ]
            if chunk.down is not None and "down" in work:
                layer = chunk.down
                for r in range(2 * PAIR):
                    first = (r // PAIR) * D
                    work["down"][layer : layer + 1, r * D : (r + 1) * D] = parts[2][
                        r % PAIR : r % PAIR + 1, first : first + D
                    ]

    by_core(place, run)
    for i, name in enumerate(names):
        new = adam_math(
            fix_ref[0],
            flats[3 * i][...],
            flats[3 * i + 1][...],
            flats[3 * i + 2][...],
            small_flat(work[name][...]) if name == "small" else work[name][...],
            rate_small if name == "small" else rate_matrix,
            0.0 if name == "small" else decay_matrix,
        )
        for k in range(3):
            outs[3 * i + k][...] = new[k]


class Step:
    def __init__(self, crop_devices, dp_devices, arguments):
        (
            self.patches,
            self.kept_index,
            self.lengths,
            self.source_order,
            self.cot_tokens,
            self.cot_cls,
            step_count,
        ) = arguments[:7]
        self.masters, self.firsts, self.seconds = arguments[7:12], arguments[12:17], arguments[17:22]
        self.crop_count, self.patch_count = self.patches.shape[:2]
        self.half = self.crop_count // 2
        self.dp_devices = dp_devices
        me = lax.axis_index(AXES)
        self.place = jnp.stack([me, me // dp_devices]).astype(jnp.int32)
        self.swap = functools.partial(lax.ppermute, axis_name="crop", perm=[(0, 1), (1, 0)])
        self.crops_half = sds((self.half, SLOTS, D), BF16)
        self.rows = (self.half + 1) * SLOTS
        self.fix = (1.0 - jnp.power(0.5, step_count[0].astype(F32))).reshape(1)

    def tokens(self):
        positions = jnp.arange(SLOTS, dtype=jnp.int32)[None, :]
        rest = SLOTS - self.kept_index.shape[1] - 1
        slots = jnp.pad(self.kept_index, ((0, 0), (1, rest)), constant_values=-1)
        self.slots = jnp.where(positions <= self.lengths[:, None], slots + 1, -1)
        return call(
            functools.partial(tokens_body, self.half, self.patch_count),
            [self.crops_half] * 2,
        )(self.place, self.patches, self.slots)

    def arrange(self, keep, recv):
        return call(
            functools.partial(arrange_body, self.half),
            [
                sds((self.rows, D), F32),
                sds((self.half + 1, SLOTS, 2 * SLOTS), F32),
                sds((2 * self.half, 128), F32),
            ],
        )(self.place, keep, recv)

    def first_ids(self, place):
        views = self.crop_count * (place[0] - place[1] * self.dp_devices) + self.half * place[1]
        return views, views + self.crop_count * self.dp_devices

    def cot_send(self):
        start, count = self.half * (1 - self.place[1]), self.half // 2
        return [
            lax.dynamic_slice_in_dim(self.cot_tokens, start + i * count, count, 0) for i in range(2)
        ]

    def turn(self, x, lens, cot_a, cot_b, order, every_cot):
        shapes = [self.crops_half] * 2 + [sds((self.rows, D), F32), sds(every_cot.shape, F32)]
        return call(functools.partial(turn_body, self.half, self.first_ids), shapes)(
            self.place, x, lens, self.cot_tokens, cot_a, cot_b, order, every_cot
        )

    def split(self, x):
        return call(functools.partial(split_body, self.half), [self.crops_half] * 2)(self.place, x)

    def join(self, keep, recv):
        return call(
            functools.partial(join_body, self.half), sds((self.crop_count, SLOTS, D), BF16)
        )(self.place, keep, recv)

    def scatter(self, keep, recv):
        stride = -(-self.patch_count // 8) * 8
        out = call(
            functools.partial(scatter_body, self.half, self.patch_count),
            sds((self.patch_count, self.crop_count, D), F32),
            scratch=[pltpu.VMEM((self.crop_count * stride, 128), F32)] * (D // 128),
        )(self.place, keep, recv, self.slots)
        return jnp.transpose(out, (1, 0, 2))

    def adam_flat(self, kind, grad):
        return adam_math(
            self.fix[0],
            self.masters[kind],
            self.firsts[kind],
            self.seconds[kind],
            grad,
            rate_small if kind == 4 else rate_matrix,
            0.0 if kind == 4 else decay_matrix,
        )

    def adam_rows(self, fix, chunks, names, kinds, parts, extras, small=False):
        names, kinds = names + ["small"] * small, kinds + [4] * small
        flats = [f[kind] for kind in kinds for f in (self.masters, self.firsts, self.seconds)]
        shapes = [sds(f.shape, F32) for f in flats] + [shape for _, shape in extras]
        plan = (chunks, names, [name for name, _ in extras])
        out = call(
            functools.partial(adam_body, plan),
            shapes,
            scratch=[
                pltpu.VMEM((ROWS, SMALL) if name == "small" else flats[3 * i].shape, F32)
                for i, name in enumerate(names)
            ],
            smem=2,
        )(self.place, fix, *[a for part in parts for a in part], *flats)
        return [list(out[3 * i : 3 * i + 3]) for i in range(len(kinds))], out[3 * len(kinds) :]


def outputs(block_out, cls_grouped, patch_grad, results):
    return (block_out, cls_grouped, patch_grad) + tuple(
        results[kind][part] for part in range(3) for kind in range(5)
    )


def pack_call(place, operands, shapes):
    return pl.pallas_call(
        pack_body,
        in_specs=[SM] + [pl.BlockSpec(memory_space=pltpu.HBM)] * len(operands),
        out_specs=[VM] * len(shapes),
        out_shape=shapes,
        scratch_shapes=[pltpu.VMEM(a.shape, a.dtype) for a in operands]
        + [pltpu.SemaphoreType.DMA((len(operands),))],
        compiler_params=pltpu.CompilerParams(vmem_limit_bytes=VMEM_LIMIT),
        cost_estimate=NO_COST,
    )(place, *[pltpu.with_memory_space_constraint(a, pltpu.HBM) for a in operands])


def staged_step(step):
    place = step.place
    total_half = sum(c.half for c in GATHERED)
    rows_shape = sds((ROWS, total_half), F32)
    keep, send, downs = pack_call(
        place,
        step.masters[:3]
        + (step.masters[4], step.cot_cls, step.source_order[None, :], step.masters[3]),
        [rows_shape, rows_shape, sds((PAIR, 4 * D), F32)],
    )
    recv = permute(send, CORE)
    width = GATHERED[1].width
    a, b = call(
        merge_body,
        [
            sds((1, PAIR, GATHERED[0].width), BF16),
            sds((1, PAIR, width + GATHERED[2].width), BF16),
        ],
        scratch=[pltpu.VMEM((PAIR, total_half), F32)],
    )(place, keep, recv, downs)

    step.kept_index, step.patches, a = tie(step.kept_index, step.patches, a)
    a_recv = permute(a, GATHER_STAGES[0])
    tok_keep, tok_send = step.tokens()
    tok_recv = step.swap(tok_send)
    a_recv, b = tie(a_recv, b)
    a = jnp.concatenate([a, a_recv])
    a_recv = permute(a, GATHER_STAGES[1])
    b_recv = permute(b, BESIDE_STAGES[0])
    a_recv, b_recv = tie(a_recv, b_recv)
    a = jnp.concatenate([a, a_recv])
    b = jnp.concatenate([b, b_recv])
    a_recv = permute(a, GATHER_STAGES[2])
    b_recv = permute(b, BESIDE_STAGES[1])
    a_recv, b_recv, tok_recv = tie(a_recv, b_recv, tok_recv)
    a = jnp.concatenate([a, a_recv])
    b = jnp.concatenate([b, b_recv])
    a_recv = permute(a, GATHER_STAGES[3])
    b_recv = permute(b, BESIDE_STAGES[2])
    x, bias, lens = step.arrange(tok_keep, tok_recv)
    a_sib = permute(a, CORE)
    cot_a, cot_b = step.cot_send()
    a, a_recv, a_sib, b_recv, x, cot_a, cot_b = tie(a, a_recv, a_sib, b_recv, x, cot_a, cot_b)
    a_sib = (a_sib, permute(a_recv, CORE))
    b = jnp.concatenate([b, b_recv])
    b_recv = permute(b, BESIDE_STAGES[3])
    b_sib = permute(b, CORE)
    qkv0, proj0, up0, down0, small, up_bias = unpack(
        GATHERED[0], 0, GATHER_STAGES, (a, a_recv), a_sib, place
    )

    small0, small1 = small[0:12], small[12:24]
    norms_0, n1_0, qkv_0, att_0, prob_0, mid_0, n2_0 = layer_forward_one(
        x, bias, qkv0, proj0, small0
    )
    x_1, act_0, slope_0 = layer_forward_two(mid_0, n2_0, up0, down0, small0, up_bias[0:1])
    x_1, b_recv, b_sib = tie(x_1, b_recv, b_sib)
    b_sib = (b_sib, permute(b_recv, CORE))
    cot_a = step.swap(cot_a)
    qkv1, proj1, every_cot, order = unpack(
        GATHERED[1], 0, BESIDE_STAGES, (b, b_recv), b_sib, place
    )
    norms_1, n1_1, qkv_1, att_1, prob_1, mid_1, n2_1 = layer_forward_one(
        x_1, bias, qkv1, proj1, small1
    )
    mid_1, n2_1, cot_a, cot_b = tie(mid_1, n2_1, cot_a, cot_b)
    cot_b = step.swap(cot_b)
    up1, down1 = unpack(GATHERED[2], width, BESIDE_STAGES, (b, b_recv), b_sib, place)
    final, act_1, slope_1 = layer_forward_two(mid_1, n2_1, up1, down1, small1, up_bias[1:2])
    out_keep, out_send, g, dense_cls = step.turn(final, lens, cot_a, cot_b, order, every_cot)

    def mlp_finish(layer):
        def finish(place, matrices, outs):
            arrange_sums(MLP_SUMS[layer], place, matrices, outs[0], outs[1])

        return finish

    def qkv_finish(layer):
        def finish(place, matrices, outs, rows):
            matrices = list(matrices)
            if layer == 0:
                weight, proj, rows_one1, rows_two1, up1, rows_two0, up0 = matrices
                table = outs[2]
                table[...] = jnp.zeros(table.shape, F32)
                table[:, 0:32] = small_table(((rows, rows_two0, up0), (rows_one1, rows_two1, up1)))
                matrices = [weight, proj, table]
            stages = BESIDE_STAGES if layer else GATHER_STAGES
            arrange_sums(QKV_SUMS[layer], place, matrices, outs[0], outs[1], stages)

        return finish

    out_swap = Transfer(step.swap, out_send)
    keep, send, g_hid, bias_up1 = beside(
        [out_swap],
        lambda g: mlp_weights(
            place, mlp_finish(1), sum_shapes(MLP_SUMS[1]), g, n2_1, act_1, slope_1, down1
        ),
        g,
    )
    m1 = Reduction(MLP_SUMS[1], keep, send, place)
    g_mid, g_proj, g_att, rows_two1 = beside(
        [m1],
        lambda g_hid: mlp_rows(g, g_hid, norms_1[2], norms_1[3], att_1, up1, proj1, small1),
        g_hid,
    )

    def last_qkv(g_att):
        keep, send, g_nrm, rows = qkv_weights(
            place, qkv_finish(1), sum_shapes(QKV_SUMS[1]), (g_proj, dense_cls),
            g_att, n1_1, qkv_1, prob_1, norms_1[0], qkv1,
        )
        return keep, send, norm_one(g_nrm, norms_1[0], norms_1[1], g_mid, small1), rows

    keep, send, g, rows_one1 = beside([m1], last_qkv, g_att)
    q1 = Reduction(QKV_SUMS[1], keep, send, place, BESIDE_STAGES)

    keep, send, g_hid, bias_up0 = beside(
        [q1, m1],
        lambda g: mlp_weights(
            place, mlp_finish(0), sum_shapes(MLP_SUMS[0]), g, n2_0, act_0, slope_0, down0
        ),
        g,
    )
    m0 = Reduction(MLP_SUMS[0], keep, send, place)
    g_mid, g_proj, g_att, rows_two0 = beside(
        [m0, q1, m1],
        lambda g_hid: mlp_rows(g, g_hid, norms_0[2], norms_0[3], att_0, up0, proj0, small0),
        g_hid,
    )
    keep, send, _, g_nrm, _ = beside(
        [m0, q1, m1],
        lambda g_att: qkv_weights(
            place, qkv_finish(0), sum_shapes(QKV_SUMS[0]) + [sds((D, SMALL), F32)],
            (g_proj, rows_one1, rows_two1, bias_up1, rows_two0, bias_up0),
            g_att, n1_0, qkv_0, prob_0, norms_0[0], qkv0,
        ),
        g_att,
    )
    q0 = Reduction(QKV_SUMS[0], keep, send, place, direct=True)
    back_keep, back_send = beside(
        [q0, m0, q1],
        lambda g_nrm: step.split(norm_one(g_nrm, norms_0[0], norms_0[1], g_mid, small0)),
        g_nrm,
    )
    block_out = beside(
        [q0, m0, q1], lambda keep, recv: step.join(keep, recv), out_keep, out_swap.recv
    )
    back_send, q0.send = tie(back_send, q0.send)
    back_recv = step.swap(back_send)
    back_keep = beside([q0, m0, q1, m1], lambda v: v, back_keep)
    patch_grad = beside([q0, m0], lambda keep: step.scatter(keep, back_recv), back_keep)

    def adam_mlp(fix):
        new, _ = step.adam_rows(
            fix, [MLP_SUMS[1], MLP_SUMS[0]], ["up", "down"], [2, 3], [m1.result, m0.result], []
        )
        return new[0] + new[1]

    new = beside([q0], adam_mlp, step.fix)
    new_up, new_down = new[:3], new[3:]
    (new_qkv, new_proj, new_small), (cls_grouped,) = step.adam_rows(
        step.fix,
        [QKV_SUMS[1], QKV_SUMS[0]],
        ["qkv", "proj"],
        [0, 1],
        [q1.result, q0.result],
        [("cls", sds((step.crop_count, CLS), BF16))],
        small=True,
    )
    return outputs(block_out, cls_grouped, patch_grad, (new_qkv, new_proj, new_up, new_down, new_small))


def plain_step(step):
    def gather(values):
        return lax.all_gather(values, AXES, axis=0, tiled=True)

    weights, smalls, up_biases = [], [], []
    for layer in range(LAYERS):
        flat = [gather(m[layer].astype(BF16)) for m in step.masters]
        small = flat[4].reshape(D, 8 + FF // D).astype(F32)
        weights.append(
            (
                flat[0].reshape(D, QKV),
                flat[1].reshape(D, D),
                flat[2].reshape(D, FF),
                flat[3].reshape(FF, D),
            )
        )
        smalls.append(jnp.transpose(small[:, :8]))
        up_biases.append(small[:, 8:].reshape(1, FF))
    keep, send = step.tokens()
    x, bias, lens = step.arrange(keep, step.swap(send))
    saved = []
    for layer in range(LAYERS):
        qkv_w, proj_w, up_w, down_w = weights[layer]
        one = layer_forward_one(x, bias, qkv_w, proj_w, smalls[layer])
        x, active, slope = layer_forward_two(
            one[5], one[6], up_w, down_w, smalls[layer], up_biases[layer]
        )
        saved.append(one + (active, slope))
    order = gather(step.source_order).astype(F32)[None, :]
    out_keep, out_send, g, dense_cls = step.turn(
        x, lens, *[step.swap(item) for item in step.cot_send()], order, gather(step.cot_cls)
    )
    block_out = step.join(out_keep, step.swap(out_send))
    gradients = [None] * LAYERS

    def two_out(place, matrices, outs, *_):
        for value, out in zip(matrices, outs):
            out[...] = value[...]

    for layer in reversed(range(LAYERS)):
        norms, normed_one, qkv, attended, prob, _, normed_two, active, slope = saved[layer]
        qkv_w, proj_w, up_w, down_w = weights[layer]
        g_up, g_down, g_hid, bias_up = mlp_weights(
            step.place, two_out, [sds((D, FF), F32), sds((FF, D), F32)],
            g, normed_two, active, slope, down_w,
        )
        g_mid, g_proj, g_att, two = mlp_rows(
            g, g_hid, norms[2], norms[3], attended, up_w, proj_w, smalls[layer]
        )
        g_qkv_w, g_nrm, one = qkv_weights(
            step.place, two_out, [sds((D, QKV), F32)], (),
            g_att, normed_one, qkv, prob, norms[0], qkv_w,
        )
        g = norm_one(g_nrm, norms[0], norms[1], g_mid, smalls[layer])
        eight = jnp.concatenate([one[0:4], two[3:4], two[0:3]])
        table = jnp.concatenate([jnp.transpose(eight), bias_up.reshape(D, FF // D)], 1)
        gradients[layer] = (g_qkv_w, g_proj, g_up, g_down, table)
    back_keep, back_send = step.split(g)
    patch_grad = step.scatter(back_keep, step.swap(back_send))

    def scatter_sum(values):
        return lax.psum_scatter(values, AXES, scatter_dimension=0, tiled=True)

    results = []
    for kind in range(5):
        shares = [
            scatter_sum(gradients[layer][kind].reshape(-1).astype(F32)) for layer in range(LAYERS)
        ]
        results.append(step.adam_flat(kind, jnp.stack(shares)))
    cls_grouped = scatter_sum(dense_cls).astype(BF16)
    return outputs(block_out, cls_grouped, patch_grad, results)


def on_device(crop_devices, dp_devices, *arguments):
    step = Step(crop_devices, dp_devices, arguments)
    owned = step.masters[0].shape[1]
    staged = crop_devices * dp_devices == 2 * CHIPS and owned == ROWS * QKV
    if staged and step.crop_count <= ROWS:
        return staged_step(step)
    return plain_step(step)


def solution(mesh):
    crops = [P(AXES, None, None), P(AXES, None), P(AXES), P(AXES), P(AXES, None, None)]
    flat = P(None, AXES)
    return jax.shard_map(
        functools.partial(on_device, mesh.shape["crop"], mesh.shape["dp"]),
        mesh=mesh,
        in_specs=tuple(crops + [P(AXES, None), P()] + [flat] * 15),
        out_specs=(crops[0], crops[1], crops[0]) + (flat,) * 15,
        check_vma=False,
    )
```
